32 devices in a mesh: grp: 4 (over x, core), blk: 8 (over z, y).
Axes of the slice: x: 2, y: 2, z: 4, core: 2. Of those that a mesh axis runs over, the one named last changes fastest.
Arguments:
- vertices: float32 [3, 8192], P(None, ('grp', 'blk')), may hold values from -6 to 6
- faces: int32 [3, 16384], P(None, ('grp', 'blk')), may hold values from 0 to 255
- trial_step: float32 [3, 8192], P(None, ('grp', 'blk')), may hold values from -2 to 2
- accepted: int32 [4], P('grp'), may hold values from 0 to 1
- face_weight: float32 [16384], P(('grp', 'blk')), may hold values from 0.5 to 6
- partner_shift: int32 [2, 4], replicated, may hold values from 1 to 3, as said below
Outputs:
- vertex_grad: float32 [3, 8192], P(None, ('grp', 'blk'))
- energy: float32 [1], replicated
The draws below stay inside these ranges and needn't reach their ends.
Inputs may be any that keep to these rules, and one draw needn't show every extreme that they name: `partner_shift`: for each group the 2 offsets are all different, and the first round's offset is 4 // 2 for every group.
All inputs are finite; a program needn't handle non-finite values.
Results may differ from the reference program's by a relative error of at most 0.0001.
Values sent between devices are 32-bit elements; how exact they have to be, the bound alone decides.
No kernel may reach another device: no remote copies, remote signals or barrier semaphores. Data moves between devices by JAX's collectives and lax.ppermute only.
A program may use at most 64 MiB of HBM per device.

```python
import jax
import jax.numpy as jnp
from jax import lax

FACES_DEV = 512
VERT_DEV = 256
HOPS = 4
ROUNDS = 2
FACES = 16384
VERTS = 8192
N_GRP = 4
N_BLK = 8


def draw_face_weight(key, part):
    total = FACES_DEV * N_GRP * N_BLK
    base = jnp.exp(jax.random.uniform(key, (total,), jnp.float32, jnp.log(0.5), jnp.log(2.0)))
    owner = (jnp.arange(total) // FACES_DEV).astype(jnp.float32)
    rise = 1.0 + 2.0 * owner / max(N_GRP * N_BLK - 1, 1)
    return base * rise


def draw_partner_shift(key, part):
    half = N_GRP // 2
    others = jnp.array([s for s in range(1, N_GRP) if s != half], jnp.int32)
    keys = jax.random.split(jax.random.fold_in(key, 41), N_GRP)

    def pick(one_key):
        return jax.random.permutation(one_key, others)[:ROUNDS - 1]
    rest = jax.vmap(pick)(keys).astype(jnp.int32)
    first = jnp.full((1, N_GRP), half, jnp.int32)
    return jnp.concatenate([first, rest.T], 0).astype(jnp.int32)


def touch_ends(result, stream_key, least, high):
    index_at = [jax.random.randint(jax.random.fold_in(stream_key, axis), (), 0, length) for axis, length in enumerate(result.shape)]
    longest = result.shape.index(max(result.shape))
    neighbour = index_at[:longest] + [(index_at[longest] + 1) % result.shape[longest]] + index_at[longest + 1:]
    return result.at[tuple(index_at)].set(least).at[tuple(neighbour)].set(high)


def block_levels(stream_key, extent, shards, least, largest):
    def one(axis_at, shards_of):
        steps = jax.random.uniform(jax.random.fold_in(jax.random.fold_in(stream_key, 6), axis_at), (shards_of,), jnp.float32, least / len(shards), largest / len(shards))
        return jnp.repeat(jnp.exp(steps), extent[axis_at] // shards_of).reshape((-1,) + (1,) * (len(extent) - axis_at - 1))

    gain = one(*shards[0])
    for cut in shards[1:]:
        gain = gain * one(*cut)
    return gain


def scatter_about(key, shape, width, reach, shards=(), kind=jnp.bfloat16):
    values = jax.random.normal(key, shape, jnp.float32) * width
    if len(shards) > 0:
        values = block_levels(key, shape, shards, -0.22, 0.18) * values
    return jnp.clip(values, min=-reach, max=reach).astype(kind)


def setup_inputs(seed: int = 0) -> dict:
    key_of = jax.random.split(jax.random.key(seed), 7)
    vertices = scatter_about(key_of[0], (3, VERTS), 1.0, 6.0, ((1, 32),), jnp.float32)
    faces = touch_ends(jax.random.randint(key_of[1], (3, FACES), 0, VERT_DEV), jax.random.fold_in(key_of[1], 1), 0, VERT_DEV - 1).astype(jnp.int32)
    trial_step = scatter_about(key_of[2], (3, VERTS), 0.3, 2.0, ((1, 32),), jnp.float32)
    accepted = touch_ends(jax.random.randint(key_of[3], (N_GRP,), 0, 2), jax.random.fold_in(key_of[3], 1), 0, 1).astype(jnp.int32)
    face_weight = draw_face_weight(jax.random.fold_in(key_of[6], 71), 0)
    partner_shift = draw_partner_shift(jax.random.fold_in(key_of[6], 71), 0)
    return {"vertices": vertices, "faces": faces, "trial_step": trial_step, "accepted": accepted, "face_weight": face_weight, "partner_shift": partner_shift}


EPS2 = 0.05

def pair_energy(own_geo, own_weight, other_geo, other_weight):
    d0 = own_geo[0][:, None] - other_geo[0][None, :]
    d1 = own_geo[1][:, None] - other_geo[1][None, :]
    d2 = own_geo[2][:, None] - other_geo[2][None, :]
    dist = d0 * d0 + d1 * d1 + d2 * d2 + EPS2
    proj_own = own_geo[3][:, None] * d0 + own_geo[4][:, None] * d1 + own_geo[5][:, None] * d2
    proj_other = other_geo[3][None, :] * d0 + other_geo[4][None, :] * d1 + other_geo[5][None, :] * d2
    kernel = own_weight[:, None] * other_weight[None, :] * (proj_own * proj_own + proj_other * proj_other) / (dist * dist)
    return jnp.sum(kernel)

def tile_grads(own, other):

    def energy_of(first, second):
        return pair_energy(first, own[6], second, other[6])
    value, pullback = jax.vjp(energy_of, own[:6], other[:6])
    grad_own, grad_other = pullback(jnp.ones_like(value))
    return (value, grad_own, grad_other)

def geometry(pos, tri):
    first = pos[:, tri[0]]
    second = pos[:, tri[1]]
    third = pos[:, tri[2]]
    center = (first + second + third) / 3.0
    normal = 0.5 * jnp.cross(second - first, third - first, axis=0)
    return jnp.concatenate([center, normal], 0)

def reference(vertices, faces, trial_step, accepted, face_weight, partner_shift):
    devices = N_GRP * N_BLK
    step_on = jnp.repeat(accepted.astype(vertices.dtype), N_BLK * VERT_DEV)
    pos = vertices + step_on[None, :] * trial_step
    owner = jnp.arange(FACES, dtype=jnp.int32) // FACES_DEV * VERT_DEV
    tri = faces + owner[None, :]

    def geo_of(p):
        return geometry(p, tri)
    geo, pull = jax.vjp(geo_of, pos)
    data = jnp.concatenate([geo, face_weight[None, :].astype(geo.dtype)], 0)
    blocks = data.reshape(7, N_GRP, N_BLK, FACES_DEV).transpose(1, 2, 0, 3)

    def visit(index, carry):
        energy, grads = carry
        g = index // N_BLK
        b = index % N_BLK
        own = blocks[g, b]
        value, grad_a, grad_b = tile_grads(own, own)
        energy = energy + 0.5 * value
        grads = grads.at[g, b].add(0.5 * (grad_a + grad_b))
        for k in range(1, HOPS + 1):
            later = (b + k) % N_BLK
            value, grad_a, grad_b = tile_grads(own, blocks[g, later])
            energy = energy + value
            grads = grads.at[g, b].add(grad_a).at[g, later].add(grad_b)
        for r in range(ROUNDS):
            other_group = (g + partner_shift[r, g]) % N_GRP
            value, grad_a, grad_b = tile_grads(own, blocks[other_group, b])
            energy = energy + value
            grads = grads.at[g, b].add(grad_a).at[other_group, b].add(grad_b)
        return (energy, grads)
    init = (jnp.zeros((), geo.dtype), jnp.zeros((N_GRP, N_BLK, 6, FACES_DEV), geo.dtype))
    energy, grads = lax.fori_loop(0, N_GRP * N_BLK, visit, init)
    face_grad = grads.transpose(2, 0, 1, 3).reshape(6, FACES)
    vertex_grad = pull(face_grad)[0] / FACES_DEV
    total = energy / (FACES_DEV * FACES_DEV * devices)
    return (vertex_grad, total.reshape(1))
```

```python
import functools

import jax
import jax.numpy as jnp
from jax import lax
from jax.experimental import pallas as pl
from jax.experimental.pallas import tpu as pltpu
from jax.sharding import PartitionSpec as P

HOPS = 4
EPS2 = 0.05
ROWS = 8
LANES = 128
F32 = jnp.float32
BF16 = jnp.bfloat16
VMEM = pl.BlockSpec(memory_space=pltpu.VMEM)
SMEM = pl.BlockSpec(memory_space=pltpu.SMEM)


def flip(value, axis, mask):
    count = lax.axis_size(axis)
    return lax.ppermute(value, axis, [(i, i ^ mask) for i in range(count)])


def from_ahead(value, axis, by):
    count = lax.axis_size(axis)
    return lax.ppermute(value, axis, [(i, (i - by) % count) for i in range(count)])


def pieces(value):
    high = value.astype(BF16)
    rest = value - high.astype(F32)
    middle = rest.astype(BF16)
    low = (rest - middle.astype(F32)).astype(BF16)
    return high, middle, low


def one_hot(row, count):
    rows = lax.broadcasted_iota(jnp.int32, (count, row.shape[1]), 0)
    return jnp.where(rows == row, 1.0, 0.0).astype(BF16)


def geometry_kernel(accepted, vertices, trial_step, faces, weight, own, edges, padded):
    verts = vertices.shape[1]
    count = faces.shape[1]
    padded[...] = jnp.zeros_like(padded)
    padded[0:3, :] = vertices[...] + accepted[0].astype(F32) * trial_step[...]
    left = jnp.concatenate(pieces(padded[...]), 0)

    def corner(k):
        picked = jnp.dot(left, one_hot(faces[k : k + 1, :], verts), preferred_element_type=F32)
        picked = picked[0:ROWS] + picked[ROWS : 2 * ROWS] + picked[2 * ROWS : 3 * ROWS]
        return [picked[c : c + 1] for c in range(3)]

    first, second, third = corner(0), corner(1), corner(2)
    for c in range(3):
        own[c : c + 1, :] = (first[c] + second[c] + third[c]) / 3.0
    e1 = [second[c] - first[c] for c in range(3)]
    e2 = [third[c] - first[c] for c in range(3)]
    for c in range(3):
        n, m = (c + 1) % 3, (c + 2) % 3
        own[3 + c : 4 + c, :] = 0.5 * (e1[n] * e2[m] - e1[m] * e2[n])
        edges[c : c + 1, :] = e1[c]
        edges[3 + c : 4 + c, :] = e2[c]
    own[6:7, :] = weight[...].reshape(1, count)
    own[7:8, :] = jnp.zeros((1, count), F32)
    edges[6:8, :] = jnp.zeros((2, count), F32)


def window_times(offset, blocks):
    times = 0
    for k in range(1, HOPS + 1):
        times += ((k - offset) % blocks == 0).astype(jnp.int32) if not isinstance(offset, int) else int((k - offset) % blocks == 0)
        times += ((k + offset) % blocks == 0).astype(jnp.int32) if not isinstance(offset, int) else int((k + offset) % blocks == 0)
    return times


def partner_times(shift, here, there, groups):
    times = jnp.int32(0)
    for r in range(shift.shape[0]):
        times += (lax.rem(here + shift[r, here], groups) == there).astype(jnp.int32)
        times += (lax.rem(there + shift[r, there], groups) == here).astype(jnp.int32)
    return times


def multiplicity(kind, shift, groups, blocks):
    name, value = kind
    if name == "self":
        return 1.0 + window_times(0, blocks)
    if name == "blk":
        return float(window_times(value, blocks))
    if name == "blk^":
        here = lax.axis_index("blk")
        there = here ^ value
        return window_times(lax.rem(there - here + blocks, blocks), blocks).astype(F32)
    here = lax.axis_index("grp")
    there = here ^ value if name == "grp^" else lax.rem(here + value, groups)
    return partner_times(shift, here, there, groups).astype(F32)


def tiles_kernel(plan, groups, blocks, carry, adds, *refs):
    shift, own = refs[0], refs[1]
    count = own.shape[1]
    arrays = len(plan)
    others = refs[2 : 2 + arrays]
    at = 2 + arrays
    start = None
    if carry:
        start = refs[at]
        at += 1
    out, columns = refs[at], refs[at + 1]
    number = 0
    for ref, kinds in zip(others, plan):
        for index, kind in enumerate(kinds):
            block = ref[index] if len(ref.shape) == 3 else ref[...]
            times = multiplicity(kind, shift, groups, blocks)
            columns[number * count : (number + 1) * count, :] = block.T
            spot = slice(number * count, (number + 1) * count)
            columns[spot, 6:7] = columns[spot, 6:7] * times
            number += 1
    width = 2
    for half in range(count // (width * LANES)):
        spans = [slice((half * width + v) * LANES, (half * width + v + 1) * LANES) for v in range(width)]
        mine = [[jnp.broadcast_to(own[k : k + 1, s], (ROWS, LANES)) for k in range(6)] for s in spans]

        def body(step, sums):
            sums = [list(s) for s in sums]
            base = pl.multiple_of(step * ROWS, ROWS)
            group = columns[pl.ds(base, ROWS), :]
            b = [jnp.broadcast_to(group[:, k : k + 1], (ROWS, LANES)) for k in range(7)]
            for v in range(width):
                a, s = mine[v], sums[v]
                d0, d1, d2 = a[0] - b[0], a[1] - b[1], a[2] - b[2]
                dist = d0 * d0 + d1 * d1 + (d2 * d2 + EPS2)
                proj_a = a[3] * d0 + a[4] * d1 + a[5] * d2
                proj_b = b[3] * d0 + b[4] * d1 + b[5] * d2
                inverse = 1.0 / dist
                square = inverse * inverse * b[6]
                alpha = proj_a * square
                beta = proj_b * square
                kernel = proj_a * alpha + proj_b * beta
                gamma = 2.0 * (kernel * inverse)
                s[0] += beta * b[3] - gamma * d0
                s[1] += beta * b[4] - gamma * d1
                s[2] += beta * b[5] - gamma * d2
                s[3] += alpha * d0
                s[4] += alpha * d1
                s[5] += alpha * d2
                s[6] += alpha
                s[7] += kernel
            return tuple(tuple(s) for s in sums)

        zero = jnp.zeros((ROWS, LANES), F32)
        sums = lax.fori_loop(0, number * count // ROWS, body, ((zero,) * 8,) * width, unroll=2)
        for v, span in enumerate(spans):
            for k in range(8):
                row = jnp.sum(sums[v][k], axis=0, keepdims=True)
                if start is not None:
                    row = row + start[k : k + 1, span]
                out[k : k + 1, span] = row


def tiles(shift, own, parts, start, groups, blocks):
    arrays = [array for array, _ in parts]
    plan = tuple(kinds for _, kinds in parts)
    count = own.shape[1]
    number = sum(len(kinds) for kinds in plan)
    body = functools.partial(tiles_kernel, plan, groups, blocks, start is not None, 0)
    operands = [shift, own, *arrays] + ([start] if start is not None else [])
    pairs = number * count * count
    return pl.pallas_call(
        body,
        out_shape=jax.ShapeDtypeStruct((ROWS, count), F32),
        in_specs=[SMEM] + [VMEM] * (len(operands) - 1),
        out_specs=VMEM,
        scratch_shapes=[pltpu.VMEM((number * count, ROWS), F32)],
        cost_estimate=pl.CostEstimate(flops=60 * pairs, bytes_accessed=32 * count * number, transcendentals=pairs),
    )(*operands)


def finish_kernel(own, edges, sums, faces, grad, share):
    verts = grad.shape[1]
    count = own.shape[1]
    twice = 2.0 * own[6:7, :]
    total = sums[6:7, :]
    g_center = [twice * (own[3 + c : 4 + c, :] * total + sums[c : c + 1, :]) for c in range(3)]
    g_area = [twice * sums[3 + c : 4 + c, :] for c in range(3)]
    e1 = [edges[c : c + 1, :] for c in range(3)]
    e2 = [edges[3 + c : 4 + c, :] for c in range(3)]
    zero = jnp.zeros((ROWS - 3, count), F32)
    corners = [[], [], []]
    for c in range(3):
        n, m = (c + 1) % 3, (c + 2) % 3
        g1 = 0.5 * (e2[n] * g_area[m] - e2[m] * g_area[n])
        g2 = 0.5 * (g_area[n] * e1[m] - g_area[m] * e1[n])
        part = g_center[c] / 3.0
        corners[0].append(part - g1 - g2)
        corners[1].append(part + g1)
        corners[2].append(part + g2)
    total = jnp.zeros((3 * ROWS, verts), F32)
    for k in range(3):
        left = jnp.concatenate(pieces(jnp.concatenate(corners[k] + [zero], 0)), 0)
        total += lax.dot_general(
            left, one_hot(faces[k : k + 1, :], verts), (((1,), (1,)), ((), ())), preferred_element_type=F32
        )
    total = total[0:ROWS] + total[ROWS : 2 * ROWS] + total[2 * ROWS : 3 * ROWS]
    grad[...] = total[0:3] / count
    energy = own[6:7, :] * sums[7:8, :]
    share[...] = jnp.broadcast_to(0.5 * jnp.sum(energy, axis=1, keepdims=True), share.shape)


def shards(vertices, faces, trial_step, accepted, face_weight, partner_shift):
    count = faces.shape[1]
    verts = vertices.shape[1]
    groups, blocks = lax.axis_size("grp"), lax.axis_size("blk")
    block_shape = jax.ShapeDtypeStruct((ROWS, count), F32)
    own, edges = pl.pallas_call(
        geometry_kernel,
        out_shape=(block_shape, block_shape),
        in_specs=[SMEM] + [VMEM] * 4,
        out_specs=(VMEM, VMEM),
        scratch_shapes=[pltpu.VMEM((ROWS, verts), F32)],
    )(accepted, vertices, trial_step, faces, face_weight)
    visit = functools.partial(tiles, partner_shift, own, groups=groups, blocks=blocks)

    blk_parts, grp_parts = [], []
    held, kinds = own[None], [0]
    if blocks & (blocks - 1) == 0 and blocks <= 2 * HOPS:
        mask = blocks // 2
        while mask:
            other = flip(held, "blk", mask)
            kinds_other = [k ^ mask for k in kinds]
            blk_parts.append((other, tuple(("blk^", k) for k in kinds_other)))
            held, kinds = jnp.concatenate([held, other], 0), kinds + kinds_other
            mask //= 2
    else:
        offsets = sorted({o for k in range(1, HOPS + 1) for o in (k % blocks, -k % blocks) if o})
        for o in offsets:
            blk_parts.append((from_ahead(own, "blk", o), (("blk", o),)))
    held, kinds = own[None], [0]
    if groups & (groups - 1) == 0:
        mask = groups // 2
        while mask:
            other = flip(held, "grp", mask)
            kinds_other = [k ^ mask for k in kinds]
            grp_parts.append((other, tuple(("grp^", k) for k in kinds_other)))
            held, kinds = jnp.concatenate([held, other], 0), kinds + kinds_other
            mask //= 2
    else:
        for o in range(1, groups):
            grp_parts.append((from_ahead(own, "grp", o), (("grp", o),)))

    sums = visit([(own, (("self", 0),))], None)
    for i in range(max(len(blk_parts), len(grp_parts))):
        sums = visit(blk_parts[i : i + 1] + grp_parts[i : i + 1], sums)

    grad, share = pl.pallas_call(
        finish_kernel,
        out_shape=(jax.ShapeDtypeStruct((3, verts), F32), jax.ShapeDtypeStruct((ROWS, LANES), F32)),
        in_specs=[VMEM] * 4,
        out_specs=(VMEM, VMEM),
    )(own, edges, sums, faces)
    for axis, size in (("grp", groups), ("blk", blocks)):
        if size & (size - 1) == 0:
            mask = 1
            while mask < size:
                share = share + flip(share, axis, mask)
                mask *= 2
        else:
            share = share + sum(from_ahead(share, axis, o) for o in range(1, size))
    energy = share[0, 0:1] / (count * count * groups * blocks)
    return grad, energy


def solution(mesh):
    placed = (
        P(None, ("grp", "blk")),
        P(None, ("grp", "blk")),
        P(None, ("grp", "blk")),
        P("grp"),
        P(("grp", "blk")),
        P(),
    )
    return jax.shard_map(
        shards,
        mesh=mesh,
        in_specs=placed,
        out_specs=(P(None, ("grp", "blk")), P()),
        check_vma=False,
    )
```

```python
import functools

import jax
import jax.numpy as jnp
from jax import lax
from jax.experimental import pallas as pl
from jax.experimental.pallas import tpu as pltpu
from jax.sharding import PartitionSpec as P

HOPS = 4
EPS2 = 0.05
ROWS = 8
LANES = 128
DEPTH = 64
SUMS = 10
F32 = jnp.float32
BF16 = jnp.bfloat16
VMEM = pl.BlockSpec(memory_space=pltpu.VMEM)
SMEM = pl.BlockSpec(memory_space=pltpu.SMEM)
FLOPS_PER_PAIR = 8000


def flip(value, axis, mask):
    count = lax.axis_size(axis)
    return lax.ppermute(value, axis, [(i, i ^ mask) for i in range(count)])


def from_ahead(value, axis, by):
    count = lax.axis_size(axis)
    return lax.ppermute(value, axis, [(i, (i - by) % count) for i in range(count)])


def pieces(value):
    high = value.astype(BF16).astype(F32)
    rest = value - high
    middle = rest.astype(BF16).astype(F32)
    return high, middle, rest - middle


def one_hot(row, count):
    rows = lax.broadcasted_iota(jnp.int32, (count, row.shape[1]), 0)
    return jnp.where(rows == row, 1.0, 0.0).astype(BF16)


def geometry_kernel(accepted, vertices, trial_step, faces, weight, own, edges, padded):
    verts = vertices.shape[1]
    count = faces.shape[1]
    padded[...] = jnp.zeros_like(padded)
    padded[0:3, :] = vertices[...] + accepted[0].astype(F32) * trial_step[...]
    left = jnp.concatenate(pieces(padded[...]), 0).astype(BF16)

    def corner(k):
        picked = jnp.dot(left, one_hot(faces[k : k + 1, :], verts), preferred_element_type=F32)
        picked = picked[0:ROWS] + picked[ROWS : 2 * ROWS] + picked[2 * ROWS : 3 * ROWS]
        return [picked[c : c + 1] for c in range(3)]

    first, second, third = corner(0), corner(1), corner(2)
    center = [(first[c] + second[c] + third[c]) / 3.0 for c in range(3)]
    e1 = [second[c] - first[c] for c in range(3)]
    e2 = [third[c] - first[c] for c in range(3)]
    area = []
    for c in range(3):
        n, m = (c + 1) % 3, (c + 2) % 3
        area.append(0.5 * (e1[n] * e2[m] - e1[m] * e2[n]))
    for c in range(3):
        own[c : c + 1, :] = center[c]
        own[3 + c : 4 + c, :] = area[c]
        edges[c : c + 1, :] = e1[c]
        edges[3 + c : 4 + c, :] = e2[c]
    own[6:7, :] = weight[...].reshape(1, count)
    own[7:8, :] = center[0] * area[0] + center[1] * area[1] + center[2] * area[2]
    edges[6:8, :] = jnp.zeros((2, count), F32)


def window_times(offset, blocks):
    return sum(int((k - offset) % blocks == 0) + int((k + offset) % blocks == 0) for k in range(1, HOPS + 1))


def partner_times(shift, here, there, groups):
    times = jnp.int32(0)
    for r in range(shift.shape[0]):
        times += (lax.rem(here + shift[r, here], groups) == there).astype(jnp.int32)
        times += (lax.rem(there + shift[r, there], groups) == here).astype(jnp.int32)
    return times


def place_of(mask, size):
    place, step, bit = 0, 1, size // 2
    while bit:
        place = place + jnp.bitwise_and(mask // bit, 1) * step
        step, bit = step * 2, bit // 2
    return place


def tiles_kernel(plan, groups, blocks, unit, cut, factor, carry, *refs):
    shift, own = refs[0], refs[1]
    arrays = 1 + max(item[0] for item in plan)
    others = refs[2 : 2 + arrays]
    at = 2 + arrays
    total, share_in = None, None
    if carry:
        total = refs[at]
        at += 1
        if factor:
            share_in = refs[at]
            at += 1
    out = refs[at]
    at += 1
    if factor:
        share = refs[at]
        at += 1
    columns, left, right, wide0, wide1, proj0, proj1, sums = refs[at:]
    count = own.shape[1]
    chunks = count // LANES
    part = unit // chunks
    kept = SUMS + (1 if factor else 0)
    row = lax.broadcasted_iota(jnp.int32, (ROWS, count), 0)
    zero = jnp.zeros((ROWS, count), F32)
    zero1, zero3 = jnp.zeros((1, count), F32), jnp.zeros((3, count), F32)
    from_own = jnp.concatenate([-own[3:6, :], zero3, own[7:8, :], zero1], 0)
    from_other = jnp.concatenate([zero3, own[0:3, :], zero1, zero1 - 1.0], 0)
    for side, rows in enumerate((from_own, from_other)):
        high, middle, low = pieces(rows)
        right[:, side * count : (side + 1) * count] = jnp.concatenate(
            [zero, high, middle, low, high, middle, high, zero], 0
        ).astype(BF16)
    for t, (source, index, axis, offset) in enumerate(plan):
        if index == "ring":
            size = groups if axis == "grp" else blocks
            here = lax.axis_index(axis)
            there = lax.rem(here + offset, size)
            first = size // 2 // (offset & -offset)
            block = others[source][place_of(jnp.bitwise_xor(here, there), size) - first]
        elif index is None:
            block = others[source][...]
        else:
            block = others[source][index]
        if axis == "self":
            times = 1.0 + window_times(0, blocks)
        elif axis == "blk":
            times = float(window_times(offset, blocks))
        else:
            here = lax.axis_index("grp")
            times = partner_times(shift, here, lax.rem(here + offset, groups), groups).astype(F32)
        block = jnp.where(row == 6, block * times, block)
        high, middle, low = pieces(jnp.where(row == 6, 1.0, block))
        turned = jnp.concatenate([block, high, high, high, middle, middle, low, zero], 0).T
        columns[t * count : (t + 1) * count, :] = turned[:, 0:ROWS]
        left[t * count : (t + 1) * count, :] = turned.astype(BF16)
    for k in range(kept):
        sums[k] = zero

    def fill(u, chunk, wide, proj):
        source = pl.multiple_of(u * unit + chunk * part, part)
        target = pl.multiple_of(chunk * part, part)
        proj[pl.ds(target, part), :] = jnp.dot(left[pl.ds(source, part), :], right[...], preferred_element_type=F32)
        for g in range(part // ROWS):
            group = columns[pl.ds(pl.multiple_of(source + g * ROWS, ROWS), ROWS), :]
            for k in range(7):
                wide[k, pl.ds(pl.multiple_of(target + g * ROWS, ROWS), ROWS), :] = jnp.broadcast_to(
                    group[:, k : k + 1], (ROWS, LANES)
                )

    def work(chunk, wide, proj, next_wide, next_proj):
        at_lane = pl.multiple_of(chunk * LANES, LANES)
        span = pl.ds(at_lane, LANES)
        a = [jnp.broadcast_to(own[k : k + 1, span], (ROWS, LANES)) for k in range(3)]
        s = [sums[k, :, span] for k in range(kept)]
        for g in range(unit // ROWS):
            if g == cut:
                stored = pl.ds(pl.multiple_of(chunk * part, ROWS), ROWS)
                seen = next_wide[6, stored, :] + next_proj[stored, 0:LANES]
                s[6] = s[6] + jnp.where(chunk < 0, seen, 0.0)
            rows = slice(g * ROWS, (g + 1) * ROWS)
            b = [wide[k, rows, :] for k in range(7)]
            proj_a = proj[rows, span]
            proj_b = proj[rows, pl.ds(pl.multiple_of(count + at_lane, LANES), LANES)]
            d0, d1, d2 = a[0] - b[0], a[1] - b[1], a[2] - b[2]
            dist = d0 * d0 + d1 * d1 + (d2 * d2 + EPS2)
            inverse = 1.0 / dist
            square = inverse * inverse * b[6]
            alpha = proj_a * square
            beta = proj_b * square
            kernel = proj_a * alpha + proj_b * beta
            gamma = kernel * inverse
            s[0] += beta * b[3]
            s[1] += beta * b[4]
            s[2] += beta * b[5]
            s[3] += alpha * d0
            s[4] += alpha * d1
            s[5] += alpha * d2
            s[6] += alpha
            s[7] += gamma * d0
            s[8] += gamma * d1
            s[9] += gamma * d2
            if factor:
                s[10] += kernel
        for k in range(kept):
            sums[k, :, span] = s[k]

    def over_chunks(visit):
        def step(chunk, carried):
            visit(chunk)
            return carried

        lax.fori_loop(0, chunks, step, 0)

    units = len(plan) * count // unit
    for chunk in range(chunks):
        fill(0, chunk, wide0, proj0)

    def pair(step, carried):
        def even(chunk):
            fill(2 * step + 1, chunk, wide1, proj1)
            work(chunk, wide0, proj0, wide1, proj1)

        def odd(chunk):
            fill(jnp.minimum(2 * step + 2, units - 1), chunk, wide0, proj0)
            work(chunk, wide1, proj1, wide0, proj0)

        over_chunks(even)
        over_chunks(odd)
        return carried

    lax.fori_loop(0, units // 2, pair, 0)
    for k in range(SUMS):
        line = jnp.sum(sums[k], axis=0, keepdims=True)
        out[k : k + 1, :] = line + total[k : k + 1, :] if carry else line
    if factor:
        weighted = sums[SUMS] * (factor * own[6:7, :])
        part_share = weighted[:, 0:LANES]
        for chunk in range(1, chunks):
            part_share = part_share + weighted[:, chunk * LANES : (chunk + 1) * LANES]
        share[...] = part_share + share_in[...] if carry else part_share


def tiles(shift, own, arrays, plan, factor, carried, groups, blocks):
    count = own.shape[1]
    number = len(plan)
    unit = min(count // 2, 256)
    groups_in_unit = unit // ROWS
    cut = groups_in_unit - max(1, groups_in_unit // 8)
    body = functools.partial(tiles_kernel, plan, groups, blocks, unit, cut, factor, carried is not None)
    operands = [shift, own, *arrays]
    if carried is not None:
        operands += [carried[0]] + ([carried[1]] if factor else [])
    shapes = [jax.ShapeDtypeStruct((SUMS, count), F32)]
    if factor:
        shapes.append(jax.ShapeDtypeStruct((ROWS, LANES), F32))
    pairs = number * count * count
    result = pl.pallas_call(
        body,
        out_shape=shapes,
        in_specs=[SMEM] + [VMEM] * (len(operands) - 1),
        out_specs=[VMEM] * len(shapes),
        scratch_shapes=[
            pltpu.VMEM((number * count, ROWS), F32),
            pltpu.VMEM((number * count, DEPTH), BF16),
            pltpu.VMEM((DEPTH, 2 * count), BF16),
            pltpu.VMEM((7, unit, LANES), F32),
            pltpu.VMEM((7, unit, LANES), F32),
            pltpu.VMEM((unit, 2 * count), F32),
            pltpu.VMEM((unit, 2 * count), F32),
            pltpu.VMEM((SUMS + 1, ROWS, count), F32),
        ],
        cost_estimate=pl.CostEstimate(
            flops=FLOPS_PER_PAIR * pairs, bytes_accessed=32 * count * number, transcendentals=pairs
        ),
    )(*operands)
    share = result[1] if factor else (carried[1] if carried is not None else None)
    return result[0], share


def finish_kernel(own, edges, sums, faces, grad):
    verts = grad.shape[1]
    count = own.shape[1]
    twice = 2.0 * own[6:7, :]
    total = sums[6:7, :]
    g_center = [
        twice * (own[3 + c : 4 + c, :] * total + sums[c : c + 1, :] - 2.0 * sums[7 + c : 8 + c, :]) for c in range(3)
    ]
    g_area = [twice * sums[3 + c : 4 + c, :] for c in range(3)]
    e1 = [edges[c : c + 1, :] for c in range(3)]
    e2 = [edges[3 + c : 4 + c, :] for c in range(3)]
    zero = jnp.zeros((ROWS - 3, count), F32)
    corners = [[], [], []]
    for c in range(3):
        n, m = (c + 1) % 3, (c + 2) % 3
        g1 = 0.5 * (e2[n] * g_area[m] - e2[m] * g_area[n])
        g2 = 0.5 * (g_area[n] * e1[m] - g_area[m] * e1[n])
        part = g_center[c] / 3.0
        corners[0].append(part - g1 - g2)
        corners[1].append(part + g1)
        corners[2].append(part + g2)
    total = jnp.zeros((3 * ROWS, verts), F32)
    for k in range(3):
        left = jnp.concatenate(pieces(jnp.concatenate(corners[k] + [zero], 0)), 0).astype(BF16)
        total += lax.dot_general(
            left, one_hot(faces[k : k + 1, :], verts), (((1,), (1,)), ((), ())), preferred_element_type=F32
        )
    total = total[0:ROWS] + total[ROWS : 2 * ROWS] + total[2 * ROWS : 3 * ROWS]
    grad[...] = total[0:3] / count


def gather(own, axis, size, wanted):
    if size & (size - 1) == 0 and len(wanted) == size - 1:
        found = {}
        held = own[None]
        mask = size // 2
        while mask:
            other = flip(held, axis, mask)
            for offset in wanted:
                if offset & -offset == mask:
                    found[offset] = (other, "ring")
            held = jnp.concatenate([held, other], 0) if mask > 1 else held
            mask //= 2
        return found
    return {offset: (from_ahead(own, axis, offset), None) for offset in wanted}


def shards(vertices, faces, trial_step, accepted, face_weight, partner_shift):
    count = faces.shape[1]
    verts = vertices.shape[1]
    groups, blocks = lax.axis_size("grp"), lax.axis_size("blk")
    block_shape = jax.ShapeDtypeStruct((ROWS, count), F32)
    own, edges = pl.pallas_call(
        geometry_kernel,
        out_shape=(block_shape, block_shape),
        in_specs=[SMEM] + [VMEM] * 4,
        out_specs=(VMEM, VMEM),
        scratch_shapes=[pltpu.VMEM((ROWS, verts), F32)],
    )(accepted, vertices, trial_step, faces, face_weight)

    window = [o for o in range(1, blocks) if window_times(o, blocks)]
    ring = gather(own, "blk", blocks, window)
    across = gather(own, "grp", groups, list(range(1, groups)))

    def visit(items, factor, carried):
        arrays, plan = [], []
        for axis, offset in items:
            if axis == "self":
                array, index = own, None
            else:
                array, index = (ring if axis == "blk" else across)[offset]
            where = [i for i, known in enumerate(arrays) if known is array]
            if not where:
                arrays.append(array)
                where = [len(arrays) - 1]
            plan.append((where[0], index, axis, offset))
        return tiles(partner_shift, own, arrays, tuple(plan), factor, carried, groups, blocks)

    def stage(offset, size):
        return -(offset & -offset) if size & (size - 1) == 0 else 0

    middle = [("blk", o) for o in window if 2 * o == blocks] + [("grp", o) for o in range(1, groups) if 2 * o == groups]
    early_blk = sorted((o for o in window if 2 * o < blocks), key=lambda o: (stage(o, blocks), o))
    early_grp = [("grp", o) for o in range(1, groups) if 2 * o < groups]
    late = [("grp", o) for o in range(1, groups) if 2 * o > groups]
    late += [("blk", o) for o in sorted((o for o in window if 2 * o > blocks), key=lambda o: (stage(o, blocks), o))]
    first = early_grp + [("blk", o) for o in early_blk[: len(early_blk) // 3]]
    second = [("blk", o) for o in early_blk[len(early_blk) // 3 :]]

    carried = visit([("self", 0)], 0.5, None)
    for items, factor in ((middle, 0.5), (first, 1.0), (second, 1.0)):
        if items:
            carried = visit(items, factor, carried)
    share = carried[1]
    half = len(late) // 2
    for items in (late[:half], late[half:]):
        if items:
            carried = visit(items, 0.0, carried)

    grad = pl.pallas_call(
        finish_kernel,
        out_shape=jax.ShapeDtypeStruct((3, verts), F32),
        in_specs=[VMEM] * 4,
        out_specs=VMEM,
        cost_estimate=pl.CostEstimate(flops=1500000000, bytes_accessed=64 * count, transcendentals=0),
    )(own, edges, carried[0], faces)
    for axis, size in (("blk", blocks), ("grp", groups)):
        if size & (size - 1) == 0:
            mask = size // 2
            while mask:
                share = share + flip(share, axis, mask)
                mask //= 2
        else:
            share = share + sum(from_ahead(share, axis, o) for o in range(1, size))
    energy = jnp.sum(share) / (count * count * groups * blocks)
    return grad, energy.reshape(1)


def solution(mesh):
    placed = (
        P(None, ("grp", "blk")),
        P(None, ("grp", "blk")),
        P(None, ("grp", "blk")),
        P("grp"),
        P(("grp", "blk")),
        P(),
    )
    return jax.shard_map(
        shards,
        mesh=mesh,
        in_specs=placed,
        out_specs=(P(None, ("grp", "blk")), P()),
        check_vma=False,
    )
```

```python
import functools

import jax
import jax.numpy as jnp
from jax import lax
from jax.experimental import pallas as pl
from jax.experimental.pallas import tpu as pltpu
from jax.sharding import PartitionSpec as P

HOPS = 4
EPS2 = 0.05
ROWS = 8
LANES = 128
DEPTH = 64
SUMS = 10
F32 = jnp.float32
BF16 = jnp.bfloat16
VMEM = pl.BlockSpec(memory_space=pltpu.VMEM)
SMEM = pl.BlockSpec(memory_space=pltpu.SMEM)
FLOPS_PER_PAIR = 8000
PARAMS = pltpu.CompilerParams(vmem_limit_bytes=16 * 1024 * 1024)


def flip(value, axis, mask):
    count = lax.axis_size(axis)
    return lax.ppermute(value, axis, [(i, i ^ mask) for i in range(count)])


def from_ahead(value, axis, by):
    count = lax.axis_size(axis)
    return lax.ppermute(value, axis, [(i, (i - by) % count) for i in range(count)])


def pieces(value):
    high = value.astype(BF16).astype(F32)
    rest = value - high
    middle = rest.astype(BF16).astype(F32)
    return high, middle, rest - middle


def one_hot(row, count):
    rows = lax.broadcasted_iota(jnp.int32, (count, row.shape[1]), 0)
    return jnp.where(rows == row, 1.0, 0.0).astype(BF16)


def geometry_kernel(accepted, vertices, trial_step, faces, weight, own, edges, padded):
    verts = vertices.shape[1]
    count = faces.shape[1]
    padded[...] = jnp.zeros_like(padded)
    padded[0:3, :] = vertices[...] + accepted[0].astype(F32) * trial_step[...]
    left = jnp.concatenate(pieces(padded[...]), 0).astype(BF16)

    def corner(k):
        picked = jnp.dot(left, one_hot(faces[k : k + 1, :], verts), preferred_element_type=F32)
        picked = picked[0:ROWS] + picked[ROWS : 2 * ROWS] + picked[2 * ROWS : 3 * ROWS]
        return [picked[c : c + 1] for c in range(3)]

    first, second, third = corner(0), corner(1), corner(2)
    center = [(first[c] + second[c] + third[c]) / 3.0 for c in range(3)]
    e1 = [second[c] - first[c] for c in range(3)]
    e2 = [third[c] - first[c] for c in range(3)]
    area = []
    for c in range(3):
        n, m = (c + 1) % 3, (c + 2) % 3
        area.append(0.5 * (e1[n] * e2[m] - e1[m] * e2[n]))
    for c in range(3):
        own[c : c + 1, :] = center[c]
        own[3 + c : 4 + c, :] = area[c]
        edges[c : c + 1, :] = e1[c]
        edges[3 + c : 4 + c, :] = e2[c]
    own[6:7, :] = weight[...].reshape(1, count)
    own[7:8, :] = center[0] * area[0] + center[1] * area[1] + center[2] * area[2]
    edges[6:8, :] = jnp.zeros((2, count), F32)


def window_times(offset, blocks):
    return sum(int((k - offset) % blocks == 0) + int((k + offset) % blocks == 0) for k in range(1, HOPS + 1))


def partner_times(shift, here, there, groups):
    times = jnp.int32(0)
    for r in range(shift.shape[0]):
        times += (lax.rem(here + shift[r, here], groups) == there).astype(jnp.int32)
        times += (lax.rem(there + shift[r, there], groups) == here).astype(jnp.int32)
    return times


def place_of(mask, size):
    place, step, bit = 0, 1, size // 2
    while bit:
        place = place + jnp.bitwise_and(mask // bit, 1) * step
        step, bit = step * 2, bit // 2
    return place


def tiles_kernel(plan, groups, blocks, unit, cut, factor, carry, *refs):
    shift, own = refs[0], refs[1]
    arrays = 1 + max(item[0] for item in plan)
    others = refs[2 : 2 + arrays]
    at = 2 + arrays
    total, share_in = None, None
    if carry:
        total = refs[at]
        at += 1
        if factor:
            share_in = refs[at]
            at += 1
    out = refs[at]
    at += 1
    if factor:
        share = refs[at]
        at += 1
    columns, left, right, wide0, wide1, proj0, proj1, sums = refs[at:]
    count = own.shape[1]
    chunks = count // LANES
    part = unit // chunks
    kept = SUMS + (1 if factor else 0)
    row = lax.broadcasted_iota(jnp.int32, (ROWS, count), 0)
    zero = jnp.zeros((ROWS, count), F32)
    zero1, zero3 = jnp.zeros((1, count), F32), jnp.zeros((3, count), F32)
    from_own = jnp.concatenate([-own[3:6, :], zero3, own[7:8, :], zero1], 0)
    from_other = jnp.concatenate([zero3, own[0:3, :], zero1, zero1 - 1.0], 0)
    for side, rows in enumerate((from_own, from_other)):
        high, middle, low = pieces(rows)
        right[:, side * count : (side + 1) * count] = jnp.concatenate(
            [zero, high, middle, low, high, middle, high, zero], 0
        ).astype(BF16)
    for t, (source, index, axis, offset) in enumerate(plan):
        if index == "ring":
            size = groups if axis == "grp" else blocks
            here = lax.axis_index(axis)
            there = lax.rem(here + offset, size)
            first = size // 2 // (offset & -offset)
            block = others[source][place_of(jnp.bitwise_xor(here, there), size) - first]
        elif index is None:
            block = others[source][...]
        else:
            block = others[source][index]
        if axis == "self":
            times = 1.0 + window_times(0, blocks)
        elif axis == "blk":
            times = float(window_times(offset, blocks))
        else:
            here = lax.axis_index("grp")
            times = partner_times(shift, here, lax.rem(here + offset, groups), groups).astype(F32)
        block = jnp.where(row == 6, block * times, block)
        high, middle, low = pieces(jnp.where(row == 6, 1.0, block))
        turned = jnp.concatenate([block, high, high, high, middle, middle, low, zero], 0).T
        columns[t * count : (t + 1) * count, :] = turned[:, 0:ROWS]
        left[t * count : (t + 1) * count, :] = turned.astype(BF16)
    for k in range(kept):
        sums[k] = zero

    def fill(u, chunk, wide, proj):
        source = pl.multiple_of(u * unit + chunk * part, part)
        target = pl.multiple_of(chunk * part, part)
        proj[pl.ds(target, part), :] = jnp.dot(left[pl.ds(source, part), :], right[...], preferred_element_type=F32)
        for g in range(part // ROWS):
            group = columns[pl.ds(pl.multiple_of(source + g * ROWS, ROWS), ROWS), :]
            for k in range(7):
                wide[k, pl.ds(pl.multiple_of(target + g * ROWS, ROWS), ROWS), :] = jnp.broadcast_to(
                    group[:, k : k + 1], (ROWS, LANES)
                )

    def work(chunk, wide, proj, next_wide, next_proj):
        at_lane = pl.multiple_of(chunk * LANES, LANES)
        span = pl.ds(at_lane, LANES)
        a = [jnp.broadcast_to(own[k : k + 1, span], (ROWS, LANES)) for k in range(3)]
        s = [sums[k, :, span] for k in range(kept)]
        for g in range(unit // ROWS):
            if g == cut:
                stored = pl.ds(pl.multiple_of(chunk * part, ROWS), ROWS)
                seen = next_wide[6, stored, :] + next_proj[stored, 0:LANES]
                s[6] = s[6] + jnp.where(chunk < 0, seen, 0.0)
            rows = slice(g * ROWS, (g + 1) * ROWS)
            b = [wide[k, rows, :] for k in range(7)]
            proj_a = proj[rows, span]
            proj_b = proj[rows, pl.ds(pl.multiple_of(count + at_lane, LANES), LANES)]
            d0, d1, d2 = a[0] - b[0], a[1] - b[1], a[2] - b[2]
            dist = d0 * d0 + d1 * d1 + (d2 * d2 + EPS2)
            inverse = 1.0 / dist
            square = inverse * inverse * b[6]
            alpha = proj_a * square
            beta = proj_b * square
            kernel = proj_a * alpha + proj_b * beta
            gamma = kernel * inverse
            s[0] += beta * b[3]
            s[1] += beta * b[4]
            s[2] += beta * b[5]
            s[3] += alpha * d0
            s[4] += alpha * d1
            s[5] += alpha * d2
            s[6] += alpha
            s[7] += gamma * d0
            s[8] += gamma * d1
            s[9] += gamma * d2
            if factor:
                s[10] += kernel
        for k in range(kept):
            sums[k, :, span] = s[k]

    def over_chunks(visit):
        def step(chunk, carried):
            visit(chunk)
            return carried

        lax.fori_loop(0, chunks, step, 0)

    units = len(plan) * count // unit
    for chunk in range(chunks):
        fill(0, chunk, wide0, proj0)

    def pair(step, carried):
        def even(chunk):
            fill(2 * step + 1, chunk, wide1, proj1)
            work(chunk, wide0, proj0, wide1, proj1)

        def odd(chunk):
            fill(jnp.minimum(2 * step + 2, units - 1), chunk, wide0, proj0)
            work(chunk, wide1, proj1, wide0, proj0)

        over_chunks(even)
        over_chunks(odd)
        return carried

    lax.fori_loop(0, units // 2, pair, 0)
    for k in range(SUMS):
        line = jnp.sum(sums[k], axis=0, keepdims=True)
        out[k : k + 1, :] = line + total[k : k + 1, :] if carry else line
    if factor:
        weighted = sums[SUMS] * (factor * own[6:7, :])
        part_share = weighted[:, 0:LANES]
        for chunk in range(1, chunks):
            part_share = part_share + weighted[:, chunk * LANES : (chunk + 1) * LANES]
        share[...] = part_share + share_in[...] if carry else part_share


def tiles(shift, own, arrays, plan, factor, carried, groups, blocks):
    count = own.shape[1]
    number = len(plan)
    unit = min(count // 2, 256)
    groups_in_unit = unit // ROWS
    cut = groups_in_unit - max(1, groups_in_unit // 8)
    body = functools.partial(tiles_kernel, plan, groups, blocks, unit, cut, factor, carried is not None)
    operands = [shift, own, *arrays]
    if carried is not None:
        operands += [carried[0]] + ([carried[1]] if factor else [])
    shapes = [jax.ShapeDtypeStruct((SUMS, count), F32)]
    if factor:
        shapes.append(jax.ShapeDtypeStruct((ROWS, LANES), F32))
    pairs = number * count * count
    result = pl.pallas_call(
        body,
        out_shape=shapes,
        in_specs=[SMEM] + [VMEM] * (len(operands) - 1),
        out_specs=[VMEM] * len(shapes),
        scratch_shapes=[
            pltpu.VMEM((number * count, ROWS), F32),
            pltpu.VMEM((number * count, DEPTH), BF16),
            pltpu.VMEM((DEPTH, 2 * count), BF16),
            pltpu.VMEM((7, unit, LANES), F32),
            pltpu.VMEM((7, unit, LANES), F32),
            pltpu.VMEM((unit, 2 * count), F32),
            pltpu.VMEM((unit, 2 * count), F32),
            pltpu.VMEM((SUMS + 1, ROWS, count), F32),
        ],
        compiler_params=PARAMS,
        cost_estimate=pl.CostEstimate(
            flops=FLOPS_PER_PAIR * pairs, bytes_accessed=32 * count * number, transcendentals=pairs
        ),
    )(*operands)
    share = result[1] if factor else (carried[1] if carried is not None else None)
    return result[0], share


def finish_kernel(own, edges, sums, faces, grad):
    verts = grad.shape[1]
    count = own.shape[1]
    twice = 2.0 * own[6:7, :]
    total = sums[6:7, :]
    g_center = [
        twice * (own[3 + c : 4 + c, :] * total + sums[c : c + 1, :] - 2.0 * sums[7 + c : 8 + c, :]) for c in range(3)
    ]
    g_area = [twice * sums[3 + c : 4 + c, :] for c in range(3)]
    e1 = [edges[c : c + 1, :] for c in range(3)]
    e2 = [edges[3 + c : 4 + c, :] for c in range(3)]
    zero = jnp.zeros((ROWS - 3, count), F32)
    corners = [[], [], []]
    for c in range(3):
        n, m = (c + 1) % 3, (c + 2) % 3
        g1 = 0.5 * (e2[n] * g_area[m] - e2[m] * g_area[n])
        g2 = 0.5 * (g_area[n] * e1[m] - g_area[m] * e1[n])
        part = g_center[c] / 3.0
        corners[0].append(part - g1 - g2)
        corners[1].append(part + g1)
        corners[2].append(part + g2)
    total = jnp.zeros((3 * ROWS, verts), F32)
    for k in range(3):
        left = jnp.concatenate(pieces(jnp.concatenate(corners[k] + [zero], 0)), 0).astype(BF16)
        total += lax.dot_general(
            left, one_hot(faces[k : k + 1, :], verts), (((1,), (1,)), ((), ())), preferred_element_type=F32
        )
    total = total[0:ROWS] + total[ROWS : 2 * ROWS] + total[2 * ROWS : 3 * ROWS]
    grad[...] = total[0:3] / count


def gather(own, axis, size, wanted):
    if size & (size - 1) == 0 and len(wanted) == size - 1:
        found = {}
        held = own[None]
        mask = size // 2
        while mask:
            other = flip(held, axis, mask)
            for offset in wanted:
                if offset & -offset == mask:
                    found[offset] = (other, "ring")
            held = jnp.concatenate([held, other], 0) if mask > 1 else held
            mask //= 2
        return found
    return {offset: (from_ahead(own, axis, offset), None) for offset in wanted}


def shards(vertices, faces, trial_step, accepted, face_weight, partner_shift):
    count = faces.shape[1]
    verts = vertices.shape[1]
    groups, blocks = lax.axis_size("grp"), lax.axis_size("blk")
    block_shape = jax.ShapeDtypeStruct((ROWS, count), F32)
    own, edges = pl.pallas_call(
        geometry_kernel,
        out_shape=(block_shape, block_shape),
        in_specs=[SMEM] + [VMEM] * 4,
        out_specs=(VMEM, VMEM),
        scratch_shapes=[pltpu.VMEM((ROWS, verts), F32)],
        compiler_params=PARAMS,
    )(accepted, vertices, trial_step, faces, face_weight)

    window = [o for o in range(1, blocks) if window_times(o, blocks)]
    ring = gather(own, "blk", blocks, window)
    across = gather(own, "grp", groups, list(range(1, groups)))

    def visit(items, factor, carried):
        arrays, plan = [], []
        for axis, offset in items:
            if axis == "self":
                array, index = own, None
            else:
                array, index = (ring if axis == "blk" else across)[offset]
            where = [i for i, known in enumerate(arrays) if known is array]
            if not where:
                arrays.append(array)
                where = [len(arrays) - 1]
            plan.append((where[0], index, axis, offset))
        return tiles(partner_shift, own, arrays, tuple(plan), factor, carried, groups, blocks)

    def stage(offset, size):
        return -(offset & -offset) if size & (size - 1) == 0 else 0

    middle = [("blk", o) for o in window if 2 * o == blocks] + [("grp", o) for o in range(1, groups) if 2 * o == groups]
    early_blk = sorted((o for o in window if 2 * o < blocks), key=lambda o: (stage(o, blocks), o))
    early_grp = [("grp", o) for o in range(1, groups) if 2 * o < groups]
    late = [("grp", o) for o in range(1, groups) if 2 * o > groups]
    late += [("blk", o) for o in sorted((o for o in window if 2 * o > blocks), key=lambda o: (stage(o, blocks), o))]
    first = early_grp + [("blk", o) for o in early_blk[: len(early_blk) // 3]]
    second = [("blk", o) for o in early_blk[len(early_blk) // 3 :]]

    carried = visit([("self", 0)], 0.5, None)
    for items, factor in ((middle, 0.5), (first, 1.0), (second, 1.0)):
        if items:
            carried = visit(items, factor, carried)
    total, share = carried
    rounds = []
    for axis, size in (("blk", blocks), ("grp", groups)):
        if size & (size - 1) == 0:
            rounds += [(axis, size >> k) for k in range(1, size.bit_length())]
        else:
            rounds.append((axis, 0))

    def exchange(value, axis, mask):
        if mask:
            return flip(value, axis, mask)
        return sum(from_ahead(value, axis, o) for o in range(1, lax.axis_size(axis)))

    def last_of(total):
        return pl.pallas_call(
            finish_kernel,
            out_shape=jax.ShapeDtypeStruct((3, verts), F32),
            in_specs=[VMEM] * 4,
            out_specs=VMEM,
            compiler_params=PARAMS,
            cost_estimate=pl.CostEstimate(flops=1500000000, bytes_accessed=64 * count, transcendentals=0),
        )(own, edges, total, faces)

    half = len(late) // 2
    covers = [functools.partial(visit, items, 0.0) for items in (late[:half], late[half:]) if items]
    for index, (axis, mask) in enumerate(rounds):
        received = exchange(share, axis, mask)
        if index < len(covers):
            total = covers[index]((total, None))[0]
            total, received = lax.optimization_barrier((total, received))
        elif index == len(covers):
            grad, received = lax.optimization_barrier((last_of(total), received))
        share = share + received
    if len(rounds) <= len(covers):
        for cover in covers[len(rounds) :]:
            total = cover((total, None))[0]
        grad = last_of(total)
    energy = jnp.sum(share) / (count * count * groups * blocks)
    return grad, energy.reshape(1)


def solution(mesh):
    placed = (
        P(None, ("grp", "blk")),
        P(None, ("grp", "blk")),
        P(None, ("grp", "blk")),
        P("grp"),
        P(("grp", "blk")),
        P(),
    )
    return jax.shard_map(
        shards,
        mesh=mesh,
        in_specs=placed,
        out_specs=(P(None, ("grp", "blk")), P()),
        check_vma=False,
    )
```

```python
import functools

import jax
import jax.numpy as jnp
from jax import lax
from jax.experimental import pallas as pl
from jax.experimental.pallas import tpu as pltpu
from jax.sharding import PartitionSpec as P

HOPS = 4
EPS2 = 0.05
ROWS = 8
LANES = 128
DEPTH = 64
SUMS = 10
F32 = jnp.float32
BF16 = jnp.bfloat16
VMEM = pl.BlockSpec(memory_space=pltpu.VMEM)
SMEM = pl.BlockSpec(memory_space=pltpu.SMEM)
FLOPS_PER_PAIR = 8000
PARAMS = pltpu.CompilerParams(vmem_limit_bytes=16 * 1024 * 1024)


def flip(value, axis, mask):
    count = lax.axis_size(axis)
    return lax.ppermute(value, axis, [(i, i ^ mask) for i in range(count)])


def from_ahead(value, axis, by):
    count = lax.axis_size(axis)
    return lax.ppermute(value, axis, [(i, (i - by) % count) for i in range(count)])


def pieces(value):
    high = value.astype(BF16).astype(F32)
    rest = value - high
    middle = rest.astype(BF16).astype(F32)
    return high, middle, rest - middle


def one_hot(row, count):
    rows = lax.broadcasted_iota(jnp.int32, (count, row.shape[1]), 0)
    return jnp.where(rows == row, 1.0, 0.0).astype(BF16)


def partner_times(shift, here, there, groups):
    times = jnp.int32(0)
    for r in range(shift.shape[0]):
        times += (lax.rem(here + shift[r, here], groups) == there).astype(jnp.int32)
        times += (lax.rem(there + shift[r, there], groups) == here).astype(jnp.int32)
    return times


def geometry_kernel(groups, accepted, shift, v_far, t_far, f_far, w_far, own, edges, times, *scratch):
    vertices, trial_step, faces, weight, padded, arrived = scratch
    copies = [
        pltpu.make_async_copy(far, near, arrived.at[i])
        for i, (far, near) in enumerate(
            ((v_far, vertices), (t_far, trial_step), (f_far, faces), (w_far, weight))
        )
    ]
    for copy in copies:
        copy.start()
    verts = vertices.shape[1]
    count = faces.shape[1]
    padded[...] = jnp.zeros_like(padded)
    here = lax.axis_index("grp")
    times[...] = jnp.zeros_like(times)
    for offset in range(1, groups):
        met = partner_times(shift, here, lax.rem(here + offset, groups), groups).astype(F32)
        times[offset : offset + 1, :] = jnp.zeros((1, LANES), F32) + met
    for copy in copies:
        copy.wait()
    padded[0:3, :] = vertices[...] + accepted[0].astype(F32) * trial_step[...]
    left = jnp.concatenate(pieces(padded[...]), 0).astype(BF16)

    def corner(k):
        picked = jnp.dot(left, one_hot(faces[k : k + 1, :], verts), preferred_element_type=F32)
        picked = picked[0:ROWS] + picked[ROWS : 2 * ROWS] + picked[2 * ROWS : 3 * ROWS]
        return [picked[c : c + 1] for c in range(3)]

    first, second, third = corner(0), corner(1), corner(2)
    center = [(first[c] + second[c] + third[c]) / 3.0 for c in range(3)]
    e1 = [second[c] - first[c] for c in range(3)]
    e2 = [third[c] - first[c] for c in range(3)]
    area = []
    for c in range(3):
        n, m = (c + 1) % 3, (c + 2) % 3
        area.append(0.5 * (e1[n] * e2[m] - e1[m] * e2[n]))
    for c in range(3):
        own[c : c + 1, :] = center[c]
        own[3 + c : 4 + c, :] = area[c]
        edges[c : c + 1, :] = e1[c]
        edges[3 + c : 4 + c, :] = e2[c]
    own[6:7, :] = weight[...].reshape(1, count)
    own[7:8, :] = center[0] * area[0] + center[1] * area[1] + center[2] * area[2]
    edges[6:8, :] = jnp.zeros((2, count), F32)


def window_times(offset, blocks):
    return sum(int((k - offset) % blocks == 0) + int((k + offset) % blocks == 0) for k in range(1, HOPS + 1))


def place_of(mask, size):
    place, step, bit = 0, 1, size // 2
    while bit:
        place = place + jnp.bitwise_and(mask // bit, 1) * step
        step, bit = step * 2, bit // 2
    return place


def tiles_kernel(plan, groups, blocks, unit, cut, factor, carry, *refs):
    met, own = refs[0], refs[1]
    arrays = 1 + max(item[0] for item in plan)
    others = refs[2 : 2 + arrays]
    at = 2 + arrays
    total, share_in = None, None
    if carry:
        total = refs[at]
        at += 1
        if factor:
            share_in = refs[at]
            at += 1
    out = refs[at]
    at += 1
    if factor:
        share = refs[at]
        at += 1
    columns, left, right, wide0, wide1, proj0, proj1, sums = refs[at:]
    count = own.shape[1]
    chunks = count // LANES
    part = unit // chunks
    kept = SUMS + (1 if factor else 0)
    row = lax.broadcasted_iota(jnp.int32, (ROWS, count), 0)
    zero = jnp.zeros((ROWS, count), F32)
    zero1, zero3 = jnp.zeros((1, count), F32), jnp.zeros((3, count), F32)
    from_own = jnp.concatenate([-own[3:6, :], zero3, own[7:8, :], zero1], 0)
    from_other = jnp.concatenate([zero3, own[0:3, :], zero1, zero1 - 1.0], 0)
    for side, rows in enumerate((from_own, from_other)):
        high, middle, low = pieces(rows)
        right[:, side * count : (side + 1) * count] = jnp.concatenate(
            [zero, high, middle, low, high, middle, high, zero], 0
        ).astype(BF16)
    for t, (source, index, axis, offset) in enumerate(plan):
        if index == "ring":
            size = groups if axis == "grp" else blocks
            here = lax.axis_index(axis)
            there = lax.rem(here + offset, size)
            first = size // 2 // (offset & -offset)
            block = others[source][place_of(jnp.bitwise_xor(here, there), size) - first]
        elif index is None:
            block = others[source][...]
        else:
            block = others[source][index]
        if axis == "self":
            times = 1.0 + window_times(0, blocks)
        elif axis == "blk":
            times = float(window_times(offset, blocks))
        else:
            times = jnp.concatenate([met[offset : offset + 1, :]] * chunks, 1)
        block = jnp.where(row == 6, block * times, block)
        high, middle, low = pieces(jnp.where(row == 6, 1.0, block))
        turned = jnp.concatenate([block, high, high, high, middle, middle, low, zero], 0).T
        columns[t * count : (t + 1) * count, :] = turned[:, 0:ROWS]
        left[t * count : (t + 1) * count, :] = turned.astype(BF16)
    for k in range(kept):
        sums[k] = zero

    def fill(u, chunk, wide, proj):
        source = pl.multiple_of(u * unit + chunk * part, part)
        target = pl.multiple_of(chunk * part, part)
        proj[pl.ds(target, part), :] = jnp.dot(left[pl.ds(source, part), :], right[...], preferred_element_type=F32)
        for g in range(part // ROWS):
            group = columns[pl.ds(pl.multiple_of(source + g * ROWS, ROWS), ROWS), :]
            for k in range(7):
                wide[k, pl.ds(pl.multiple_of(target + g * ROWS, ROWS), ROWS), :] = jnp.broadcast_to(
                    group[:, k : k + 1], (ROWS, LANES)
                )

    def work(chunk, wide, proj, next_wide, next_proj):
        at_lane = pl.multiple_of(chunk * LANES, LANES)
        span = pl.ds(at_lane, LANES)
        a = [jnp.broadcast_to(own[k : k + 1, span], (ROWS, LANES)) for k in range(3)]
        s = [sums[k, :, span] for k in range(kept)]
        for g in range(unit // ROWS):
            if g == cut:
                stored = pl.ds(pl.multiple_of(chunk * part, ROWS), ROWS)
                seen = next_wide[6, stored, :] + next_proj[stored, 0:LANES]
                s[6] = s[6] + jnp.where(chunk < 0, seen, 0.0)
            rows = slice(g * ROWS, (g + 1) * ROWS)
            b = [wide[k, rows, :] for k in range(7)]
            proj_a = proj[rows, span]
            proj_b = proj[rows, pl.ds(pl.multiple_of(count + at_lane, LANES), LANES)]
            d0, d1, d2 = a[0] - b[0], a[1] - b[1], a[2] - b[2]
            dist = d0 * d0 + d1 * d1 + (d2 * d2 + EPS2)
            inverse = 1.0 / dist
            square = inverse * inverse * b[6]
            alpha = proj_a * square
            beta = proj_b * square
            kernel = proj_a * alpha + proj_b * beta
            gamma = kernel * inverse
            s[0] += beta * b[3]
            s[1] += beta * b[4]
            s[2] += beta * b[5]
            s[3] += alpha * d0
            s[4] += alpha * d1
            s[5] += alpha * d2
            s[6] += alpha
            s[7] += gamma * d0
            s[8] += gamma * d1
            s[9] += gamma * d2
            if factor:
                s[10] += kernel
        for k in range(kept):
            sums[k, :, span] = s[k]

    def over_chunks(visit):
        def step(chunk, carried):
            visit(chunk)
            return carried

        lax.fori_loop(0, chunks, step, 0)

    units = len(plan) * count // unit
    for chunk in range(chunks):
        fill(0, chunk, wide0, proj0)

    def pair(step, carried):
        def even(chunk):
            fill(2 * step + 1, chunk, wide1, proj1)
            work(chunk, wide0, proj0, wide1, proj1)

        def odd(chunk):
            fill(jnp.minimum(2 * step + 2, units - 1), chunk, wide0, proj0)
            work(chunk, wide1, proj1, wide0, proj0)

        over_chunks(even)
        over_chunks(odd)
        return carried

    lax.fori_loop(0, units // 2, pair, 0)
    for k in range(SUMS):
        line = jnp.sum(sums[k], axis=0, keepdims=True)
        out[k : k + 1, :] = line + total[k : k + 1, :] if carry else line
    if factor:
        weighted = sums[SUMS] * (factor * own[6:7, :])
        part_share = weighted[:, 0:LANES]
        for chunk in range(1, chunks):
            part_share = part_share + weighted[:, chunk * LANES : (chunk + 1) * LANES]
        share[...] = part_share + share_in[...] if carry else part_share


def tiles(times, own, arrays, plan, factor, carried, groups, blocks):
    count = own.shape[1]
    number = len(plan)
    unit = min(count // 2, 256)
    groups_in_unit = unit // ROWS
    cut = groups_in_unit - max(1, groups_in_unit // 8)
    body = functools.partial(tiles_kernel, plan, groups, blocks, unit, cut, factor, carried is not None)
    operands = [times, own, *arrays]
    if carried is not None:
        operands += [carried[0]] + ([carried[1]] if factor else [])
    shapes = [jax.ShapeDtypeStruct((SUMS, count), F32)]
    if factor:
        shapes.append(jax.ShapeDtypeStruct((ROWS, LANES), F32))
    pairs = number * count * count
    result = pl.pallas_call(
        body,
        out_shape=shapes,
        in_specs=[VMEM] * len(operands),
        out_specs=[VMEM] * len(shapes),
        scratch_shapes=[
            pltpu.VMEM((number * count, ROWS), F32),
            pltpu.VMEM((number * count, DEPTH), BF16),
            pltpu.VMEM((DEPTH, 2 * count), BF16),
            pltpu.VMEM((7, unit, LANES), F32),
            pltpu.VMEM((7, unit, LANES), F32),
            pltpu.VMEM((unit, 2 * count), F32),
            pltpu.VMEM((unit, 2 * count), F32),
            pltpu.VMEM((SUMS + 1, ROWS, count), F32),
        ],
        compiler_params=PARAMS,
        cost_estimate=pl.CostEstimate(
            flops=FLOPS_PER_PAIR * pairs, bytes_accessed=32 * count * number, transcendentals=pairs
        ),
    )(*operands)
    share = result[1] if factor else (carried[1] if carried is not None else None)
    return result[0], share


def finish_kernel(own, edges, sums, faces, grad):
    verts = grad.shape[1]
    count = own.shape[1]
    twice = 2.0 * own[6:7, :]
    total = sums[6:7, :]
    g_center = [
        twice * (own[3 + c : 4 + c, :] * total + sums[c : c + 1, :] - 2.0 * sums[7 + c : 8 + c, :]) for c in range(3)
    ]
    g_area = [twice * sums[3 + c : 4 + c, :] for c in range(3)]
    e1 = [edges[c : c + 1, :] for c in range(3)]
    e2 = [edges[3 + c : 4 + c, :] for c in range(3)]
    zero = jnp.zeros((ROWS - 3, count), F32)
    corners = [[], [], []]
    for c in range(3):
        n, m = (c + 1) % 3, (c + 2) % 3
        g1 = 0.5 * (e2[n] * g_area[m] - e2[m] * g_area[n])
        g2 = 0.5 * (g_area[n] * e1[m] - g_area[m] * e1[n])
        part = g_center[c] / 3.0
        corners[0].append(part - g1 - g2)
        corners[1].append(part + g1)
        corners[2].append(part + g2)
    total = jnp.zeros((3 * ROWS, verts), F32)
    for k in range(3):
        left = jnp.concatenate(pieces(jnp.concatenate(corners[k] + [zero], 0)), 0).astype(BF16)
        total += lax.dot_general(
            left, one_hot(faces[k : k + 1, :], verts), (((1,), (1,)), ((), ())), preferred_element_type=F32
        )
    total = total[0:ROWS] + total[ROWS : 2 * ROWS] + total[2 * ROWS : 3 * ROWS]
    grad[...] = total[0:3] / count


def gather(own, axis, size, wanted):
    if size & (size - 1) == 0 and len(wanted) == size - 1:
        found = {}
        held = own[None]
        mask = size // 2
        while mask:
            other = flip(held, axis, mask)
            for offset in wanted:
                if offset & -offset == mask:
                    found[offset] = (other, "ring")
            held = jnp.concatenate([held, other], 0) if mask > 1 else held
            mask //= 2
        return found
    return {offset: (from_ahead(own, axis, offset), None) for offset in wanted}


def shards(vertices, faces, trial_step, accepted, face_weight, partner_shift):
    count = faces.shape[1]
    verts = vertices.shape[1]
    groups, blocks = lax.axis_size("grp"), lax.axis_size("blk")
    block_shape = jax.ShapeDtypeStruct((ROWS, count), F32)
    own, edges, times = pl.pallas_call(
        functools.partial(geometry_kernel, groups),
        out_shape=(block_shape, block_shape, jax.ShapeDtypeStruct((-(-groups // ROWS) * ROWS, LANES), F32)),
        in_specs=[SMEM] * 2 + [pl.BlockSpec(memory_space=pltpu.HBM)] * 4,
        out_specs=(VMEM, VMEM, VMEM),
        scratch_shapes=[
            pltpu.VMEM(vertices.shape, F32),
            pltpu.VMEM(trial_step.shape, F32),
            pltpu.VMEM(faces.shape, jnp.int32),
            pltpu.VMEM(face_weight.shape, F32),
            pltpu.VMEM((ROWS, verts), F32),
            pltpu.SemaphoreType.DMA((4,)),
        ],
        compiler_params=PARAMS,
    )(accepted, partner_shift, vertices, trial_step, faces, face_weight)

    window = [o for o in range(1, blocks) if window_times(o, blocks)]
    ring = gather(own, "blk", blocks, window)
    across = gather(own, "grp", groups, list(range(1, groups)))

    def visit(items, factor, carried):
        arrays, plan = [], []
        for axis, offset in items:
            if axis == "self":
                array, index = own, None
            else:
                array, index = (ring if axis == "blk" else across)[offset]
            where = [i for i, known in enumerate(arrays) if known is array]
            if not where:
                arrays.append(array)
                where = [len(arrays) - 1]
            plan.append((where[0], index, axis, offset))
        return tiles(times, own, arrays, tuple(plan), factor, carried, groups, blocks)

    def stage(offset, size):
        return -(offset & -offset) if size & (size - 1) == 0 else 0

    middle = [("blk", o) for o in window if 2 * o == blocks] + [("grp", o) for o in range(1, groups) if 2 * o == groups]
    early_blk = sorted((o for o in window if 2 * o < blocks), key=lambda o: (stage(o, blocks), o))
    early_grp = [("grp", o) for o in range(1, groups) if 2 * o < groups]
    late = [("grp", o) for o in range(1, groups) if 2 * o > groups]
    late += [("blk", o) for o in sorted((o for o in window if 2 * o > blocks), key=lambda o: (stage(o, blocks), o))]
    first = early_grp + [("blk", o) for o in early_blk[: len(early_blk) // 3]]
    second = [("blk", o) for o in early_blk[len(early_blk) // 3 :]]

    carried = visit([("self", 0)], 0.5, None)
    for items, factor in ((middle, 0.5), (first, 1.0), (second, 1.0)):
        if items:
            carried = visit(items, factor, carried)
    total, share = carried
    rounds = []
    for axis, size in (("blk", blocks), ("grp", groups)):
        if size & (size - 1) == 0:
            rounds += [(axis, size >> k) for k in range(1, size.bit_length())]
        else:
            rounds.append((axis, 0))

    def exchange(value, axis, mask):
        if mask:
            return flip(value, axis, mask)
        return sum(from_ahead(value, axis, o) for o in range(1, lax.axis_size(axis)))

    def last_of(total):
        return pl.pallas_call(
            finish_kernel,
            out_shape=jax.ShapeDtypeStruct((3, verts), F32),
            in_specs=[VMEM] * 4,
            out_specs=VMEM,
            compiler_params=PARAMS,
            cost_estimate=pl.CostEstimate(flops=1500000000, bytes_accessed=64 * count, transcendentals=0),
        )(own, edges, total, faces)

    covers = [functools.partial(visit, [item], 0.0) for item in late]
    for index, (axis, mask) in enumerate(rounds):
        received = exchange(share, axis, mask)
        if index < len(covers):
            total = covers[index]((total, None))[0]
            total, received = lax.optimization_barrier((total, received))
        elif index == len(covers):
            grad, received = lax.optimization_barrier((last_of(total), received))
        share = share + received
    if len(rounds) <= len(covers):
        for cover in covers[len(rounds) :]:
            total = cover((total, None))[0]
        grad = last_of(total)
    energy = jnp.sum(share) / (count * count * groups * blocks)
    return grad, energy.reshape(1)


def solution(mesh):
    placed = (
        P(None, ("grp", "blk")),
        P(None, ("grp", "blk")),
        P(None, ("grp", "blk")),
        P("grp"),
        P(("grp", "blk")),
        P(),
    )
    return jax.shard_map(
        shards,
        mesh=mesh,
        in_specs=placed,
        out_specs=(P(None, ("grp", "blk")), P()),
        check_vma=False,
    )
```

```python
import functools

import jax
import jax.numpy as jnp
from jax import lax
from jax.experimental import pallas as pl
from jax.experimental.pallas import tpu as pltpu
from jax.sharding import PartitionSpec as P

HOPS = 4
EPS2 = 0.05
ROWS = 8
LANES = 128
DEPTH = 64
SUMS = 10
F32 = jnp.float32
BF16 = jnp.bfloat16
VMEM = pl.BlockSpec(memory_space=pltpu.VMEM)
SMEM = pl.BlockSpec(memory_space=pltpu.SMEM)
FLOPS_PER_PAIR = 8000
PARAMS = pltpu.CompilerParams(vmem_limit_bytes=16 * 1024 * 1024)


def flip(value, axis, mask):
    count = lax.axis_size(axis)
    return lax.ppermute(value, axis, [(i, i ^ mask) for i in range(count)])


def from_ahead(value, axis, by):
    count = lax.axis_size(axis)
    return lax.ppermute(value, axis, [(i, (i - by) % count) for i in range(count)])


def pieces(value):
    high = value.astype(BF16).astype(F32)
    rest = value - high
    middle = rest.astype(BF16).astype(F32)
    return high, middle, rest - middle


def one_hot(row, count):
    rows = lax.broadcasted_iota(jnp.int32, (count, row.shape[1]), 0)
    return jnp.where(rows == row, 1.0, 0.0).astype(BF16)


def partner_times(shift, here, there, groups):
    times = jnp.int32(0)
    for r in range(shift.shape[0]):
        times += (lax.rem(here + shift[r, here], groups) == there).astype(jnp.int32)
        times += (lax.rem(there + shift[r, there], groups) == here).astype(jnp.int32)
    return times


def geometry_kernel(groups, accepted, shift, v_far, t_far, f_far, w_far, own, edges, times, *scratch):
    vertices, trial_step, faces, weight, padded, arrived = scratch
    copies = [
        pltpu.make_async_copy(far, near, arrived.at[i])
        for i, (far, near) in enumerate(
            ((v_far, vertices), (t_far, trial_step), (f_far, faces), (w_far, weight))
        )
    ]
    for copy in copies:
        copy.start()
    verts = vertices.shape[1]
    count = faces.shape[1]
    padded[...] = jnp.zeros_like(padded)
    here = lax.axis_index("grp")
    times[...] = jnp.zeros_like(times)
    for offset in range(1, groups):
        met = partner_times(shift, here, lax.rem(here + offset, groups), groups).astype(F32)
        times[offset : offset + 1, :] = jnp.zeros((1, LANES), F32) + met
    for copy in copies:
        copy.wait()
    padded[0:3, :] = vertices[...] + accepted[0].astype(F32) * trial_step[...]
    left = jnp.concatenate(pieces(padded[...]), 0).astype(BF16)

    def corner(k):
        picked = jnp.dot(left, one_hot(faces[k : k + 1, :], verts), preferred_element_type=F32)
        picked = picked[0:ROWS] + picked[ROWS : 2 * ROWS] + picked[2 * ROWS : 3 * ROWS]
        return [picked[c : c + 1] for c in range(3)]

    first, second, third = corner(0), corner(1), corner(2)
    center = [(first[c] + second[c] + third[c]) / 3.0 for c in range(3)]
    e1 = [second[c] - first[c] for c in range(3)]
    e2 = [third[c] - first[c] for c in range(3)]
    area = []
    for c in range(3):
        n, m = (c + 1) % 3, (c + 2) % 3
        area.append(0.5 * (e1[n] * e2[m] - e1[m] * e2[n]))
    for c in range(3):
        own[c : c + 1, :] = center[c]
        own[3 + c : 4 + c, :] = area[c]
        edges[c : c + 1, :] = e1[c]
        edges[3 + c : 4 + c, :] = e2[c]
    own[6:7, :] = weight[...].reshape(1, count)
    own[7:8, :] = center[0] * area[0] + center[1] * area[1] + center[2] * area[2]
    edges[6:8, :] = jnp.zeros((2, count), F32)


def window_times(offset, blocks):
    return sum(int((k - offset) % blocks == 0) + int((k + offset) % blocks == 0) for k in range(1, HOPS + 1))


def place_of(mask, size):
    place, step, bit = 0, 1, size // 2
    while bit:
        place = place + jnp.bitwise_and(mask // bit, 1) * step
        step, bit = step * 2, bit // 2
    return place


def tiles_kernel(plan, groups, blocks, unit, cut, factor, carry, *refs):
    met, own = refs[0], refs[1]
    arrays = 1 + max(item[0] for item in plan)
    others = refs[2 : 2 + arrays]
    at = 2 + arrays
    total, share_in = None, None
    if carry:
        total = refs[at]
        at += 1
        if factor:
            share_in = refs[at]
            at += 1
    out = refs[at]
    at += 1
    if factor:
        share = refs[at]
        at += 1
    columns, left, right, wide0, wide1, proj0, proj1, sums = refs[at:]
    count = own.shape[1]
    chunks = count // LANES
    part = unit // chunks
    kept = SUMS + (1 if factor else 0)
    row = lax.broadcasted_iota(jnp.int32, (ROWS, count), 0)
    zero = jnp.zeros((ROWS, count), F32)
    zero1, zero3 = jnp.zeros((1, count), F32), jnp.zeros((3, count), F32)
    from_own = jnp.concatenate([-own[3:6, :], zero3, own[7:8, :], zero1], 0)
    from_other = jnp.concatenate([zero3, own[0:3, :], zero1, zero1 - 1.0], 0)
    for side, rows in enumerate((from_own, from_other)):
        high, middle, low = pieces(rows)
        right[:, side * count : (side + 1) * count] = jnp.concatenate(
            [zero, high, middle, low, high, middle, high, zero], 0
        ).astype(BF16)
    for t, (source, index, axis, offset) in enumerate(plan):
        if index == "ring":
            size = groups if axis == "grp" else blocks
            here = lax.axis_index(axis)
            there = lax.rem(here + offset, size)
            first = size // 2 // (offset & -offset)
            block = others[source][place_of(jnp.bitwise_xor(here, there), size) - first]
        elif index is None:
            block = others[source][...]
        else:
            block = others[source][index]
        if axis == "self":
            times = 1.0 + window_times(0, blocks)
        elif axis == "blk":
            times = float(window_times(offset, blocks))
        else:
            times = jnp.concatenate([met[offset : offset + 1, :]] * chunks, 1)
        block = jnp.where(row == 6, block * times, block)
        high, middle, low = pieces(jnp.where(row == 6, 1.0, block))
        turned = jnp.concatenate([block, high, high, high, middle, middle, low, zero], 0).T
        columns[t * count : (t + 1) * count, :] = turned[:, 0:ROWS]
        left[t * count : (t + 1) * count, :] = turned.astype(BF16)
    for k in range(kept):
        sums[k] = zero

    def fill(u, chunk, wide, proj):
        source = pl.multiple_of(u * unit + chunk * part, part)
        target = pl.multiple_of(chunk * part, part)
        proj[pl.ds(target, part), :] = jnp.dot(left[pl.ds(source, part), :], right[...], preferred_element_type=F32)
        for k in range(7):
            for g in range(part // ROWS):
                group = columns[pl.ds(pl.multiple_of(source + g * ROWS, ROWS), ROWS), :]
                wide[k, pl.ds(pl.multiple_of(target + g * ROWS, ROWS), ROWS), :] = jnp.broadcast_to(
                    group[:, k : k + 1], (ROWS, LANES)
                )

    def work(chunk, wide, proj, next_wide, next_proj):
        at_lane = pl.multiple_of(chunk * LANES, LANES)
        span = pl.ds(at_lane, LANES)
        a = [jnp.broadcast_to(own[k : k + 1, span], (ROWS, LANES)) for k in range(3)]
        s = [sums[k, :, span] for k in range(kept)]
        for g in range(unit // ROWS):
            if g == cut:
                stored = pl.ds(pl.multiple_of(chunk * part, ROWS), ROWS)
                seen = next_wide[6, stored, :] + next_proj[stored, 0:LANES]
                s[6] = s[6] + jnp.where(chunk < 0, seen, 0.0)
            rows = slice(g * ROWS, (g + 1) * ROWS)
            b = [wide[k, rows, :] for k in range(7)]
            proj_a = proj[rows, span]
            proj_b = proj[rows, pl.ds(pl.multiple_of(count + at_lane, LANES), LANES)]
            d0, d1, d2 = a[0] - b[0], a[1] - b[1], a[2] - b[2]
            dist = d0 * d0 + d1 * d1 + (d2 * d2 + EPS2)
            inverse = 1.0 / dist
            square = inverse * inverse * b[6]
            alpha = proj_a * square
            beta = proj_b * square
            kernel = proj_a * alpha + proj_b * beta
            gamma = kernel * inverse
            s[0] += beta * b[3]
            s[1] += beta * b[4]
            s[2] += beta * b[5]
            s[3] += alpha * d0
            s[4] += alpha * d1
            s[5] += alpha * d2
            s[6] += alpha
            s[7] += gamma * d0
            s[8] += gamma * d1
            s[9] += gamma * d2
            if factor:
                s[10] += kernel
        for k in range(kept):
            sums[k, :, span] = s[k]

    def over_chunks(visit):
        def step(chunk, carried):
            visit(chunk)
            return carried

        lax.fori_loop(0, chunks, step, 0)

    units = len(plan) * count // unit
    for chunk in range(chunks):
        fill(0, chunk, wide0, proj0)

    def pair(step, carried):
        def even(chunk):
            fill(2 * step + 1, chunk, wide1, proj1)
            work(chunk, wide0, proj0, wide1, proj1)

        def odd(chunk):
            fill(jnp.minimum(2 * step + 2, units - 1), chunk, wide0, proj0)
            work(chunk, wide1, proj1, wide0, proj0)

        over_chunks(even)
        over_chunks(odd)
        return carried

    lax.fori_loop(0, units // 2, pair, 0)
    for k in range(SUMS):
        line = jnp.sum(sums[k], axis=0, keepdims=True)
        out[k : k + 1, :] = line + total[k : k + 1, :] if carry else line
    if factor:
        weighted = sums[SUMS] * (factor * own[6:7, :])
        part_share = weighted[:, 0:LANES]
        for chunk in range(1, chunks):
            part_share = part_share + weighted[:, chunk * LANES : (chunk + 1) * LANES]
        share[...] = part_share + share_in[...] if carry else part_share


def tiles(times, own, arrays, plan, factor, carried, groups, blocks):
    count = own.shape[1]
    number = len(plan)
    unit = min(count // 2, 256)
    groups_in_unit = unit // ROWS
    cut = groups_in_unit - max(1, groups_in_unit // 8)
    body = functools.partial(tiles_kernel, plan, groups, blocks, unit, cut, factor, carried is not None)
    operands = [times, own, *arrays]
    if carried is not None:
        operands += [carried[0]] + ([carried[1]] if factor else [])
    shapes = [jax.ShapeDtypeStruct((SUMS, count), F32)]
    if factor:
        shapes.append(jax.ShapeDtypeStruct((ROWS, LANES), F32))
    pairs = number * count * count
    result = pl.pallas_call(
        body,
        out_shape=shapes,
        in_specs=[VMEM] * len(operands),
        out_specs=[VMEM] * len(shapes),
        scratch_shapes=[
            pltpu.VMEM((number * count, ROWS), F32),
            pltpu.VMEM((number * count, DEPTH), BF16),
            pltpu.VMEM((DEPTH, 2 * count), BF16),
            pltpu.VMEM((7, unit, LANES), F32),
            pltpu.VMEM((7, unit, LANES), F32),
            pltpu.VMEM((unit, 2 * count), F32),
            pltpu.VMEM((unit, 2 * count), F32),
            pltpu.VMEM((SUMS + 1, ROWS, count), F32),
        ],
        compiler_params=PARAMS,
        cost_estimate=pl.CostEstimate(
            flops=FLOPS_PER_PAIR * pairs, bytes_accessed=32 * count * number, transcendentals=pairs
        ),
    )(*operands)
    share = result[1] if factor else (carried[1] if carried is not None else None)
    return result[0], share


def finish_kernel(own, edges, sums, faces, grad):
    verts = grad.shape[1]
    count = own.shape[1]
    twice = 2.0 * own[6:7, :]
    total = sums[6:7, :]
    g_center = [
        twice * (own[3 + c : 4 + c, :] * total + sums[c : c + 1, :] - 2.0 * sums[7 + c : 8 + c, :]) for c in range(3)
    ]
    g_area = [twice * sums[3 + c : 4 + c, :] for c in range(3)]
    e1 = [edges[c : c + 1, :] for c in range(3)]
    e2 = [edges[3 + c : 4 + c, :] for c in range(3)]
    zero = jnp.zeros((ROWS - 3, count), F32)
    corners = [[], [], []]
    for c in range(3):
        n, m = (c + 1) % 3, (c + 2) % 3
        g1 = 0.5 * (e2[n] * g_area[m] - e2[m] * g_area[n])
        g2 = 0.5 * (g_area[n] * e1[m] - g_area[m] * e1[n])
        part = g_center[c] / 3.0
        corners[0].append(part - g1 - g2)
        corners[1].append(part + g1)
        corners[2].append(part + g2)
    total = jnp.zeros((3 * ROWS, verts), F32)
    for k in range(3):
        left = jnp.concatenate(pieces(jnp.concatenate(corners[k] + [zero], 0)), 0).astype(BF16)
        total += lax.dot_general(
            left, one_hot(faces[k : k + 1, :], verts), (((1,), (1,)), ((), ())), preferred_element_type=F32
        )
    total = total[0:ROWS] + total[ROWS : 2 * ROWS] + total[2 * ROWS : 3 * ROWS]
    grad[...] = total[0:3] / count


def gather(own, axis, size, wanted):
    if size & (size - 1) == 0 and len(wanted) == size - 1:
        found = {}
        held = own[None]
        mask = size // 2
        while mask:
            other = flip(held, axis, mask)
            for offset in wanted:
                if offset & -offset == mask:
                    found[offset] = (other, "ring")
            held = jnp.concatenate([held, other], 0) if mask > 1 else held
            mask //= 2
        return found
    return {offset: (from_ahead(own, axis, offset), None) for offset in wanted}


def shards(vertices, faces, trial_step, accepted, face_weight, partner_shift):
    count = faces.shape[1]
    verts = vertices.shape[1]
    groups, blocks = lax.axis_size("grp"), lax.axis_size("blk")
    block_shape = jax.ShapeDtypeStruct((ROWS, count), F32)
    own, edges, times = pl.pallas_call(
        functools.partial(geometry_kernel, groups),
        out_shape=(block_shape, block_shape, jax.ShapeDtypeStruct((-(-groups // ROWS) * ROWS, LANES), F32)),
        in_specs=[SMEM] * 2 + [pl.BlockSpec(memory_space=pltpu.HBM)] * 4,
        out_specs=(VMEM, VMEM, VMEM),
        scratch_shapes=[
            pltpu.VMEM(vertices.shape, F32),
            pltpu.VMEM(trial_step.shape, F32),
            pltpu.VMEM(faces.shape, jnp.int32),
            pltpu.VMEM(face_weight.shape, F32),
            pltpu.VMEM((ROWS, verts), F32),
            pltpu.SemaphoreType.DMA((4,)),
        ],
    )(accepted, partner_shift, vertices, trial_step, faces, face_weight)

    window = [o for o in range(1, blocks) if window_times(o, blocks)]
    ring = gather(own, "blk", blocks, window)
    across = gather(own, "grp", groups, list(range(1, groups)))

    def visit(items, factor, carried):
        arrays, plan = [], []
        for axis, offset in items:
            if axis == "self":
                array, index = own, None
            else:
                array, index = (ring if axis == "blk" else across)[offset]
            where = [i for i, known in enumerate(arrays) if known is array]
            if not where:
                arrays.append(array)
                where = [len(arrays) - 1]
            plan.append((where[0], index, axis, offset))
        return tiles(times, own, arrays, tuple(plan), factor, carried, groups, blocks)

    def stage(offset, size):
        return -(offset & -offset) if size & (size - 1) == 0 else 0

    middle = [("blk", o) for o in window if 2 * o == blocks] + [("grp", o) for o in range(1, groups) if 2 * o == groups]
    early_blk = sorted((o for o in window if 2 * o < blocks), key=lambda o: (stage(o, blocks), o))
    early_grp = [("grp", o) for o in range(1, groups) if 2 * o < groups]
    late = [("grp", o) for o in range(1, groups) if 2 * o > groups]
    late += [("blk", o) for o in sorted((o for o in window if 2 * o > blocks), key=lambda o: (stage(o, blocks), o))]
    first = early_grp + [("blk", o) for o in early_blk[: len(early_blk) // 3]]
    second = [("blk", o) for o in early_blk[len(early_blk) // 3 :]]

    carried = visit([("self", 0)], 0.5, None)
    for items, factor in ((middle, 0.5), (first, 1.0), (second, 1.0)):
        if items:
            carried = visit(items, factor, carried)
    total, share = carried
    rounds = []
    for axis, size in (("blk", blocks), ("grp", groups)):
        if size & (size - 1) == 0:
            rounds += [(axis, size >> k) for k in range(1, size.bit_length())]
        else:
            rounds.append((axis, 0))

    def exchange(value, axis, mask):
        if mask:
            return flip(value, axis, mask)
        return sum(from_ahead(value, axis, o) for o in range(1, lax.axis_size(axis)))

    def last_of(total):
        return pl.pallas_call(
            finish_kernel,
            out_shape=jax.ShapeDtypeStruct((3, verts), F32),
            in_specs=[VMEM] * 4,
            out_specs=VMEM,
            compiler_params=PARAMS,
            cost_estimate=pl.CostEstimate(flops=1500000000, bytes_accessed=64 * count, transcendentals=0),
        )(own, edges, total, faces)

    covers = [functools.partial(visit, [item], 0.0) for item in late]
    for index, (axis, mask) in enumerate(rounds):
        received = exchange(share, axis, mask)
        if index < len(covers):
            total = covers[index]((total, None))[0]
            total, received = lax.optimization_barrier((total, received))
        elif index == len(covers):
            grad, received = lax.optimization_barrier((last_of(total), received))
        share = share + received
    if len(rounds) <= len(covers):
        for cover in covers[len(rounds) :]:
            total = cover((total, None))[0]
        grad = last_of(total)
    energy = jnp.sum(share) / (count * count * groups * blocks)
    return grad, energy.reshape(1)


def solution(mesh):
    placed = (
        P(None, ("grp", "blk")),
        P(None, ("grp", "blk")),
        P(None, ("grp", "blk")),
        P("grp"),
        P(("grp", "blk")),
        P(),
    )
    return jax.shard_map(
        shards,
        mesh=mesh,
        in_specs=placed,
        out_specs=(P(None, ("grp", "blk")), P()),
        check_vma=False,
    )
```

```python
import functools

import jax
import jax.numpy as jnp
from jax import lax
from jax.experimental import pallas as pl
from jax.experimental.pallas import tpu as pltpu
from jax.sharding import PartitionSpec as P

HOPS = 4
EPS2 = 0.05
ROWS = 8
LANES = 128
DEPTH = 64
SUMS = 10
F32 = jnp.float32
BF16 = jnp.bfloat16
VMEM = pl.BlockSpec(memory_space=pltpu.VMEM)
SMEM = pl.BlockSpec(memory_space=pltpu.SMEM)
FLOPS_PER_PAIR = 8000
PARAMS = pltpu.CompilerParams(vmem_limit_bytes=16 * 1024 * 1024)


def flip(value, axis, mask):
    count = lax.axis_size(axis)
    return lax.ppermute(value, axis, [(i, i ^ mask) for i in range(count)])


def from_ahead(value, axis, by):
    count = lax.axis_size(axis)
    return lax.ppermute(value, axis, [(i, (i - by) % count) for i in range(count)])


def pieces(value):
    high = value.astype(BF16).astype(F32)
    rest = value - high
    middle = rest.astype(BF16).astype(F32)
    return high, middle, rest - middle


def one_hot(row, count):
    rows = lax.broadcasted_iota(jnp.int32, (count, row.shape[1]), 0)
    return jnp.where(rows == row, 1.0, 0.0).astype(BF16)


def partner_times(shift, here, there, groups):
    times = jnp.int32(0)
    for r in range(shift.shape[0]):
        times += (lax.rem(here + shift[r, here], groups) == there).astype(jnp.int32)
        times += (lax.rem(there + shift[r, there], groups) == here).astype(jnp.int32)
    return times


def geometry_kernel(groups, *refs):
    far, (sent, own, edges, times), near, (padded, arrived) = refs[:6], refs[6:10], refs[10:16], refs[16:]
    accepted, shift, vertices, trial_step, faces, weight = near
    copies = [pltpu.make_async_copy(far[i], near[i], arrived.at[i]) for i in range(6)]
    for copy in copies:
        copy.start()
    verts = vertices.shape[1]
    count = faces.shape[1]
    padded[...] = jnp.zeros_like(padded)
    for copy in copies:
        copy.wait()
    here = lax.axis_index("grp")
    times[...] = jnp.zeros_like(times)
    for offset in range(1, groups):
        met = partner_times(shift, here, lax.rem(here + offset, groups), groups).astype(F32)
        times[offset : offset + 1, :] = jnp.zeros((1, LANES), F32) + met
    padded[0:3, :] = vertices[...] + accepted[0].astype(F32) * trial_step[...]
    left = jnp.concatenate(pieces(padded[...]), 0).astype(BF16)

    def corner(k):
        picked = jnp.dot(left, one_hot(faces[k : k + 1, :], verts), preferred_element_type=F32)
        picked = picked[0:ROWS] + picked[ROWS : 2 * ROWS] + picked[2 * ROWS : 3 * ROWS]
        return [picked[c : c + 1] for c in range(3)]

    first, second, third = corner(0), corner(1), corner(2)
    center = [(first[c] + second[c] + third[c]) / 3.0 for c in range(3)]
    e1 = [second[c] - first[c] for c in range(3)]
    e2 = [third[c] - first[c] for c in range(3)]
    area = []
    for c in range(3):
        n, m = (c + 1) % 3, (c + 2) % 3
        area.append(0.5 * (e1[n] * e2[m] - e1[m] * e2[n]))
    for c in range(3):
        own[c : c + 1, :] = center[c]
        own[3 + c : 4 + c, :] = area[c]
        edges[c : c + 1, :] = e1[c]
        edges[3 + c : 4 + c, :] = e2[c]
    own[6:7, :] = weight[...].reshape(1, count)
    own[7:8, :] = center[0] * area[0] + center[1] * area[1] + center[2] * area[2]
    edges[6:8, :] = jnp.zeros((2, count), F32)
    sent[...] = own[...]


def window_times(offset, blocks):
    return sum(int((k - offset) % blocks == 0) + int((k + offset) % blocks == 0) for k in range(1, HOPS + 1))


def place_of(mask, size):
    place, step, bit = 0, 1, size // 2
    while bit:
        place = place + jnp.bitwise_and(mask // bit, 1) * step
        step, bit = step * 2, bit // 2
    return place


def tiles_kernel(plan, groups, blocks, unit, cut, factor, carry, *refs):
    own = refs[0]
    arrays = 1 + max(item[0] for item in plan)
    others = refs[1 : 1 + arrays]
    at = 1 + arrays
    if any(item[2] == "grp" for item in plan):
        met = refs[at]
        at += 1
    total, share_in = None, None
    if carry:
        total = refs[at]
        at += 1
        if factor:
            share_in = refs[at]
            at += 1
    out = refs[at]
    at += 1
    if factor:
        share = refs[at]
        at += 1
    columns, left, right, wide0, wide1, proj0, proj1, sums = refs[at:]
    count = own.shape[1]
    chunks = count // LANES
    part = unit // chunks
    kept = SUMS + (1 if factor else 0)
    row = lax.broadcasted_iota(jnp.int32, (ROWS, count), 0)
    zero = jnp.zeros((ROWS, count), F32)
    zero1, zero3 = jnp.zeros((1, count), F32), jnp.zeros((3, count), F32)
    from_own = jnp.concatenate([-own[3:6, :], zero3, own[7:8, :], zero1], 0)
    from_other = jnp.concatenate([zero3, own[0:3, :], zero1, zero1 - 1.0], 0)
    for side, rows in enumerate((from_own, from_other)):
        high, middle, low = pieces(rows)
        right[:, side * count : (side + 1) * count] = jnp.concatenate(
            [zero, high, middle, low, high, middle, high, zero], 0
        ).astype(BF16)
    for t, (source, index, axis, offset) in enumerate(plan):
        if index == "ring":
            size = groups if axis == "grp" else blocks
            here = lax.axis_index(axis)
            there = lax.rem(here + offset, size)
            first = size // 2 // (offset & -offset)
            block = others[source][place_of(jnp.bitwise_xor(here, there), size) - first]
        elif index is None:
            block = others[source][...]
        else:
            block = others[source][index]
        if axis == "self":
            times = 1.0 + window_times(0, blocks)
        elif axis == "blk":
            times = float(window_times(offset, blocks))
        else:
            times = jnp.concatenate([met[offset : offset + 1, :]] * chunks, 1)
        block = jnp.where(row == 6, block * times, block)
        high, middle, low = pieces(jnp.where(row == 6, 1.0, block))
        turned = jnp.concatenate([block, high, high, high, middle, middle, low, zero], 0).T
        columns[t * count : (t + 1) * count, :] = turned[:, 0:ROWS]
        left[t * count : (t + 1) * count, :] = turned.astype(BF16)
    for k in range(kept):
        sums[k] = zero

    def fill(u, chunk, wide, proj):
        source = pl.multiple_of(u * unit + chunk * part, part)
        target = pl.multiple_of(chunk * part, part)
        proj[pl.ds(target, part), :] = jnp.dot(left[pl.ds(source, part), :], right[...], preferred_element_type=F32)
        for k in range(7):
            for g in range(part // ROWS):
                group = columns[pl.ds(pl.multiple_of(source + g * ROWS, ROWS), ROWS), :]
                wide[k, pl.ds(pl.multiple_of(target + g * ROWS, ROWS), ROWS), :] = jnp.broadcast_to(
                    group[:, k : k + 1], (ROWS, LANES)
                )

    def work(chunk, wide, proj, next_wide, next_proj):
        at_lane = pl.multiple_of(chunk * LANES, LANES)
        span = pl.ds(at_lane, LANES)
        a = [jnp.broadcast_to(own[k : k + 1, span], (ROWS, LANES)) for k in range(3)]
        s = [sums[k, :, span] for k in range(kept)]
        for g in range(unit // ROWS):
            if g == cut:
                stored = pl.ds(pl.multiple_of(chunk * part, ROWS), ROWS)
                seen = next_wide[6, stored, :] + next_proj[stored, 0:LANES]
                s[6] = s[6] + jnp.where(chunk < 0, seen, 0.0)
            rows = slice(g * ROWS, (g + 1) * ROWS)
            b = [wide[k, rows, :] for k in range(7)]
            proj_a = proj[rows, span]
            proj_b = proj[rows, pl.ds(pl.multiple_of(count + at_lane, LANES), LANES)]
            d0, d1, d2 = a[0] - b[0], a[1] - b[1], a[2] - b[2]
            dist = d0 * d0 + d1 * d1 + (d2 * d2 + EPS2)
            inverse = 1.0 / dist
            square = inverse * inverse * b[6]
            alpha = proj_a * square
            beta = proj_b * square
            kernel = proj_a * alpha + proj_b * beta
            gamma = kernel * inverse
            s[0] += beta * b[3]
            s[1] += beta * b[4]
            s[2] += beta * b[5]
            s[3] += alpha * d0
            s[4] += alpha * d1
            s[5] += alpha * d2
            s[6] += alpha
            s[7] += gamma * d0
            s[8] += gamma * d1
            s[9] += gamma * d2
            if factor:
                s[10] += kernel
        for k in range(kept):
            sums[k, :, span] = s[k]

    def over_chunks(visit):
        def step(chunk, carried):
            visit(chunk)
            return carried

        lax.fori_loop(0, chunks, step, 0)

    units = len(plan) * count // unit
    for chunk in range(chunks):
        fill(0, chunk, wide0, proj0)

    def pair(step, carried):
        def even(chunk):
            fill(2 * step + 1, chunk, wide1, proj1)
            work(chunk, wide0, proj0, wide1, proj1)

        def odd(chunk):
            fill(jnp.minimum(2 * step + 2, units - 1), chunk, wide0, proj0)
            work(chunk, wide1, proj1, wide0, proj0)

        over_chunks(even)
        over_chunks(odd)
        return carried

    lax.fori_loop(0, units // 2, pair, 0)
    for k in range(SUMS):
        line = jnp.sum(sums[k], axis=0, keepdims=True)
        out[k : k + 1, :] = line + total[k : k + 1, :] if carry else line
    if factor:
        weighted = sums[SUMS] * (factor * own[6:7, :])
        part_share = weighted[:, 0:LANES]
        for chunk in range(1, chunks):
            part_share = part_share + weighted[:, chunk * LANES : (chunk + 1) * LANES]
        share[...] = part_share + share_in[...] if carry else part_share


def tiles(times, own, arrays, plan, factor, carried, groups, blocks):
    count = own.shape[1]
    number = len(plan)
    unit = min(count // 2, 256)
    groups_in_unit = unit // ROWS
    cut = groups_in_unit - 1
    body = functools.partial(tiles_kernel, plan, groups, blocks, unit, cut, factor, carried is not None)
    operands = [own, *arrays] + ([times] if any(item[2] == "grp" for item in plan) else [])
    if carried is not None:
        operands += [carried[0]] + ([carried[1]] if factor else [])
    shapes = [jax.ShapeDtypeStruct((SUMS, count), F32)]
    if factor:
        shapes.append(jax.ShapeDtypeStruct((ROWS, LANES), F32))
    pairs = number * count * count
    result = pl.pallas_call(
        body,
        out_shape=shapes,
        in_specs=[VMEM] * len(operands),
        out_specs=[VMEM] * len(shapes),
        scratch_shapes=[
            pltpu.VMEM((number * count, ROWS), F32),
            pltpu.VMEM((number * count, DEPTH), BF16),
            pltpu.VMEM((DEPTH, 2 * count), BF16),
            pltpu.VMEM((7, unit, LANES), F32),
            pltpu.VMEM((7, unit, LANES), F32),
            pltpu.VMEM((unit, 2 * count), F32),
            pltpu.VMEM((unit, 2 * count), F32),
            pltpu.VMEM((SUMS + 1, ROWS, count), F32),
        ],
        compiler_params=PARAMS,
        cost_estimate=pl.CostEstimate(
            flops=FLOPS_PER_PAIR * pairs, bytes_accessed=32 * count * number, transcendentals=pairs
        ),
    )(*operands)
    share = result[1] if factor else (carried[1] if carried is not None else None)
    return result[0], share


def finish_kernel(own, edges, sums, faces, grad):
    verts = grad.shape[1]
    count = own.shape[1]
    twice = 2.0 * own[6:7, :]
    total = sums[6:7, :]
    g_center = [
        twice * (own[3 + c : 4 + c, :] * total + sums[c : c + 1, :] - 2.0 * sums[7 + c : 8 + c, :]) for c in range(3)
    ]
    g_area = [twice * sums[3 + c : 4 + c, :] for c in range(3)]
    e1 = [edges[c : c + 1, :] for c in range(3)]
    e2 = [edges[3 + c : 4 + c, :] for c in range(3)]
    zero = jnp.zeros((ROWS - 3, count), F32)
    corners = [[], [], []]
    for c in range(3):
        n, m = (c + 1) % 3, (c + 2) % 3
        g1 = 0.5 * (e2[n] * g_area[m] - e2[m] * g_area[n])
        g2 = 0.5 * (g_area[n] * e1[m] - g_area[m] * e1[n])
        part = g_center[c] / 3.0
        corners[0].append(part - g1 - g2)
        corners[1].append(part + g1)
        corners[2].append(part + g2)
    total = jnp.zeros((3 * ROWS, verts), F32)
    for k in range(3):
        left = jnp.concatenate(pieces(jnp.concatenate(corners[k] + [zero], 0)), 0).astype(BF16)
        total += lax.dot_general(
            left, one_hot(faces[k : k + 1, :], verts), (((1,), (1,)), ((), ())), preferred_element_type=F32
        )
    total = total[0:ROWS] + total[ROWS : 2 * ROWS] + total[2 * ROWS : 3 * ROWS]
    grad[...] = total[0:3] / count


def gather(own, axis, size, wanted):
    if size & (size - 1) == 0 and len(wanted) == size - 1:
        found = {}
        held = own[None]
        mask = size // 2
        while mask:
            other = flip(held, axis, mask)
            for offset in wanted:
                if offset & -offset == mask:
                    found[offset] = (other, "ring")
            held = jnp.concatenate([held, other], 0) if mask > 1 else held
            mask //= 2
        return found
    return {offset: (from_ahead(own, axis, offset), None) for offset in wanted}


def shards(vertices, faces, trial_step, accepted, face_weight, partner_shift):
    count = faces.shape[1]
    verts = vertices.shape[1]
    groups, blocks = lax.axis_size("grp"), lax.axis_size("blk")
    block_shape = jax.ShapeDtypeStruct((ROWS, count), F32)
    arguments = (accepted, partner_shift, vertices, trial_step, faces, face_weight)
    homes = [pltpu.SMEM] * 2 + [pltpu.VMEM] * 4
    met_shape = jax.ShapeDtypeStruct((-(-groups // ROWS) * ROWS, LANES), F32)
    sent, own, edges, times = pl.pallas_call(
        functools.partial(geometry_kernel, groups),
        out_shape=(block_shape, block_shape, block_shape, met_shape),
        in_specs=[pl.BlockSpec(memory_space=pltpu.HBM)] * 6,
        out_specs=(VMEM,) * 4,
        scratch_shapes=[home(a.shape, a.dtype) for home, a in zip(homes, arguments)]
        + [pltpu.VMEM((ROWS, verts), F32), pltpu.SemaphoreType.DMA((6,))],
    )(*arguments)

    window = [o for o in range(1, blocks) if window_times(o, blocks)]
    ring = gather(sent, "blk", blocks, window)
    across = gather(sent, "grp", groups, list(range(1, groups)))

    def visit(items, factor, carried):
        arrays, plan = [], []
        for axis, offset in items:
            if axis == "self":
                array, index = own, None
            else:
                array, index = (ring if axis == "blk" else across)[offset]
            where = [i for i, known in enumerate(arrays) if known is array]
            if not where:
                arrays.append(array)
                where = [len(arrays) - 1]
            plan.append((where[0], index, axis, offset))
        return tiles(times, own, arrays, tuple(plan), factor, carried, groups, blocks)

    def stage(offset, size):
        return -(offset & -offset) if size & (size - 1) == 0 else 0

    middle = [("blk", o) for o in window if 2 * o == blocks] + [("grp", o) for o in range(1, groups) if 2 * o == groups]
    early_blk = sorted((o for o in window if 2 * o < blocks), key=lambda o: (stage(o, blocks), o))
    early_grp = [("grp", o) for o in range(1, groups) if 2 * o < groups]
    late = [("grp", o) for o in range(1, groups) if 2 * o > groups]
    late += [("blk", o) for o in sorted((o for o in window if 2 * o > blocks), key=lambda o: (stage(o, blocks), o))]
    first = early_grp + [("blk", o) for o in early_blk[: len(early_blk) // 3]]
    second = [("blk", o) for o in early_blk[len(early_blk) // 3 :]]

    carried = visit([("self", 0)], 0.5, None)
    for items, factor in ((middle, 0.5), (first, 1.0), (second, 1.0)):
        if items:
            carried = visit(items, factor, carried)
    total, share = carried
    rounds = []
    for axis, size in (("blk", blocks), ("grp", groups)):
        if size & (size - 1) == 0:
            rounds += [(axis, size >> k) for k in range(1, size.bit_length())]
        else:
            rounds.append((axis, 0))

    def exchange(value, axis, mask):
        if mask:
            return flip(value, axis, mask)
        return sum(from_ahead(value, axis, o) for o in range(1, lax.axis_size(axis)))

    def last_of(total):
        return pl.pallas_call(
            finish_kernel,
            out_shape=jax.ShapeDtypeStruct((3, verts), F32),
            in_specs=[VMEM] * 4,
            out_specs=VMEM,
            compiler_params=PARAMS,
            cost_estimate=pl.CostEstimate(flops=1500000000, bytes_accessed=64 * count, transcendentals=0),
        )(own, edges, total, faces)

    covers = [functools.partial(visit, [item], 0.0) for item in late]
    for index, (axis, mask) in enumerate(rounds):
        received = exchange(share, axis, mask)
        if index < len(covers):
            total = covers[index]((total, None))[0]
            total, received = lax.optimization_barrier((total, received))
        elif index == len(covers):
            grad, received = lax.optimization_barrier((last_of(total), received))
        share = share + received
    if len(rounds) <= len(covers):
        for cover in covers[len(rounds) :]:
            total = cover((total, None))[0]
        grad = last_of(total)
    energy = jnp.sum(share) / (count * count * groups * blocks)
    return grad, energy.reshape(1)


def solution(mesh):
    placed = (
        P(None, ("grp", "blk")),
        P(None, ("grp", "blk")),
        P(None, ("grp", "blk")),
        P("grp"),
        P(("grp", "blk")),
        P(),
    )
    return jax.shard_map(
        shards,
        mesh=mesh,
        in_specs=placed,
        out_specs=(P(None, ("grp", "blk")), P()),
        check_vma=False,
    )
```

```python
import functools

import jax
import jax.numpy as jnp
from jax import lax
from jax.experimental import pallas as pl
from jax.experimental.pallas import tpu as pltpu
from jax.sharding import PartitionSpec as P

HOPS = 4
EPS2 = 0.05
ROWS = 8
LANES = 128
DEPTH = 64
SUMS = 10
F32 = jnp.float32
BF16 = jnp.bfloat16
VMEM = pl.BlockSpec(memory_space=pltpu.VMEM)
SMEM = pl.BlockSpec(memory_space=pltpu.SMEM)
FLOPS_PER_PAIR = 8000
PARAMS = pltpu.CompilerParams(vmem_limit_bytes=16 * 1024 * 1024)


def flip(value, axis, mask):
    count = lax.axis_size(axis)
    return lax.ppermute(value, axis, [(i, i ^ mask) for i in range(count)])


def from_ahead(value, axis, by):
    count = lax.axis_size(axis)
    return lax.ppermute(value, axis, [(i, (i - by) % count) for i in range(count)])


def pieces(value):
    high = value.astype(BF16).astype(F32)
    rest = value - high
    middle = rest.astype(BF16).astype(F32)
    return high, middle, rest - middle


def one_hot(row, count):
    rows = lax.broadcasted_iota(jnp.int32, (count, row.shape[1]), 0)
    return jnp.where(rows == row, 1.0, 0.0).astype(BF16)


def partner_times(shift, here, there, groups):
    times = jnp.int32(0)
    for r in range(shift.shape[0]):
        times += (lax.rem(here + shift[r, here], groups) == there).astype(jnp.int32)
        times += (lax.rem(there + shift[r, there], groups) == here).astype(jnp.int32)
    return times


def geometry_kernel(groups, *refs):
    far, (sent, own, edges, times), near, (padded, arrived) = refs[:6], refs[6:10], refs[10:16], refs[16:]
    accepted, shift, vertices, trial_step, faces, weight = near
    copies = [pltpu.make_async_copy(far[i], near[i], arrived.at[i]) for i in range(6)]
    for copy in copies:
        copy.start()
    verts = vertices.shape[1]
    count = faces.shape[1]
    padded[...] = jnp.zeros_like(padded)
    for copy in copies:
        copy.wait()
    here = lax.axis_index("grp")
    times[...] = jnp.zeros_like(times)
    for offset in range(1, groups):
        met = partner_times(shift, here, lax.rem(here + offset, groups), groups).astype(F32)
        times[offset : offset + 1, :] = jnp.zeros((1, LANES), F32) + met
    padded[0:3, :] = vertices[...] + accepted[0].astype(F32) * trial_step[...]
    left = jnp.concatenate(pieces(padded[...]), 0).astype(BF16)

    def corner(k):
        picked = jnp.dot(left, one_hot(faces[k : k + 1, :], verts), preferred_element_type=F32)
        picked = picked[0:ROWS] + picked[ROWS : 2 * ROWS] + picked[2 * ROWS : 3 * ROWS]
        return [picked[c : c + 1] for c in range(3)]

    first, second, third = corner(0), corner(1), corner(2)
    center = [(first[c] + second[c] + third[c]) / 3.0 for c in range(3)]
    e1 = [second[c] - first[c] for c in range(3)]
    e2 = [third[c] - first[c] for c in range(3)]
    area = []
    for c in range(3):
        n, m = (c + 1) % 3, (c + 2) % 3
        area.append(0.5 * (e1[n] * e2[m] - e1[m] * e2[n]))
    for c in range(3):
        own[c : c + 1, :] = center[c]
        own[3 + c : 4 + c, :] = area[c]
        edges[c : c + 1, :] = e1[c]
        edges[3 + c : 4 + c, :] = e2[c]
    own[6:7, :] = weight[...].reshape(1, count)
    own[7:8, :] = center[0] * area[0] + center[1] * area[1] + center[2] * area[2]
    edges[6:8, :] = jnp.zeros((2, count), F32)
    sent[...] = own[...]


def window_times(offset, blocks):
    return sum(int((k - offset) % blocks == 0) + int((k + offset) % blocks == 0) for k in range(1, HOPS + 1))


def place_of(mask, size):
    place, step, bit = 0, 1, size // 2
    while bit:
        place = place + jnp.bitwise_and(mask // bit, 1) * step
        step, bit = step * 2, bit // 2
    return place


def tiles_kernel(plan, blocks, unit, factor, first, carry, lead, trail, *refs):
    refs = list(refs)
    own = refs.pop(0)
    count = own.shape[1]
    chunks = count // LANES
    part = unit // chunks
    in_block = count // unit
    kept = SUMS + (1 if factor else 0)
    others = [refs.pop(0) for _ in range(1 + max(item[0] for item in plan))]
    met = refs.pop(0) if any(item[2] == "grp" for item in plan) else None
    right = None if first else refs.pop(0)
    total = refs.pop(0) if carry else None
    share_in = refs.pop(0) if carry and factor else None
    led = (refs.pop(0), refs.pop(0)) if lead else None
    out = refs.pop(0)
    share = refs.pop(0) if factor else None
    right = refs.pop(0) if first else right
    slot0 = (refs.pop(0), refs.pop(0)) if trail else None
    columns, left, sums, wide1, proj1 = refs[:5]
    slot0 = tuple(refs[5:7]) if slot0 is None else slot0
    slot1 = (wide1, proj1)
    units = (len(plan) - (1 if trail else 0)) * in_block

    if first:
        zero = jnp.zeros((ROWS, count), F32)
        zero1, zero3 = jnp.zeros((1, count), F32), jnp.zeros((3, count), F32)
        from_own = jnp.concatenate([-own[3:6, :], zero3, own[7:8, :], zero1], 0)
        from_other = jnp.concatenate([zero3, own[0:3, :], zero1, zero1 - 1.0], 0)
        for side, rows in enumerate((from_own, from_other)):
            high, middle, low = pieces(rows)
            right[:, side * count : (side + 1) * count] = jnp.concatenate(
                [zero, high, middle, low, high, middle, high, zero], 0
            ).astype(BF16)
    for t, (source, index, axis, offset) in enumerate(plan):
        if index == "ring":
            size = blocks if axis == "blk" else 0
            size = size or lax.axis_size("grp")
            here = lax.axis_index(axis)
            there = lax.rem(here + offset, size)
            block = others[source][place_of(jnp.bitwise_xor(here, there), size) - size // 2 // (offset & -offset)]
        elif index is None:
            block = others[source][...]
        else:
            block = others[source][index]
        low_edge = unit if lead and t == 0 else 0
        high_edge = unit if trail and t == len(plan) - 1 else count
        block = block[:, low_edge:high_edge]
        span = high_edge - low_edge
        if axis == "self":
            times = 1.0 + window_times(0, blocks)
        elif axis == "blk":
            times = float(window_times(offset, blocks))
        else:
            times = jnp.concatenate([met[offset : offset + 1, :]] * (span // LANES), 1)
        row = lax.broadcasted_iota(jnp.int32, (ROWS, span), 0)
        block = jnp.where(row == 6, block * times, block)
        high, middle, low = pieces(jnp.where(row == 6, 1.0, block))
        turned = jnp.concatenate([block, high, high, high, middle, middle, low, jnp.zeros_like(block)], 0).T
        target = slice(t * count + low_edge, t * count + high_edge)
        columns[target, :] = turned[:, 0:ROWS]
        left[target, :] = turned.astype(BF16)
    for k in range(kept):
        sums[k] = jnp.zeros((ROWS, count), F32)

    def fill(u, chunk, slot):
        wide, proj = slot
        source = pl.multiple_of(u * unit + chunk * part, part)
        target = pl.multiple_of(chunk * part, part)
        proj[pl.ds(target, part), :] = jnp.dot(left[pl.ds(source, part), :], right[...], preferred_element_type=F32)
        for k in range(7):
            for g in range(part // ROWS):
                group = columns[pl.ds(pl.multiple_of(source + g * ROWS, ROWS), ROWS), :]
                wide[k, pl.ds(pl.multiple_of(target + g * ROWS, ROWS), ROWS), :] = jnp.broadcast_to(
                    group[:, k : k + 1], (ROWS, LANES)
                )

    def work(chunk, slot, following):
        wide, proj = slot
        at_lane = pl.multiple_of(chunk * LANES, LANES)
        span = pl.ds(at_lane, LANES)
        a = [jnp.broadcast_to(own[k : k + 1, span], (ROWS, LANES)) for k in range(3)]
        s = [sums[k, :, span] for k in range(kept)]
        for g in range(unit // ROWS):
            if g == unit // ROWS - 1 and following is not None:
                stored = pl.ds(pl.multiple_of(chunk * part, ROWS), ROWS)
                seen = following[0][6, stored, :] + following[1][stored, 0:LANES]
                s[6] = s[6] + jnp.where(chunk < 0, seen, 0.0)
            rows = slice(g * ROWS, (g + 1) * ROWS)
            b = [wide[k, rows, :] for k in range(7)]
            proj_a = proj[rows, span]
            proj_b = proj[rows, pl.ds(pl.multiple_of(count + at_lane, LANES), LANES)]
            d0, d1, d2 = a[0] - b[0], a[1] - b[1], a[2] - b[2]
            dist = d0 * d0 + d1 * d1 + (d2 * d2 + EPS2)
            inverse = 1.0 / dist
            square = inverse * inverse * b[6]
            alpha = proj_a * square
            beta = proj_b * square
            kernel = proj_a * alpha + proj_b * beta
            gamma = kernel * inverse
            s[0] += beta * b[3]
            s[1] += beta * b[4]
            s[2] += beta * b[5]
            s[3] += alpha * d0
            s[4] += alpha * d1
            s[5] += alpha * d2
            s[6] += alpha
            s[7] += gamma * d0
            s[8] += gamma * d1
            s[9] += gamma * d2
            if factor:
                s[10] += kernel
        for k in range(kept):
            sums[k, :, span] = s[k]

    def over_chunks(now, u, slot):
        def step(chunk, carried):
            if u is not None:
                fill(u, chunk, slot)
            work(chunk, now, slot if u is not None else None)
            return carried

        lax.fori_loop(0, chunks, step, 0)

    if not lead:
        for chunk in range(chunks):
            fill(0, chunk, slot0)
    if units == 2:
        over_chunks(led if lead else slot0, 1, slot1)
        over_chunks(slot1, 2 if trail else None, slot0)
    else:

        def pair(step, carried):
            over_chunks(slot0, 2 * step + 1, slot1)
            over_chunks(slot1, jnp.minimum(2 * step + 2, units if trail else units - 1), slot0)
            return carried

        lax.fori_loop(0, units // 2, pair, 0)
    for k in range(SUMS):
        line = jnp.sum(sums[k], axis=0, keepdims=True)
        out[k : k + 1, :] = line + total[k : k + 1, :] if carry else line
    if factor:
        weighted = sums[SUMS] * (factor * own[6:7, :])
        part_share = weighted[:, 0:LANES]
        for chunk in range(1, chunks):
            part_share = part_share + weighted[:, chunk * LANES : (chunk + 1) * LANES]
        share[...] = part_share + share_in[...] if carry else part_share


def tiles(times, own, arrays, plan, factor, state, trail, blocks):
    count = own.shape[1]
    unit = count // 2
    total, share, right, led = state
    first, carry, lead = right is None, total is not None, led is not None
    number = len(plan) - (1 if trail else 0)
    body = functools.partial(tiles_kernel, plan, blocks, unit, factor, first, carry, lead, trail)
    operands = [own, *arrays] + ([times] if any(item[2] == "grp" for item in plan) else [])
    operands += ([] if first else [right]) + ([total] if carry else []) + ([share] if carry and factor else [])
    operands += list(led) if lead else []
    slot = [((7, unit, LANES), F32), ((unit, 2 * count), F32)]
    shapes = [jax.ShapeDtypeStruct((SUMS, count), F32)]
    if factor:
        shapes.append(jax.ShapeDtypeStruct((ROWS, LANES), F32))
    if first:
        shapes.append(jax.ShapeDtypeStruct((DEPTH, 2 * count), BF16))
    if trail:
        shapes += [jax.ShapeDtypeStruct(*each) for each in slot]
    rows = number * count + (unit if trail else 0)
    pairs = number * count * count
    result = list(
        pl.pallas_call(
            body,
            out_shape=shapes,
            in_specs=[VMEM] * len(operands),
            out_specs=[VMEM] * len(shapes),
            scratch_shapes=[
                pltpu.VMEM((rows, ROWS), F32),
                pltpu.VMEM((rows, DEPTH), BF16),
                pltpu.VMEM((SUMS + 1, ROWS, count), F32),
                *[pltpu.VMEM(*each) for each in slot],
                *([] if trail else [pltpu.VMEM(*each) for each in slot]),
            ],
            compiler_params=PARAMS,
            cost_estimate=pl.CostEstimate(
                flops=FLOPS_PER_PAIR * pairs, bytes_accessed=32 * count * number, transcendentals=pairs
            ),
        )(*operands)
    )
    total = result.pop(0)
    share = result.pop(0) if factor else share
    right = result.pop(0) if first else right
    return total, share, right, (tuple(result) if trail else None)


def finish_kernel(own, edges, sums, faces, grad):
    verts = grad.shape[1]
    count = own.shape[1]
    twice = 2.0 * own[6:7, :]
    total = sums[6:7, :]
    g_center = [
        twice * (own[3 + c : 4 + c, :] * total + sums[c : c + 1, :] - 2.0 * sums[7 + c : 8 + c, :]) for c in range(3)
    ]
    g_area = [twice * sums[3 + c : 4 + c, :] for c in range(3)]
    e1 = [edges[c : c + 1, :] for c in range(3)]
    e2 = [edges[3 + c : 4 + c, :] for c in range(3)]
    zero = jnp.zeros((ROWS - 3, count), F32)
    corners = [[], [], []]
    for c in range(3):
        n, m = (c + 1) % 3, (c + 2) % 3
        g1 = 0.5 * (e2[n] * g_area[m] - e2[m] * g_area[n])
        g2 = 0.5 * (g_area[n] * e1[m] - g_area[m] * e1[n])
        part = g_center[c] / 3.0
        corners[0].append(part - g1 - g2)
        corners[1].append(part + g1)
        corners[2].append(part + g2)
    total = jnp.zeros((3 * ROWS, verts), F32)
    for k in range(3):
        left = jnp.concatenate(pieces(jnp.concatenate(corners[k] + [zero], 0)), 0).astype(BF16)
        total += lax.dot_general(
            left, one_hot(faces[k : k + 1, :], verts), (((1,), (1,)), ((), ())), preferred_element_type=F32
        )
    total = total[0:ROWS] + total[ROWS : 2 * ROWS] + total[2 * ROWS : 3 * ROWS]
    grad[...] = total[0:3] / count


def gather(own, axis, size, wanted):
    if size & (size - 1) == 0 and len(wanted) == size - 1:
        found = {}
        held = own[None]
        mask = size // 2
        while mask:
            other = flip(held, axis, mask)
            for offset in wanted:
                if offset & -offset == mask:
                    found[offset] = (other, "ring")
            held = jnp.concatenate([held, other], 0) if mask > 1 else held
            mask //= 2
        return found
    return {offset: (from_ahead(own, axis, offset), None) for offset in wanted}


def shards(vertices, faces, trial_step, accepted, face_weight, partner_shift):
    count = faces.shape[1]
    verts = vertices.shape[1]
    groups, blocks = lax.axis_size("grp"), lax.axis_size("blk")
    block_shape = jax.ShapeDtypeStruct((ROWS, count), F32)
    arguments = (accepted, partner_shift, vertices, trial_step, faces, face_weight)
    homes = [pltpu.SMEM] * 2 + [pltpu.VMEM] * 4
    met_shape = jax.ShapeDtypeStruct((-(-groups // ROWS) * ROWS, LANES), F32)
    sent, own, edges, times = pl.pallas_call(
        functools.partial(geometry_kernel, groups),
        out_shape=(block_shape, block_shape, block_shape, met_shape),
        in_specs=[pl.BlockSpec(memory_space=pltpu.HBM)] * 6,
        out_specs=(VMEM,) * 4,
        scratch_shapes=[home(a.shape, a.dtype) for home, a in zip(homes, arguments)]
        + [pltpu.VMEM((ROWS, verts), F32), pltpu.SemaphoreType.DMA((6,))],
    )(*arguments)

    window = [o for o in range(1, blocks) if window_times(o, blocks)]
    ring = gather(sent, "blk", blocks, window)
    across = gather(sent, "grp", groups, list(range(1, groups)))

    def visit(items, factor, state, following=None):
        arrays, plan = [], []
        for axis, offset in items + ([following] if following else []):
            if axis == "self":
                array, index = own, None
            else:
                array, index = (ring if axis == "blk" else across)[offset]
            where = [i for i, known in enumerate(arrays) if known is array]
            if not where:
                arrays.append(array)
                where = [len(arrays) - 1]
            plan.append((where[0], index, axis, offset))
        return tiles(times, own, arrays, tuple(plan), factor, state, following is not None, blocks)

    def stage(offset, size):
        return -(offset & -offset) if size & (size - 1) == 0 else 0

    middle = [("blk", o) for o in window if 2 * o == blocks] + [("grp", o) for o in range(1, groups) if 2 * o == groups]
    early_blk = sorted((o for o in window if 2 * o < blocks), key=lambda o: (stage(o, blocks), o))
    early_grp = [("grp", o) for o in range(1, groups) if 2 * o < groups]
    late = [("grp", o) for o in range(1, groups) if 2 * o > groups]
    late += [("blk", o) for o in sorted((o for o in window if 2 * o > blocks), key=lambda o: (stage(o, blocks), o))]
    first = early_grp + [("blk", o) for o in early_blk[: len(early_blk) // 3]]
    second = [("blk", o) for o in early_blk[len(early_blk) // 3 :]]

    state = visit([("self", 0)], 0.5, (None, None, None, None))
    chain = [(items, factor) for items, factor in ((middle, 0.5), (first, 1.0), (second, 1.0)) if items]
    for index, (items, factor) in enumerate(chain):
        state = visit(items, factor, state, late[0] if late and index == len(chain) - 1 else None)
    share = state[1]
    rounds = []
    for axis, size in (("blk", blocks), ("grp", groups)):
        if size & (size - 1) == 0:
            rounds += [(axis, size >> k) for k in range(1, size.bit_length())]
        else:
            rounds.append((axis, 0))

    def exchange(value, axis, mask):
        if mask:
            return flip(value, axis, mask)
        return sum(from_ahead(value, axis, o) for o in range(1, lax.axis_size(axis)))

    def last_of(total):
        return pl.pallas_call(
            finish_kernel,
            out_shape=jax.ShapeDtypeStruct((3, verts), F32),
            in_specs=[VMEM] * 4,
            out_specs=VMEM,
            compiler_params=PARAMS,
            cost_estimate=pl.CostEstimate(flops=1500000000, bytes_accessed=64 * count, transcendentals=0),
        )(own, edges, total, faces)

    for index, (axis, mask) in enumerate(rounds):
        received = exchange(share, axis, mask)
        if index < len(late):
            state = visit([late[index]], 0.0, state, late[index + 1] if index + 1 < len(late) else None)
            state, received = lax.optimization_barrier((state, received))
        elif index == len(late):
            grad, received = lax.optimization_barrier((last_of(state[0]), received))
        share = share + received
    if len(rounds) <= len(late):
        for index in range(len(rounds), len(late)):
            state = visit([late[index]], 0.0, state, late[index + 1] if index + 1 < len(late) else None)
        grad = last_of(state[0])
    energy = jnp.sum(share) / (count * count * groups * blocks)
    return grad, energy.reshape(1)


def solution(mesh):
    placed = (
        P(None, ("grp", "blk")),
        P(None, ("grp", "blk")),
        P(None, ("grp", "blk")),
        P("grp"),
        P(("grp", "blk")),
        P(),
    )
    return jax.shard_map(
        shards,
        mesh=mesh,
        in_specs=placed,
        out_specs=(P(None, ("grp", "blk")), P()),
        check_vma=False,
    )
```

```python
import functools

import jax
import jax.numpy as jnp
from jax import lax
from jax.experimental import pallas as pl
from jax.experimental.pallas import tpu as pltpu
from jax.sharding import PartitionSpec as P

HOPS = 4
EPS2 = 0.05
ROWS = 8
LANES = 128
DEPTH = 64
SUMS = 10
F32 = jnp.float32
BF16 = jnp.bfloat16
VMEM = pl.BlockSpec(memory_space=pltpu.VMEM)
SMEM = pl.BlockSpec(memory_space=pltpu.SMEM)
FLOPS_PER_PAIR = 8000
PARAMS = pltpu.CompilerParams(vmem_limit_bytes=16 * 1024 * 1024)


def flip(value, axis, mask):
    count = lax.axis_size(axis)
    return lax.ppermute(value, axis, [(i, i ^ mask) for i in range(count)])


def from_ahead(value, axis, by):
    count = lax.axis_size(axis)
    return lax.ppermute(value, axis, [(i, (i - by) % count) for i in range(count)])


def pieces(value):
    high = value.astype(BF16).astype(F32)
    rest = value - high
    middle = rest.astype(BF16).astype(F32)
    return high, middle, rest - middle


def one_hot(row, count):
    rows = lax.broadcasted_iota(jnp.int32, (count, row.shape[1]), 0)
    return jnp.where(rows == row, 1.0, 0.0).astype(BF16)


def partner_times(shift, here, there, groups):
    times = jnp.int32(0)
    for r in range(shift.shape[0]):
        times += (lax.rem(here + shift[r, here], groups) == there).astype(jnp.int32)
        times += (lax.rem(there + shift[r, there], groups) == here).astype(jnp.int32)
    return times


def geometry_kernel(groups, *refs):
    far, (sent, own, edges, times), near, (padded, arrived) = refs[:6], refs[6:10], refs[10:16], refs[16:]
    accepted, shift, vertices, trial_step, faces, weight = near
    copies = [pltpu.make_async_copy(far[i], near[i], arrived.at[i]) for i in range(6)]
    for copy in copies:
        copy.start()
    verts = vertices.shape[1]
    count = faces.shape[1]
    padded[...] = jnp.zeros_like(padded)
    for copy in copies:
        copy.wait()
    here = lax.axis_index("grp")
    times[...] = jnp.zeros_like(times)
    for offset in range(1, groups):
        met = partner_times(shift, here, lax.rem(here + offset, groups), groups).astype(F32)
        times[offset : offset + 1, :] = jnp.zeros((1, LANES), F32) + met
    padded[0:3, :] = vertices[...] + accepted[0].astype(F32) * trial_step[...]
    left = jnp.concatenate(pieces(padded[...]), 0).astype(BF16)

    def corner(k):
        picked = jnp.dot(left, one_hot(faces[k : k + 1, :], verts), preferred_element_type=F32)
        picked = picked[0:ROWS] + picked[ROWS : 2 * ROWS] + picked[2 * ROWS : 3 * ROWS]
        return [picked[c : c + 1] for c in range(3)]

    first, second, third = corner(0), corner(1), corner(2)
    center = [(first[c] + second[c] + third[c]) / 3.0 for c in range(3)]
    e1 = [second[c] - first[c] for c in range(3)]
    e2 = [third[c] - first[c] for c in range(3)]
    area = []
    for c in range(3):
        n, m = (c + 1) % 3, (c + 2) % 3
        area.append(0.5 * (e1[n] * e2[m] - e1[m] * e2[n]))
    for c in range(3):
        own[c : c + 1, :] = center[c]
        own[3 + c : 4 + c, :] = area[c]
        edges[c : c + 1, :] = e1[c]
        edges[3 + c : 4 + c, :] = e2[c]
    own[6:7, :] = weight[...].reshape(1, count)
    own[7:8, :] = center[0] * area[0] + center[1] * area[1] + center[2] * area[2]
    edges[6:8, :] = jnp.zeros((2, count), F32)
    sent[...] = own[...]


def window_times(offset, blocks):
    return sum(int((k - offset) % blocks == 0) + int((k + offset) % blocks == 0) for k in range(1, HOPS + 1))


def place_of(mask, size):
    place, step, bit = 0, 1, size // 2
    while bit:
        place = place + jnp.bitwise_and(mask // bit, 1) * step
        step, bit = step * 2, bit // 2
    return place


def tiles_kernel(plan, blocks, factor, gradient, first, carry, lead, trail, *refs):
    refs = list(refs)
    own = refs.pop(0)
    count = own.shape[1]
    unit = count // 2
    chunks = count // LANES
    part = unit // chunks
    others = [refs.pop(0) for _ in range(1 + max(item[0] for item in plan))]
    met = refs.pop(0) if any(item[2] == "grp" for item in plan) else None
    right = None if first else refs.pop(0)
    total = refs.pop(0) if carry and gradient else None
    share_in = refs.pop(0) if carry and factor else None
    led = (refs.pop(0), refs.pop(0)) if lead else None
    out = refs.pop(0) if gradient else None
    share = refs.pop(0) if factor else None
    right = refs.pop(0) if first else right
    units = len(plan) - (1 if trail else 0)
    slots = [None, None]
    if trail:
        slots[units % 2] = (refs.pop(0), refs.pop(0))
    columns, left, sums = refs[:3]
    refs = refs[3:]
    for side in range(2):
        if slots[side] is None:
            slots[side] = (refs.pop(0), refs.pop(0))
    places = (list(range(SUMS)) if gradient else []) + ([SUMS] if factor else [])

    if first:
        zero = jnp.zeros((ROWS, count), F32)
        zero1, zero3 = jnp.zeros((1, count), F32), jnp.zeros((3, count), F32)
        from_own = jnp.concatenate([-own[3:6, :], zero3, own[7:8, :], zero1], 0)
        from_other = jnp.concatenate([zero3, own[0:3, :], zero1, zero1 - 1.0], 0)
        for side, rows in enumerate((from_own, from_other)):
            high, middle, low = pieces(rows)
            right[:, side * count : (side + 1) * count] = jnp.concatenate(
                [zero, high, middle, low, high, middle, high, zero], 0
            ).astype(BF16)
    row = lax.broadcasted_iota(jnp.int32, (ROWS, unit), 0)
    for u, (source, index, axis, offset, half) in enumerate(plan):
        if lead and u == 0:
            continue
        if index == "ring":
            size = lax.axis_size(axis)
            here = lax.axis_index(axis)
            there = lax.rem(here + offset, size)
            block = others[source][place_of(jnp.bitwise_xor(here, there), size) - size // 2 // (offset & -offset)]
        elif index is None:
            block = others[source][...]
        else:
            block = others[source][index]
        block = block[:, half * unit : (half + 1) * unit]
        if axis == "self":
            times = 1.0 + window_times(0, blocks)
        elif axis == "blk":
            times = float(window_times(offset, blocks))
        else:
            times = jnp.concatenate([met[offset : offset + 1, :]] * (unit // LANES), 1)
        block = jnp.where(row == 6, block * times, block)
        high, middle, low = pieces(jnp.where(row == 6, 1.0, block))
        turned = jnp.concatenate([block, high, high, high, middle, middle, low, jnp.zeros_like(block)], 0).T
        columns[u * unit : (u + 1) * unit, :] = turned[:, 0:ROWS]
        left[u * unit : (u + 1) * unit, :] = turned.astype(BF16)
    for k in places:
        sums[k] = jnp.zeros((ROWS, count), F32)

    def fill(u, chunk, slot):
        wide, proj = slot
        source = pl.multiple_of(u * unit + chunk * part, part)
        target = pl.multiple_of(chunk * part, part)
        proj[pl.ds(target, part), :] = jnp.dot(left[pl.ds(source, part), :], right[...], preferred_element_type=F32)
        for k in range(7) if gradient or u == units else (0, 1, 2, 6):
            for g in range(part // ROWS):
                group = columns[pl.ds(pl.multiple_of(source + g * ROWS, ROWS), ROWS), :]
                wide[k, pl.ds(pl.multiple_of(target + g * ROWS, ROWS), ROWS), :] = jnp.broadcast_to(
                    group[:, k : k + 1], (ROWS, LANES)
                )

    def work(chunk, slot, following):
        wide, proj = slot
        at_lane = pl.multiple_of(chunk * LANES, LANES)
        span = pl.ds(at_lane, LANES)
        a = [jnp.broadcast_to(own[k : k + 1, span], (ROWS, LANES)) for k in range(3)]
        s = {k: sums[k, :, span] for k in places}
        for g in range(unit // ROWS):
            if g == unit // ROWS - 1:
                stored = pl.ds(pl.multiple_of(chunk * part, ROWS), ROWS)
                seen = following[0][6, stored, :] + following[1][stored, 0:LANES]
                s[places[-1]] += jnp.where(chunk < 0, seen, 0.0)
            rows = slice(g * ROWS, (g + 1) * ROWS)
            b = {k: wide[k, rows, :] for k in (range(7) if gradient else (0, 1, 2, 6))}
            proj_a = proj[rows, span]
            proj_b = proj[rows, pl.ds(pl.multiple_of(count + at_lane, LANES), LANES)]
            d0, d1, d2 = a[0] - b[0], a[1] - b[1], a[2] - b[2]
            dist = d0 * d0 + d1 * d1 + (d2 * d2 + EPS2)
            inverse = 1.0 / dist
            square = inverse * inverse * b[6]
            if not gradient:
                s[SUMS] += (proj_a * proj_a + proj_b * proj_b) * square
                continue
            alpha = proj_a * square
            beta = proj_b * square
            kernel = proj_a * alpha + proj_b * beta
            gamma = kernel * inverse
            s[0] += beta * b[3]
            s[1] += beta * b[4]
            s[2] += beta * b[5]
            s[3] += alpha * d0
            s[4] += alpha * d1
            s[5] += alpha * d2
            s[6] += alpha
            s[7] += gamma * d0
            s[8] += gamma * d1
            s[9] += gamma * d2
            if factor:
                s[SUMS] += kernel
        for k in places:
            sums[k, :, span] = s[k]

    def over_chunks(now, u, slot):
        def step(chunk, carried):
            fill(u, chunk, slot)
            work(chunk, now, slot)
            return carried

        lax.fori_loop(0, chunks, step, 0)

    if not lead:
        for chunk in range(chunks):
            fill(0, chunk, slots[0])
    for u in range(units):
        over_chunks(led if lead and u == 0 else slots[u % 2], min(u + 1, len(plan) - 1), slots[(u + 1) % 2])
    if gradient:
        for k in range(SUMS):
            line = jnp.sum(sums[k], axis=0, keepdims=True)
            out[k : k + 1, :] = line + total[k : k + 1, :] if carry else line
    if factor:
        weighted = sums[SUMS] * (factor * own[6:7, :])
        part_share = weighted[:, 0:LANES]
        for chunk in range(1, chunks):
            part_share = part_share + weighted[:, chunk * LANES : (chunk + 1) * LANES]
        share[...] = part_share + share_in[...] if carry else part_share


def tiles(times, own, arrays, plan, factor, gradient, state, trail, blocks):
    count = own.shape[1]
    unit = count // 2
    total, share, right, led = state
    first, carry, lead = right is None, total is not None, led is not None
    number = len(plan) - (1 if trail else 0)
    body = functools.partial(tiles_kernel, plan, blocks, factor, gradient, first, carry, lead, trail)
    operands = [own, *arrays] + ([times] if any(item[2] == "grp" for item in plan) else [])
    operands += ([] if first else [right]) + ([total] if carry and gradient else [])
    operands += ([share] if carry and factor else []) + (list(led) if lead else [])
    slot = [((7, unit, LANES), F32), ((unit, 2 * count), F32)]
    shapes = [jax.ShapeDtypeStruct((SUMS, count), F32)] if gradient else []
    if factor:
        shapes.append(jax.ShapeDtypeStruct((ROWS, LANES), F32))
    if first:
        shapes.append(jax.ShapeDtypeStruct((DEPTH, 2 * count), BF16))
    if trail:
        shapes += [jax.ShapeDtypeStruct(*each) for each in slot]
    pairs = number * unit * count
    result = list(
        pl.pallas_call(
            body,
            out_shape=shapes,
            in_specs=[VMEM] * len(operands),
            out_specs=[VMEM] * len(shapes),
            scratch_shapes=[
                pltpu.VMEM((len(plan) * unit, ROWS), F32),
                pltpu.VMEM((len(plan) * unit, DEPTH), BF16),
                pltpu.VMEM((SUMS + 1, ROWS, count), F32),
                *[pltpu.VMEM(*each) for each in slot],
                *([] if trail else [pltpu.VMEM(*each) for each in slot]),
            ],
            compiler_params=PARAMS,
            cost_estimate=pl.CostEstimate(
                flops=FLOPS_PER_PAIR * pairs, bytes_accessed=32 * unit * number, transcendentals=pairs
            ),
        )(*operands)
    )
    total = result.pop(0) if gradient else total
    share = result.pop(0) if factor else share
    right = result.pop(0) if first else right
    return total, share, right, (tuple(result) if trail else None)


def finish_kernel(own, edges, sums, faces, grad):
    verts = grad.shape[1]
    count = own.shape[1]
    twice = 2.0 * own[6:7, :]
    total = sums[6:7, :]
    g_center = [
        twice * (own[3 + c : 4 + c, :] * total + sums[c : c + 1, :] - 2.0 * sums[7 + c : 8 + c, :]) for c in range(3)
    ]
    g_area = [twice * sums[3 + c : 4 + c, :] for c in range(3)]
    e1 = [edges[c : c + 1, :] for c in range(3)]
    e2 = [edges[3 + c : 4 + c, :] for c in range(3)]
    zero = jnp.zeros((ROWS - 3, count), F32)
    corners = [[], [], []]
    for c in range(3):
        n, m = (c + 1) % 3, (c + 2) % 3
        g1 = 0.5 * (e2[n] * g_area[m] - e2[m] * g_area[n])
        g2 = 0.5 * (g_area[n] * e1[m] - g_area[m] * e1[n])
        part = g_center[c] / 3.0
        corners[0].append(part - g1 - g2)
        corners[1].append(part + g1)
        corners[2].append(part + g2)
    total = jnp.zeros((3 * ROWS, verts), F32)
    for k in range(3):
        left = jnp.concatenate(pieces(jnp.concatenate(corners[k] + [zero], 0)), 0).astype(BF16)
        total += lax.dot_general(
            left, one_hot(faces[k : k + 1, :], verts), (((1,), (1,)), ((), ())), preferred_element_type=F32
        )
    total = total[0:ROWS] + total[ROWS : 2 * ROWS] + total[2 * ROWS : 3 * ROWS]
    grad[...] = total[0:3] / count


def gather(own, axis, size, wanted):
    if size & (size - 1) == 0 and len(wanted) == size - 1:
        found = {}
        held = own[None]
        mask = size // 2
        while mask:
            other = flip(held, axis, mask)
            for offset in wanted:
                if offset & -offset == mask:
                    found[offset] = (other, "ring")
            held = jnp.concatenate([held, other], 0) if mask > 1 else held
            mask //= 2
        return found
    return {offset: (from_ahead(own, axis, offset), None) for offset in wanted}


def shards(vertices, faces, trial_step, accepted, face_weight, partner_shift):
    count = faces.shape[1]
    verts = vertices.shape[1]
    groups, blocks = lax.axis_size("grp"), lax.axis_size("blk")
    block_shape = jax.ShapeDtypeStruct((ROWS, count), F32)
    arguments = (accepted, partner_shift, vertices, trial_step, faces, face_weight)
    homes = [pltpu.SMEM] * 2 + [pltpu.VMEM] * 4
    met_shape = jax.ShapeDtypeStruct((-(-groups // ROWS) * ROWS, LANES), F32)
    sent, own, edges, times = pl.pallas_call(
        functools.partial(geometry_kernel, groups),
        out_shape=(block_shape, block_shape, block_shape, met_shape),
        in_specs=[pl.BlockSpec(memory_space=pltpu.HBM)] * 6,
        out_specs=(VMEM,) * 4,
        scratch_shapes=[home(a.shape, a.dtype) for home, a in zip(homes, arguments)]
        + [pltpu.VMEM((ROWS, verts), F32), pltpu.SemaphoreType.DMA((6,))],
    )(*arguments)

    window = [o for o in range(1, blocks) if window_times(o, blocks)]
    ring = gather(sent, "blk", blocks, window)
    across = gather(sent, "grp", groups, list(range(1, groups)))

    def halves(items):
        return [(axis, offset, half) for axis, offset in items for half in range(2)]

    def visit(parts, factor, gradient, state, following):
        arrays, plan = [], []
        for axis, offset, half in parts + following:
            if axis == "self":
                array, index = own, None
            else:
                array, index = (ring if axis == "blk" else across)[offset]
            where = [i for i, known in enumerate(arrays) if known is array]
            if not where:
                arrays.append(array)
                where = [len(arrays) - 1]
            plan.append((where[0], index, axis, offset, half))
        return tiles(times, own, arrays, tuple(plan), factor, gradient, state, len(following) > 0, blocks)

    def stage(offset, size):
        return -(offset & -offset) if size & (size - 1) == 0 else 0

    middle = [("blk", o) for o in window if 2 * o == blocks] + [("grp", o) for o in range(1, groups) if 2 * o == groups]
    early_blk = sorted((o for o in window if 2 * o < blocks), key=lambda o: (stage(o, blocks), o))
    early_grp = [("grp", o) for o in range(1, groups) if 2 * o < groups]
    late = [("grp", o) for o in range(1, groups) if 2 * o > groups]
    late += [("blk", o) for o in sorted((o for o in window if 2 * o > blocks), key=lambda o: (stage(o, blocks), o))]
    first = early_grp + [("blk", o) for o in early_blk[: len(early_blk) // 3]]
    second = [("blk", o) for o in early_blk[len(early_blk) // 3 :]]

    state = visit(halves([("self", 0)]), 0.5, True, (None, None, None, None), [])
    for items, factor in ((middle, 0.5), (first, 1.0)):
        if items:
            state = visit(halves(items), factor, True, state, [])
    late = halves(late + second)
    if second:
        state = visit(halves(second), 1.0, False, state, late[:1])
    share = state[1]
    rounds = []
    for axis, size in (("blk", blocks), ("grp", groups)):
        if size & (size - 1) == 0:
            rounds += [(axis, size >> k) for k in range(1, size.bit_length())]
        else:
            rounds.append((axis, 0))

    def exchange(value, axis, mask):
        if mask:
            return flip(value, axis, mask)
        return sum(from_ahead(value, axis, o) for o in range(1, lax.axis_size(axis)))

    def last_of(total):
        return pl.pallas_call(
            finish_kernel,
            out_shape=jax.ShapeDtypeStruct((3, verts), F32),
            in_specs=[VMEM] * 4,
            out_specs=VMEM,
            compiler_params=PARAMS,
            cost_estimate=pl.CostEstimate(flops=1500000000, bytes_accessed=64 * count, transcendentals=0),
        )(own, edges, total, faces)

    covers = max(1, len(rounds) - 1)
    edges_of = [len(late) * i // covers for i in range(covers + 1)]
    for index in range(max(covers, len(rounds))):
        received = None
        if index < len(rounds):
            received = exchange(share, *rounds[index])
        if index < covers:
            begin, end = edges_of[index], edges_of[index + 1]
            if end > begin:
                state = visit(late[begin:end], 0.0, True, state, late[end : end + 1])
            done = state
        if index == len(rounds) - 1:
            grad = last_of(state[0])
            done = grad
        if received is not None:
            if index < len(rounds) - 1:
                state, received = lax.optimization_barrier((done, received))
            share = share + received
    if not rounds:
        grad = last_of(state[0])
    energy = jnp.sum(share) / (count * count * groups * blocks)
    return grad, energy.reshape(1)


def solution(mesh):
    placed = (
        P(None, ("grp", "blk")),
        P(None, ("grp", "blk")),
        P(None, ("grp", "blk")),
        P("grp"),
        P(("grp", "blk")),
        P(),
    )
    return jax.shard_map(
        shards,
        mesh=mesh,
        in_specs=placed,
        out_specs=(P(None, ("grp", "blk")), P()),
        check_vma=False,
    )
```

```python
import functools

import jax
import jax.numpy as jnp
from jax import lax
from jax.experimental import pallas as pl
from jax.experimental.pallas import tpu as pltpu
from jax.sharding import PartitionSpec as P

HOPS = 4
EPS2 = 0.05
ROWS = 8
LANES = 128
DEPTH = 64
SUMS = 10
F32 = jnp.float32
BF16 = jnp.bfloat16
VMEM = pl.BlockSpec(memory_space=pltpu.VMEM)
SMEM = pl.BlockSpec(memory_space=pltpu.SMEM)
FLOPS_PER_PAIR = 8000
GRADIENT_CHUNKS = 1
PARAMS = pltpu.CompilerParams(vmem_limit_bytes=16 * 1024 * 1024)


def flip(value, axis, mask):
    count = lax.axis_size(axis)
    return lax.ppermute(value, axis, [(i, i ^ mask) for i in range(count)])


def from_ahead(value, axis, by):
    count = lax.axis_size(axis)
    return lax.ppermute(value, axis, [(i, (i - by) % count) for i in range(count)])


def pieces(value):
    high = value.astype(BF16).astype(F32)
    rest = value - high
    middle = rest.astype(BF16).astype(F32)
    return high, middle, rest - middle


def one_hot(row, count):
    rows = lax.broadcasted_iota(jnp.int32, (count, row.shape[1]), 0)
    return jnp.where(rows == row, 1.0, 0.0).astype(BF16)


def partner_times(shift, here, there, groups):
    times = jnp.int32(0)
    for r in range(shift.shape[0]):
        times += (lax.rem(here + shift[r, here], groups) == there).astype(jnp.int32)
        times += (lax.rem(there + shift[r, there], groups) == here).astype(jnp.int32)
    return times


def geometry_kernel(groups, *refs):
    far, (sent, own, edges, times), near, (padded, arrived) = refs[:6], refs[6:10], refs[10:16], refs[16:]
    accepted, shift, vertices, trial_step, faces, weight = near
    copies = [pltpu.make_async_copy(far[i], near[i], arrived.at[i]) for i in range(6)]
    for copy in copies:
        copy.start()
    verts = vertices.shape[1]
    count = faces.shape[1]
    padded[...] = jnp.zeros_like(padded)
    for copy in copies:
        copy.wait()
    here = lax.axis_index("grp")
    times[...] = jnp.zeros_like(times)
    for offset in range(1, groups):
        met = partner_times(shift, here, lax.rem(here + offset, groups), groups).astype(F32)
        times[offset : offset + 1, :] = jnp.zeros((1, LANES), F32) + met
    padded[0:3, :] = vertices[...] + accepted[0].astype(F32) * trial_step[...]
    left = jnp.concatenate(pieces(padded[...]), 0).astype(BF16)

    def corner(k):
        picked = jnp.dot(left, one_hot(faces[k : k + 1, :], verts), preferred_element_type=F32)
        picked = picked[0:ROWS] + picked[ROWS : 2 * ROWS] + picked[2 * ROWS : 3 * ROWS]
        return [picked[c : c + 1] for c in range(3)]

    first, second, third = corner(0), corner(1), corner(2)
    center = [(first[c] + second[c] + third[c]) / 3.0 for c in range(3)]
    e1 = [second[c] - first[c] for c in range(3)]
    e2 = [third[c] - first[c] for c in range(3)]
    area = []
    for c in range(3):
        n, m = (c + 1) % 3, (c + 2) % 3
        area.append(0.5 * (e1[n] * e2[m] - e1[m] * e2[n]))
    for c in range(3):
        own[c : c + 1, :] = center[c]
        own[3 + c : 4 + c, :] = area[c]
        edges[c : c + 1, :] = e1[c]
        edges[3 + c : 4 + c, :] = e2[c]
    own[6:7, :] = weight[...].reshape(1, count)
    own[7:8, :] = center[0] * area[0] + center[1] * area[1] + center[2] * area[2]
    edges[6:8, :] = jnp.zeros((2, count), F32)
    sent[...] = own[...]


def window_times(offset, blocks):
    return sum(int((k - offset) % blocks == 0) + int((k + offset) % blocks == 0) for k in range(1, HOPS + 1))


def place_of(mask, size):
    place, step, bit = 0, 1, size // 2
    while bit:
        place = place + jnp.bitwise_and(mask // bit, 1) * step
        step, bit = step * 2, bit // 2
    return place


def tiles_kernel(plan, blocks, factor, gradient, first, carry, lead, trail, *refs):
    refs = list(refs)
    own = refs.pop(0)
    count = own.shape[1]
    unit = count // 2
    chunks = count // LANES
    part = unit // chunks
    others = [refs.pop(0) for _ in range(1 + max(item[0] for item in plan))]
    met = refs.pop(0) if any(item[2] == "grp" for item in plan) else None
    right = None if first else refs.pop(0)
    total = refs.pop(0) if carry and gradient else None
    share_in = refs.pop(0) if carry and factor else None
    led = (refs.pop(0), refs.pop(0)) if lead else None
    out = refs.pop(0) if gradient else None
    share = refs.pop(0) if factor else None
    right = refs.pop(0) if first else right
    units = len(plan) - (1 if trail else 0)
    slots = [None, None]
    if trail:
        slots[units % 2] = (refs.pop(0), refs.pop(0))
    columns, left, sums = refs[:3]
    refs = refs[3:]
    for side in range(2):
        if slots[side] is None:
            slots[side] = (refs.pop(0), refs.pop(0))
    places = (list(range(SUMS)) if gradient else []) + ([SUMS] if factor else [])

    if first:
        zero = jnp.zeros((ROWS, count), F32)
        zero1, zero3 = jnp.zeros((1, count), F32), jnp.zeros((3, count), F32)
        from_own = jnp.concatenate([-own[3:6, :], zero3, own[7:8, :], zero1], 0)
        from_other = jnp.concatenate([zero3, own[0:3, :], zero1, zero1 - 1.0], 0)
        for side, rows in enumerate((from_own, from_other)):
            high, middle, low = pieces(rows)
            right[:, side * count : (side + 1) * count] = jnp.concatenate(
                [zero, high, middle, low, high, middle, high, zero], 0
            ).astype(BF16)
    row = lax.broadcasted_iota(jnp.int32, (ROWS, unit), 0)
    for u, (source, index, axis, offset, half) in enumerate(plan):
        if lead and u == 0:
            continue
        if index == "ring":
            size = lax.axis_size(axis)
            here = lax.axis_index(axis)
            there = lax.rem(here + offset, size)
            block = others[source][place_of(jnp.bitwise_xor(here, there), size) - size // 2 // (offset & -offset)]
        elif index is None:
            block = others[source][...]
        else:
            block = others[source][index]
        block = block[:, half * unit : (half + 1) * unit]
        if axis == "self":
            times = 1.0 + window_times(0, blocks)
        elif axis == "blk":
            times = float(window_times(offset, blocks))
        else:
            times = jnp.concatenate([met[offset : offset + 1, :]] * (unit // LANES), 1)
        block = jnp.where(row == 6, block * times, block)
        high, middle, low = pieces(jnp.where(row == 6, 1.0, block))
        turned = jnp.concatenate([block, high, high, high, middle, middle, low, jnp.zeros_like(block)], 0).T
        columns[u * unit : (u + 1) * unit, :] = turned[:, 0:ROWS]
        left[u * unit : (u + 1) * unit, :] = turned.astype(BF16)
    for k in places:
        sums[k] = jnp.zeros((ROWS, count), F32)

    def fill(u, chunk, slot):
        wide, proj = slot
        source = pl.multiple_of(u * unit + chunk * part, part)
        target = pl.multiple_of(chunk * part, part)
        proj[pl.ds(target, part), :] = jnp.dot(left[pl.ds(source, part), :], right[...], preferred_element_type=F32)
        for k in range(7) if gradient or u == units else (0, 1, 2, 6):
            for g in range(part // ROWS):
                group = columns[pl.ds(pl.multiple_of(source + g * ROWS, ROWS), ROWS), :]
                wide[k, pl.ds(pl.multiple_of(target + g * ROWS, ROWS), ROWS), :] = jnp.broadcast_to(
                    group[:, k : k + 1], (ROWS, LANES)
                )

    together = GRADIENT_CHUNKS if gradient else chunks
    never = lax.axis_index("blk") < 0

    def work(chunk, slot, following, is_last):
        wide, proj = slot
        at_lane = pl.multiple_of(chunk * LANES, LANES)
        span = pl.ds(at_lane, LANES)
        a = [jnp.broadcast_to(own[k : k + 1, span], (ROWS, LANES)) for k in range(3)]
        s = {k: sums[k, :, span] for k in places}
        for g in range(unit // ROWS):
            if is_last and g == unit // ROWS - 1:
                stored = pl.ds(pl.multiple_of(chunk * part, ROWS), ROWS)
                seen = following[0][6, stored, :] + following[1][stored, 0:LANES]
                s[places[-1]] += jnp.where(never, seen, 0.0)
            rows = slice(g * ROWS, (g + 1) * ROWS)
            b = {k: wide[k, rows, :] for k in (range(7) if gradient else (0, 1, 2, 6))}
            proj_a = proj[rows, span]
            proj_b = proj[rows, pl.ds(pl.multiple_of(count + at_lane, LANES), LANES)]
            d0, d1, d2 = a[0] - b[0], a[1] - b[1], a[2] - b[2]
            dist = d0 * d0 + d1 * d1 + (d2 * d2 + EPS2)
            inverse = 1.0 / dist
            square = inverse * inverse * b[6]
            if not gradient:
                s[SUMS] += (proj_a * proj_a + proj_b * proj_b) * square
                continue
            alpha = proj_a * square
            beta = proj_b * square
            kernel = proj_a * alpha + proj_b * beta
            gamma = kernel * inverse
            s[0] += beta * b[3]
            s[1] += beta * b[4]
            s[2] += beta * b[5]
            s[3] += alpha * d0
            s[4] += alpha * d1
            s[5] += alpha * d2
            s[6] += alpha
            s[7] += gamma * d0
            s[8] += gamma * d1
            s[9] += gamma * d2
            if factor:
                s[SUMS] += kernel
        for k in places:
            sums[k, :, span] = s[k]

    def over_chunks(now, u, slot):
        def step(index, carried):
            for k in range(together):
                fill(u, index * together + k, slot)
            for k in range(together):
                work(index * together + k, now, slot, k == together - 1)
            return carried

        if together == chunks:
            step(0, 0)
        else:
            lax.fori_loop(0, chunks // together, step, 0)

    if not lead:
        for chunk in range(chunks):
            fill(0, chunk, slots[0])
    for u in range(units):
        over_chunks(led if lead and u == 0 else slots[u % 2], min(u + 1, len(plan) - 1), slots[(u + 1) % 2])
    if gradient:
        for k in range(SUMS):
            line = jnp.sum(sums[k], axis=0, keepdims=True)
            out[k : k + 1, :] = line + total[k : k + 1, :] if carry else line
    if factor:
        weighted = sums[SUMS] * (factor * own[6:7, :])
        part_share = weighted[:, 0:LANES]
        for chunk in range(1, chunks):
            part_share = part_share + weighted[:, chunk * LANES : (chunk + 1) * LANES]
        share[...] = part_share + share_in[...] if carry else part_share


def tiles(times, own, arrays, plan, factor, gradient, state, trail, blocks):
    count = own.shape[1]
    unit = count // 2
    total, share, right, led = state
    first, carry, lead = right is None, total is not None, led is not None
    number = len(plan) - (1 if trail else 0)
    body = functools.partial(tiles_kernel, plan, blocks, factor, gradient, first, carry, lead, trail)
    operands = [own, *arrays] + ([times] if any(item[2] == "grp" for item in plan) else [])
    operands += ([] if first else [right]) + ([total] if carry and gradient else [])
    operands += ([share] if carry and factor else []) + (list(led) if lead else [])
    slot = [((7, unit, LANES), F32), ((unit, 2 * count), F32)]
    shapes = [jax.ShapeDtypeStruct((SUMS, count), F32)] if gradient else []
    if factor:
        shapes.append(jax.ShapeDtypeStruct((ROWS, LANES), F32))
    if first:
        shapes.append(jax.ShapeDtypeStruct((DEPTH, 2 * count), BF16))
    if trail:
        shapes += [jax.ShapeDtypeStruct(*each) for each in slot]
    pairs = number * unit * count
    result = list(
        pl.pallas_call(
            body,
            out_shape=shapes,
            in_specs=[VMEM] * len(operands),
            out_specs=[VMEM] * len(shapes),
            scratch_shapes=[
                pltpu.VMEM((len(plan) * unit, ROWS), F32),
                pltpu.VMEM((len(plan) * unit, DEPTH), BF16),
                pltpu.VMEM((SUMS + 1, ROWS, count), F32),
                *[pltpu.VMEM(*each) for each in slot],
                *([] if trail else [pltpu.VMEM(*each) for each in slot]),
            ],
            compiler_params=PARAMS,
            cost_estimate=pl.CostEstimate(
                flops=FLOPS_PER_PAIR * pairs, bytes_accessed=32 * unit * number, transcendentals=pairs
            ),
        )(*operands)
    )
    total = result.pop(0) if gradient else total
    share = result.pop(0) if factor else share
    right = result.pop(0) if first else right
    return total, share, right, (tuple(result) if trail else None)


def finish_kernel(own, edges, sums, faces, grad):
    verts = grad.shape[1]
    count = own.shape[1]
    twice = 2.0 * own[6:7, :]
    total = sums[6:7, :]
    g_center = [
        twice * (own[3 + c : 4 + c, :] * total + sums[c : c + 1, :] - 2.0 * sums[7 + c : 8 + c, :]) for c in range(3)
    ]
    g_area = [twice * sums[3 + c : 4 + c, :] for c in range(3)]
    e1 = [edges[c : c + 1, :] for c in range(3)]
    e2 = [edges[3 + c : 4 + c, :] for c in range(3)]
    zero = jnp.zeros((ROWS - 3, count), F32)
    corners = [[], [], []]
    for c in range(3):
        n, m = (c + 1) % 3, (c + 2) % 3
        g1 = 0.5 * (e2[n] * g_area[m] - e2[m] * g_area[n])
        g2 = 0.5 * (g_area[n] * e1[m] - g_area[m] * e1[n])
        part = g_center[c] / 3.0
        corners[0].append(part - g1 - g2)
        corners[1].append(part + g1)
        corners[2].append(part + g2)
    total = jnp.zeros((3 * ROWS, verts), F32)
    for k in range(3):
        left = jnp.concatenate(pieces(jnp.concatenate(corners[k] + [zero], 0)), 0).astype(BF16)
        total += lax.dot_general(
            left, one_hot(faces[k : k + 1, :], verts), (((1,), (1,)), ((), ())), preferred_element_type=F32
        )
    total = total[0:ROWS] + total[ROWS : 2 * ROWS] + total[2 * ROWS : 3 * ROWS]
    grad[...] = total[0:3] / count


def gather(own, axis, size, wanted):
    if size & (size - 1) == 0 and len(wanted) == size - 1:
        found = {}
        held = own[None]
        mask = size // 2
        while mask:
            other = flip(held, axis, mask)
            for offset in wanted:
                if offset & -offset == mask:
                    found[offset] = (other, "ring")
            held = jnp.concatenate([held, other], 0) if mask > 1 else held
            mask //= 2
        return found
    return {offset: (from_ahead(own, axis, offset), None) for offset in wanted}


def shards(vertices, faces, trial_step, accepted, face_weight, partner_shift):
    count = faces.shape[1]
    verts = vertices.shape[1]
    groups, blocks = lax.axis_size("grp"), lax.axis_size("blk")
    block_shape = jax.ShapeDtypeStruct((ROWS, count), F32)
    arguments = (accepted, partner_shift, vertices, trial_step, faces, face_weight)
    homes = [pltpu.SMEM] * 2 + [pltpu.VMEM] * 4
    met_shape = jax.ShapeDtypeStruct((-(-groups // ROWS) * ROWS, LANES), F32)
    sent, own, edges, times = pl.pallas_call(
        functools.partial(geometry_kernel, groups),
        out_shape=(block_shape, block_shape, block_shape, met_shape),
        in_specs=[pl.BlockSpec(memory_space=pltpu.HBM)] * 6,
        out_specs=(VMEM,) * 4,
        scratch_shapes=[home(a.shape, a.dtype) for home, a in zip(homes, arguments)]
        + [pltpu.VMEM((ROWS, verts), F32), pltpu.SemaphoreType.DMA((6,))],
    )(*arguments)

    window = [o for o in range(1, blocks) if window_times(o, blocks)]
    ring = gather(sent, "blk", blocks, window)
    across = gather(sent, "grp", groups, list(range(1, groups)))

    def halves(items):
        return [(axis, offset, half) for axis, offset in items for half in range(2)]

    def visit(parts, factor, gradient, state, following):
        arrays, plan = [], []
        for axis, offset, half in parts + following:
            if axis == "self":
                array, index = own, None
            else:
                array, index = (ring if axis == "blk" else across)[offset]
            where = [i for i, known in enumerate(arrays) if known is array]
            if not where:
                arrays.append(array)
                where = [len(arrays) - 1]
            plan.append((where[0], index, axis, offset, half))
        return tiles(times, own, arrays, tuple(plan), factor, gradient, state, len(following) > 0, blocks)

    def stage(offset, size):
        return -(offset & -offset) if size & (size - 1) == 0 else 0

    middle = [("blk", o) for o in window if 2 * o == blocks] + [("grp", o) for o in range(1, groups) if 2 * o == groups]
    early_blk = sorted((o for o in window if 2 * o < blocks), key=lambda o: (stage(o, blocks), o))
    early_grp = [("grp", o) for o in range(1, groups) if 2 * o < groups]
    late = [("grp", o) for o in range(1, groups) if 2 * o > groups]
    late += [("blk", o) for o in sorted((o for o in window if 2 * o > blocks), key=lambda o: (stage(o, blocks), o))]
    first = early_grp + [("blk", o) for o in early_blk[: len(early_blk) // 3]]
    second = [("blk", o) for o in early_blk[len(early_blk) // 3 :]]

    state = visit(halves([("self", 0)]), 0.5, True, (None, None, None, None), [])
    for items, factor in ((middle, 0.5), (first, 1.0)):
        if items:
            state = visit(halves(items), factor, True, state, [])
    late = halves(late + second)
    if second:
        state = visit(halves(second), 1.0, False, state, late[:1])
    share = state[1]
    rounds = []
    for axis, size in (("blk", blocks), ("grp", groups)):
        if size & (size - 1) == 0:
            rounds += [(axis, size >> k) for k in range(1, size.bit_length())]
        else:
            rounds.append((axis, 0))

    def exchange(value, axis, mask):
        if mask:
            return flip(value, axis, mask)
        return sum(from_ahead(value, axis, o) for o in range(1, lax.axis_size(axis)))

    def last_of(total):
        return pl.pallas_call(
            finish_kernel,
            out_shape=jax.ShapeDtypeStruct((3, verts), F32),
            in_specs=[VMEM] * 4,
            out_specs=VMEM,
            compiler_params=PARAMS,
            cost_estimate=pl.CostEstimate(flops=1500000000, bytes_accessed=64 * count, transcendentals=0),
        )(own, edges, total, faces)

    covers = max(1, len(rounds) - 1)
    edges_of = [len(late) * i // covers for i in range(covers + 1)]
    for index in range(max(covers, len(rounds))):
        received = None
        if index < len(rounds):
            received = exchange(share, *rounds[index])
        if index < covers:
            begin, end = edges_of[index], edges_of[index + 1]
            if end > begin:
                state = visit(late[begin:end], 0.0, True, state, late[end : end + 1])
            done = state
        if index == len(rounds) - 1:
            grad = last_of(state[0])
            done = grad
        if received is not None:
            if index < len(rounds) - 1:
                state, received = lax.optimization_barrier((done, received))
            share = share + received
    if not rounds:
        grad = last_of(state[0])
    energy = jnp.sum(share) / (count * count * groups * blocks)
    return grad, energy.reshape(1)


def solution(mesh):
    placed = (
        P(None, ("grp", "blk")),
        P(None, ("grp", "blk")),
        P(None, ("grp", "blk")),
        P("grp"),
        P(("grp", "blk")),
        P(),
    )
    return jax.shard_map(
        shards,
        mesh=mesh,
        in_specs=placed,
        out_specs=(P(None, ("grp", "blk")), P()),
        check_vma=False,
    )
```

```python
import functools

import jax
import jax.numpy as jnp
from jax import lax
from jax.experimental import pallas as pl
from jax.experimental.pallas import tpu as pltpu
from jax.sharding import PartitionSpec as P

HOPS = 4
EPS2 = 0.05
ROWS = 8
LANES = 128
DEPTH = 64
SUMS = 10
F32 = jnp.float32
BF16 = jnp.bfloat16
VMEM = pl.BlockSpec(memory_space=pltpu.VMEM)
SMEM = pl.BlockSpec(memory_space=pltpu.SMEM)
FLOPS_PER_PAIR = 8000
GRADIENT_CHUNKS = 1
PARAMS = pltpu.CompilerParams(vmem_limit_bytes=16 * 1024 * 1024)


def flip(value, axis, mask):
    count = lax.axis_size(axis)
    return lax.ppermute(value, axis, [(i, i ^ mask) for i in range(count)])


def from_ahead(value, axis, by):
    count = lax.axis_size(axis)
    return lax.ppermute(value, axis, [(i, (i - by) % count) for i in range(count)])


def pieces(value):
    high = value.astype(BF16).astype(F32)
    rest = value - high
    middle = rest.astype(BF16).astype(F32)
    return high, middle, rest - middle


def one_hot(row, count):
    rows = lax.broadcasted_iota(jnp.int32, (count, row.shape[1]), 0)
    return jnp.where(rows == row, 1.0, 0.0).astype(BF16)


def partner_times(shift, here, there, groups):
    times = jnp.int32(0)
    for r in range(shift.shape[0]):
        times += (lax.rem(here + shift[r, here], groups) == there).astype(jnp.int32)
        times += (lax.rem(there + shift[r, there], groups) == here).astype(jnp.int32)
    return times


def geometry_kernel(groups, *refs):
    far, (sent, own, edges, times), near, (padded, arrived) = refs[:6], refs[6:10], refs[10:16], refs[16:]
    accepted, shift, vertices, trial_step, faces, weight = near
    copies = [pltpu.make_async_copy(far[i], near[i], arrived.at[i]) for i in range(6)]
    for copy in copies:
        copy.start()
    verts = vertices.shape[1]
    count = faces.shape[1]
    padded[...] = jnp.zeros_like(padded)
    for copy in copies:
        copy.wait()
    here = lax.axis_index("grp")
    times[...] = jnp.zeros_like(times)
    for offset in range(1, groups):
        met = partner_times(shift, here, lax.rem(here + offset, groups), groups).astype(F32)
        times[offset : offset + 1, :] = jnp.zeros((1, LANES), F32) + met
    padded[0:3, :] = vertices[...] + accepted[0].astype(F32) * trial_step[...]
    left = jnp.concatenate(pieces(padded[...]), 0).astype(BF16)

    def corner(k):
        picked = jnp.dot(left, one_hot(faces[k : k + 1, :], verts), preferred_element_type=F32)
        picked = picked[0:ROWS] + picked[ROWS : 2 * ROWS] + picked[2 * ROWS : 3 * ROWS]
        return [picked[c : c + 1] for c in range(3)]

    first, second, third = corner(0), corner(1), corner(2)
    center = [(first[c] + second[c] + third[c]) / 3.0 for c in range(3)]
    e1 = [second[c] - first[c] for c in range(3)]
    e2 = [third[c] - first[c] for c in range(3)]
    area = []
    for c in range(3):
        n, m = (c + 1) % 3, (c + 2) % 3
        area.append(0.5 * (e1[n] * e2[m] - e1[m] * e2[n]))
    for c in range(3):
        own[c : c + 1, :] = center[c]
        own[3 + c : 4 + c, :] = area[c]
        edges[c : c + 1, :] = e1[c]
        edges[3 + c : 4 + c, :] = e2[c]
    own[6:7, :] = weight[...].reshape(1, count)
    own[7:8, :] = center[0] * area[0] + center[1] * area[1] + center[2] * area[2]
    edges[6:8, :] = jnp.zeros((2, count), F32)
    sent[...] = own[...]


def window_times(offset, blocks):
    return sum(int((k - offset) % blocks == 0) + int((k + offset) % blocks == 0) for k in range(1, HOPS + 1))


def place_of(mask, size):
    place, step, bit = 0, 1, size // 2
    while bit:
        place = place + jnp.bitwise_and(mask // bit, 1) * step
        step, bit = step * 2, bit // 2
    return place


def tiles_kernel(plan, blocks, factor, gradient, first, carry, lead, trail, *refs):
    refs = list(refs)
    own = refs.pop(0)
    count = own.shape[1]
    unit = count // 2
    chunks = count // LANES
    part = unit // chunks
    others = [refs.pop(0) for _ in range(1 + max(item[0] for item in plan))]
    met = refs.pop(0) if any(item[2] == "grp" for item in plan) else None
    right = None if first else refs.pop(0)
    total = refs.pop(0) if carry and gradient else None
    share_in = refs.pop(0) if carry and factor else None
    led = (refs.pop(0), refs.pop(0)) if lead else None
    out = refs.pop(0) if gradient else None
    share = refs.pop(0) if factor else None
    right = refs.pop(0) if first else right
    units = len(plan) - (1 if trail else 0)
    slots = [None, None]
    if trail:
        slots[units % 2] = (refs.pop(0), refs.pop(0))
    columns, left, sums = refs[:3]
    refs = refs[3:]
    for side in range(2):
        if slots[side] is None:
            slots[side] = (refs.pop(0), refs.pop(0))
    places = (list(range(SUMS)) if gradient else []) + ([SUMS] if factor else [])

    if first:
        zero = jnp.zeros((ROWS, count), F32)
        zero1, zero3 = jnp.zeros((1, count), F32), jnp.zeros((3, count), F32)
        from_own = jnp.concatenate([-own[3:6, :], zero3, own[7:8, :], zero1], 0)
        from_other = jnp.concatenate([zero3, own[0:3, :], zero1, zero1 - 1.0], 0)
        for side, rows in enumerate((from_own, from_other)):
            high, middle, low = pieces(rows)
            right[:, side * count : (side + 1) * count] = jnp.concatenate(
                [zero, high, middle, low, high, middle, high, zero], 0
            ).astype(BF16)
    row = lax.broadcasted_iota(jnp.int32, (ROWS, unit), 0)
    for u, (source, index, axis, offset, half) in enumerate(plan):
        if lead and u == 0:
            continue
        if index == "ring":
            size = lax.axis_size(axis)
            here = lax.axis_index(axis)
            there = lax.rem(here + offset, size)
            block = others[source][place_of(jnp.bitwise_xor(here, there), size) - size // 2 // (offset & -offset)]
        elif index is None:
            block = others[source][...]
        else:
            block = others[source][index]
        block = block[:, half * unit : (half + 1) * unit]
        if axis == "self":
            times = 1.0 + window_times(0, blocks)
        elif axis == "blk":
            times = float(window_times(offset, blocks))
        else:
            times = jnp.concatenate([met[offset : offset + 1, :]] * (unit // LANES), 1)
        block = jnp.where(row == 6, block * times, block)
        high, middle, low = pieces(jnp.where(row == 6, 1.0, block))
        turned = jnp.concatenate([block, high, high, high, middle, middle, low, jnp.zeros_like(block)], 0).T
        columns[u * unit : (u + 1) * unit, :] = turned[:, 0:ROWS]
        left[u * unit : (u + 1) * unit, :] = turned.astype(BF16)
    for k in places:
        sums[k] = jnp.zeros((ROWS, count), F32)

    def fill(u, chunk, slot):
        wide, proj = slot
        source = pl.multiple_of(u * unit + chunk * part, part)
        target = pl.multiple_of(chunk * part, part)
        proj[pl.ds(target, part), :] = jnp.dot(left[pl.ds(source, part), :], right[...], preferred_element_type=F32)
        for k in range(7) if gradient or u == units else (0, 1, 2, 6):
            for g in range(part // ROWS):
                group = columns[pl.ds(pl.multiple_of(source + g * ROWS, ROWS), ROWS), :]
                wide[k, pl.ds(pl.multiple_of(target + g * ROWS, ROWS), ROWS), :] = jnp.broadcast_to(
                    group[:, k : k + 1], (ROWS, LANES)
                )

    together = GRADIENT_CHUNKS if gradient else chunks
    never = lax.axis_index("blk") < 0

    def work(chunk, slot, following, is_last):
        wide, proj = slot
        at_lane = pl.multiple_of(chunk * LANES, LANES)
        span = pl.ds(at_lane, LANES)
        a = [jnp.broadcast_to(own[k : k + 1, span], (ROWS, LANES)) for k in range(3)]
        s = {k: sums[k, :, span] for k in places}
        for g in range(unit // ROWS):
            if is_last and g == unit // ROWS - 1:
                stored = pl.ds(pl.multiple_of(chunk * part, ROWS), ROWS)
                seen = following[0][6, stored, :] + following[1][stored, 0:LANES]
                s[places[-1]] += jnp.where(never, seen, 0.0)
            rows = slice(g * ROWS, (g + 1) * ROWS)
            b = {k: wide[k, rows, :] for k in (range(7) if gradient else (0, 1, 2, 6))}
            proj_a = proj[rows, span]
            proj_b = proj[rows, pl.ds(pl.multiple_of(count + at_lane, LANES), LANES)]
            d0, d1, d2 = a[0] - b[0], a[1] - b[1], a[2] - b[2]
            dist = d0 * d0 + d1 * d1 + (d2 * d2 + EPS2)
            inverse = 1.0 / dist
            square = inverse * inverse * b[6]
            if not gradient:
                s[SUMS] += (proj_a * proj_a + proj_b * proj_b) * square
                continue
            alpha = proj_a * square
            beta = proj_b * square
            kernel = proj_a * alpha + proj_b * beta
            gamma = kernel * inverse
            s[0] += beta * b[3]
            s[1] += beta * b[4]
            s[2] += beta * b[5]
            s[3] += alpha * d0
            s[4] += alpha * d1
            s[5] += alpha * d2
            s[6] += alpha
            s[7] += gamma * d0
            s[8] += gamma * d1
            s[9] += gamma * d2
            if factor:
                s[SUMS] += kernel
        for k in places:
            sums[k, :, span] = s[k]

    def over_chunks(now, u, slot):
        def step(index, carried):
            for k in range(together):
                fill(u, index * together + k, slot)
            for k in range(together):
                work(index * together + k, now, slot, k == together - 1)
            return carried

        if together == chunks:
            step(0, 0)
        else:
            lax.fori_loop(0, chunks // together, step, 0)

    if not lead:
        for chunk in range(chunks):
            fill(0, chunk, slots[0])
    for u in range(units):
        over_chunks(led if lead and u == 0 else slots[u % 2], min(u + 1, len(plan) - 1), slots[(u + 1) % 2])
    if gradient:
        for k in range(SUMS):
            line = jnp.sum(sums[k], axis=0, keepdims=True)
            out[k : k + 1, :] = line + total[k : k + 1, :] if carry else line
    if factor:
        weighted = sums[SUMS] * (factor * own[6:7, :])
        part_share = weighted[:, 0:LANES]
        for chunk in range(1, chunks):
            part_share = part_share + weighted[:, chunk * LANES : (chunk + 1) * LANES]
        share[...] = part_share + share_in[...] if carry else part_share


def tiles(times, own, arrays, plan, factor, gradient, state, trail, blocks):
    count = own.shape[1]
    unit = count // 2
    total, share, right, led = state
    first, carry, lead = right is None, total is not None, led is not None
    number = len(plan) - (1 if trail else 0)
    body = functools.partial(tiles_kernel, plan, blocks, factor, gradient, first, carry, lead, trail)
    operands = [own, *arrays] + ([times] if any(item[2] == "grp" for item in plan) else [])
    operands += ([] if first else [right]) + ([total] if carry and gradient else [])
    operands += ([share] if carry and factor else []) + (list(led) if lead else [])
    slot = [((7, unit, LANES), F32), ((unit, 2 * count), F32)]
    shapes = [jax.ShapeDtypeStruct((SUMS, count), F32)] if gradient else []
    if factor:
        shapes.append(jax.ShapeDtypeStruct((ROWS, LANES), F32))
    if first:
        shapes.append(jax.ShapeDtypeStruct((DEPTH, 2 * count), BF16))
    if trail:
        shapes += [jax.ShapeDtypeStruct(*each) for each in slot]
    pairs = number * unit * count
    result = list(
        pl.pallas_call(
            body,
            out_shape=shapes,
            in_specs=[VMEM] * len(operands),
            out_specs=[VMEM] * len(shapes),
            scratch_shapes=[
                pltpu.VMEM((len(plan) * unit, ROWS), F32),
                pltpu.VMEM((len(plan) * unit, DEPTH), BF16),
                pltpu.VMEM((SUMS + 1, ROWS, count), F32),
                *[pltpu.VMEM(*each) for each in slot],
                *([] if trail else [pltpu.VMEM(*each) for each in slot]),
            ],
            compiler_params=PARAMS,
            cost_estimate=pl.CostEstimate(
                flops=FLOPS_PER_PAIR * pairs, bytes_accessed=32 * unit * number, transcendentals=pairs
            ),
        )(*operands)
    )
    total = result.pop(0) if gradient else total
    share = result.pop(0) if factor else share
    right = result.pop(0) if first else right
    return total, share, right, (tuple(result) if trail else None)


def finish_kernel(own, edges, sums, faces, grad):
    verts = grad.shape[1]
    count = own.shape[1]
    twice = 2.0 * own[6:7, :]
    total = sums[6:7, :]
    g_center = [
        twice * (own[3 + c : 4 + c, :] * total + sums[c : c + 1, :] - 2.0 * sums[7 + c : 8 + c, :]) for c in range(3)
    ]
    g_area = [twice * sums[3 + c : 4 + c, :] for c in range(3)]
    e1 = [edges[c : c + 1, :] for c in range(3)]
    e2 = [edges[3 + c : 4 + c, :] for c in range(3)]
    zero = jnp.zeros((ROWS - 3, count), F32)
    corners = [[], [], []]
    for c in range(3):
        n, m = (c + 1) % 3, (c + 2) % 3
        g1 = 0.5 * (e2[n] * g_area[m] - e2[m] * g_area[n])
        g2 = 0.5 * (g_area[n] * e1[m] - g_area[m] * e1[n])
        part = g_center[c] / 3.0
        corners[0].append(part - g1 - g2)
        corners[1].append(part + g1)
        corners[2].append(part + g2)
    total = jnp.zeros((3 * ROWS, verts), F32)
    for k in range(3):
        left = jnp.concatenate(pieces(jnp.concatenate(corners[k] + [zero], 0)), 0).astype(BF16)
        total += lax.dot_general(
            left, one_hot(faces[k : k + 1, :], verts), (((1,), (1,)), ((), ())), preferred_element_type=F32
        )
    total = total[0:ROWS] + total[ROWS : 2 * ROWS] + total[2 * ROWS : 3 * ROWS]
    grad[...] = total[0:3] / count


def gather(own, axis, size, wanted):
    if size & (size - 1) == 0 and len(wanted) == size - 1:
        found = {}
        held = own[None]
        mask = size // 2
        while mask:
            other = flip(held, axis, mask)
            for offset in wanted:
                if offset & -offset == mask:
                    found[offset] = (other, "ring")
            held = jnp.concatenate([held, other], 0) if mask > 1 else held
            mask //= 2
        return found
    return {offset: (from_ahead(own, axis, offset), None) for offset in wanted}


def shards(vertices, faces, trial_step, accepted, face_weight, partner_shift):
    count = faces.shape[1]
    verts = vertices.shape[1]
    groups, blocks = lax.axis_size("grp"), lax.axis_size("blk")
    block_shape = jax.ShapeDtypeStruct((ROWS, count), F32)
    arguments = (accepted, partner_shift, vertices, trial_step, faces, face_weight)
    homes = [pltpu.SMEM] * 2 + [pltpu.VMEM] * 4
    met_shape = jax.ShapeDtypeStruct((-(-groups // ROWS) * ROWS, LANES), F32)
    sent, own, edges, times = pl.pallas_call(
        functools.partial(geometry_kernel, groups),
        out_shape=(block_shape, block_shape, block_shape, met_shape),
        in_specs=[pl.BlockSpec(memory_space=pltpu.HBM)] * 6,
        out_specs=(VMEM,) * 4,
        scratch_shapes=[home(a.shape, a.dtype) for home, a in zip(homes, arguments)]
        + [pltpu.VMEM((ROWS, verts), F32), pltpu.SemaphoreType.DMA((6,))],
    )(*arguments)

    window = [o for o in range(1, blocks) if window_times(o, blocks)]
    ring = gather(sent, "blk", blocks, window)
    across = gather(sent, "grp", groups, list(range(1, groups)))

    def halves(items):
        return [(axis, offset, half) for axis, offset in items for half in range(2)]

    def visit(parts, factor, gradient, state, following):
        arrays, plan = [], []
        for axis, offset, half in parts + following:
            if axis == "self":
                array, index = own, None
            else:
                array, index = (ring if axis == "blk" else across)[offset]
            where = [i for i, known in enumerate(arrays) if known is array]
            if not where:
                arrays.append(array)
                where = [len(arrays) - 1]
            plan.append((where[0], index, axis, offset, half))
        return tiles(times, own, arrays, tuple(plan), factor, gradient, state, len(following) > 0, blocks)

    def stage(offset, size):
        return -(offset & -offset) if size & (size - 1) == 0 else 0

    middle = [("blk", o) for o in window if 2 * o == blocks] + [("grp", o) for o in range(1, groups) if 2 * o == groups]
    early_blk = sorted((o for o in window if 2 * o < blocks), key=lambda o: (stage(o, blocks), o))
    early_grp = [("grp", o) for o in range(1, groups) if 2 * o < groups]
    late = [("grp", o) for o in range(1, groups) if 2 * o > groups]
    late += [("blk", o) for o in sorted((o for o in window if 2 * o > blocks), key=lambda o: (stage(o, blocks), o))]
    first = early_grp
    second = [("blk", o) for o in early_blk]

    state = visit(halves([("self", 0)]), 0.5, True, (None, None, None, None), [])
    for items, factor in ((middle, 0.5), (first, 1.0)):
        if items:
            state = visit(halves(items), factor, True, state, [])
    late = halves(late + second)
    if second:
        state = visit(halves(second), 1.0, False, state, late[:1])
    share = state[1]
    rounds = []
    for axis, size in (("blk", blocks), ("grp", groups)):
        if size & (size - 1) == 0:
            rounds += [(axis, size >> k) for k in range(1, size.bit_length())]
        else:
            rounds.append((axis, 0))

    def exchange(value, axis, mask):
        if mask:
            return flip(value, axis, mask)
        return sum(from_ahead(value, axis, o) for o in range(1, lax.axis_size(axis)))

    def last_of(total):
        return pl.pallas_call(
            finish_kernel,
            out_shape=jax.ShapeDtypeStruct((3, verts), F32),
            in_specs=[VMEM] * 4,
            out_specs=VMEM,
            compiler_params=PARAMS,
            cost_estimate=pl.CostEstimate(flops=1500000000, bytes_accessed=64 * count, transcendentals=0),
        )(own, edges, total, faces)

    covers = max(1, len(rounds) - 1)
    edges_of = [len(late) * i // covers for i in range(covers + 1)]
    for index in range(max(covers, len(rounds))):
        received = None
        if index < len(rounds):
            received = exchange(share, *rounds[index])
        if index < covers:
            begin, end = edges_of[index], edges_of[index + 1]
            if end > begin:
                state = visit(late[begin:end], 0.0, True, state, late[end : end + 1])
            done = state
        if index == len(rounds) - 1:
            grad = last_of(state[0])
            done = grad
        if received is not None:
            if index < len(rounds) - 1:
                state, received = lax.optimization_barrier((done, received))
            share = share + received
    if not rounds:
        grad = last_of(state[0])
    energy = jnp.sum(share) / (count * count * groups * blocks)
    return grad, energy.reshape(1)


def solution(mesh):
    placed = (
        P(None, ("grp", "blk")),
        P(None, ("grp", "blk")),
        P(None, ("grp", "blk")),
        P("grp"),
        P(("grp", "blk")),
        P(),
    )
    return jax.shard_map(
        shards,
        mesh=mesh,
        in_specs=placed,
        out_specs=(P(None, ("grp", "blk")), P()),
        check_vma=False,
    )
```

```python
import functools

import jax
import jax.numpy as jnp
from jax import lax
from jax.experimental import pallas as pl
from jax.experimental.pallas import tpu as pltpu
from jax.sharding import PartitionSpec as P

HOPS = 4
EPS2 = 0.05
ROWS = 8
LANES = 128
DEPTH = 64
SUMS = 10
F32 = jnp.float32
BF16 = jnp.bfloat16
VMEM = pl.BlockSpec(memory_space=pltpu.VMEM)
SMEM = pl.BlockSpec(memory_space=pltpu.SMEM)
FLOPS_PER_PAIR = 8000
GRADIENT_CHUNKS = 1
PARAMS = pltpu.CompilerParams(vmem_limit_bytes=16 * 1024 * 1024)


def flip(value, axis, mask):
    count = lax.axis_size(axis)
    return lax.ppermute(value, axis, [(i, i ^ mask) for i in range(count)])


def from_ahead(value, axis, by):
    count = lax.axis_size(axis)
    return lax.ppermute(value, axis, [(i, (i - by) % count) for i in range(count)])


def pieces(value):
    high = value.astype(BF16).astype(F32)
    rest = value - high
    middle = rest.astype(BF16).astype(F32)
    return high, middle, rest - middle


def one_hot(row, count):
    rows = lax.broadcasted_iota(jnp.int32, (count, row.shape[1]), 0)
    return jnp.where(rows == row, 1.0, 0.0).astype(BF16)


def partner_times(shift, here, there, groups):
    times = jnp.int32(0)
    for r in range(shift.shape[0]):
        times += (lax.rem(here + shift[r, here], groups) == there).astype(jnp.int32)
        times += (lax.rem(there + shift[r, there], groups) == here).astype(jnp.int32)
    return times


def geometry_kernel(groups, *refs):
    far, (sent, own, edges, times), near, (padded, arrived) = refs[:6], refs[6:10], refs[10:16], refs[16:]
    accepted, shift, vertices, trial_step, faces, weight = near
    copies = [pltpu.make_async_copy(far[i], near[i], arrived.at[i]) for i in range(6)]
    for copy in copies:
        copy.start()
    verts = vertices.shape[1]
    count = faces.shape[1]
    padded[...] = jnp.zeros_like(padded)
    for copy in copies:
        copy.wait()
    here = lax.axis_index("grp")
    times[...] = jnp.zeros_like(times)
    for offset in range(1, groups):
        met = partner_times(shift, here, lax.rem(here + offset, groups), groups).astype(F32)
        times[offset : offset + 1, :] = jnp.zeros((1, LANES), F32) + met
    padded[0:3, :] = vertices[...] + accepted[0].astype(F32) * trial_step[...]
    left = jnp.concatenate(pieces(padded[...]), 0).astype(BF16)

    def corner(k):
        picked = jnp.dot(left, one_hot(faces[k : k + 1, :], verts), preferred_element_type=F32)
        picked = picked[0:ROWS] + picked[ROWS : 2 * ROWS] + picked[2 * ROWS : 3 * ROWS]
        return [picked[c : c + 1] for c in range(3)]

    first, second, third = corner(0), corner(1), corner(2)
    center = [(first[c] + second[c] + third[c]) / 3.0 for c in range(3)]
    e1 = [second[c] - first[c] for c in range(3)]
    e2 = [third[c] - first[c] for c in range(3)]
    area = []
    for c in range(3):
        n, m = (c + 1) % 3, (c + 2) % 3
        area.append(0.5 * (e1[n] * e2[m] - e1[m] * e2[n]))
    for c in range(3):
        own[c : c + 1, :] = center[c]
        own[3 + c : 4 + c, :] = area[c]
        edges[c : c + 1, :] = e1[c]
        edges[3 + c : 4 + c, :] = e2[c]
    own[6:7, :] = weight[...].reshape(1, count)
    own[7:8, :] = center[0] * area[0] + center[1] * area[1] + center[2] * area[2]
    edges[6:8, :] = jnp.zeros((2, count), F32)
    sent[...] = own[...]


def window_times(offset, blocks):
    return sum(int((k - offset) % blocks == 0) + int((k + offset) % blocks == 0) for k in range(1, HOPS + 1))


def place_of(mask, size):
    place, step, bit = 0, 1, size // 2
    while bit:
        place = place + jnp.bitwise_and(mask // bit, 1) * step
        step, bit = step * 2, bit // 2
    return place


def tiles_kernel(plan, blocks, factor, gradient, first, carry, lead, trail, *refs):
    refs = list(refs)
    own = refs.pop(0)
    count = own.shape[1]
    unit = count // 2
    chunks = count // LANES
    part = unit // chunks
    others = [refs.pop(0) for _ in range(1 + max(item[0] for item in plan))]
    met = refs.pop(0) if any(item[2] == "grp" for item in plan) else None
    right = None if first else refs.pop(0)
    total = refs.pop(0) if carry and gradient else None
    share_in = refs.pop(0) if carry and factor else None
    led = (refs.pop(0), refs.pop(0)) if lead else None
    out = refs.pop(0) if gradient else None
    share = refs.pop(0) if factor else None
    right = refs.pop(0) if first else right
    units = len(plan) - (1 if trail else 0)
    slots = [None, None]
    if trail:
        slots[units % 2] = (refs.pop(0), refs.pop(0))
    columns, left, sums = refs[:3]
    refs = refs[3:]
    for side in range(2):
        if slots[side] is None:
            slots[side] = (refs.pop(0), refs.pop(0))
    places = (list(range(SUMS)) if gradient else []) + ([SUMS] if factor else [])

    if first:
        zero = jnp.zeros((ROWS, count), F32)
        zero1, zero3 = jnp.zeros((1, count), F32), jnp.zeros((3, count), F32)
        from_own = jnp.concatenate([-own[3:6, :], zero3, own[7:8, :], zero1], 0)
        from_other = jnp.concatenate([zero3, own[0:3, :], zero1, zero1 - 1.0], 0)
        for side, rows in enumerate((from_own, from_other)):
            high, middle, low = pieces(rows)
            right[:, side * count : (side + 1) * count] = jnp.concatenate(
                [zero, high, middle, low, high, middle, high, zero], 0
            ).astype(BF16)
    row = lax.broadcasted_iota(jnp.int32, (ROWS, unit), 0)
    for u, (source, index, axis, offset, half) in enumerate(plan):
        if lead and u == 0:
            continue
        if index == "ring":
            size = lax.axis_size(axis)
            here = lax.axis_index(axis)
            there = lax.rem(here + offset, size)
            block = others[source][place_of(jnp.bitwise_xor(here, there), size) - size // 2 // (offset & -offset)]
        elif index is None:
            block = others[source][...]
        else:
            block = others[source][index]
        block = block[:, half * unit : (half + 1) * unit]
        if axis == "self":
            times = 1.0 + window_times(0, blocks)
        elif axis == "blk":
            times = float(window_times(offset, blocks))
        else:
            times = jnp.concatenate([met[offset : offset + 1, :]] * (unit // LANES), 1)
        block = jnp.where(row == 6, block * times, block)
        high, middle, low = pieces(jnp.where(row == 6, 1.0, block))
        turned = jnp.concatenate([block, high, high, high, middle, middle, low, jnp.zeros_like(block)], 0).T
        columns[u * unit : (u + 1) * unit, :] = turned[:, 0:ROWS]
        left[u * unit : (u + 1) * unit, :] = turned.astype(BF16)
    for k in places:
        sums[k] = jnp.zeros((ROWS, count), F32)

    def fill(u, chunk, slot):
        wide, proj = slot
        source = pl.multiple_of(u * unit + chunk * part, part)
        target = pl.multiple_of(chunk * part, part)
        proj[pl.ds(target, part), :] = jnp.dot(left[pl.ds(source, part), :], right[...], preferred_element_type=F32)
        for k in range(7) if gradient or u == units else (0, 1, 2, 6):
            for g in range(part // ROWS):
                group = columns[pl.ds(pl.multiple_of(source + g * ROWS, ROWS), ROWS), :]
                wide[k, pl.ds(pl.multiple_of(target + g * ROWS, ROWS), ROWS), :] = jnp.broadcast_to(
                    group[:, k : k + 1], (ROWS, LANES)
                )

    together = GRADIENT_CHUNKS if gradient else chunks
    never = lax.axis_index("blk") < 0

    def work(chunk, slot, following, is_last):
        wide, proj = slot
        at_lane = pl.multiple_of(chunk * LANES, LANES)
        span = pl.ds(at_lane, LANES)
        a = [jnp.broadcast_to(own[k : k + 1, span], (ROWS, LANES)) for k in range(3)]
        s = {k: sums[k, :, span] for k in places}
        for g in range(unit // ROWS):
            if is_last and g == unit // ROWS - 1:
                stored = pl.ds(pl.multiple_of(chunk * part, ROWS), ROWS)
                seen = following[0][6, stored, :] + following[1][stored, 0:LANES]
                s[places[-1]] += jnp.where(never, seen, 0.0)
            rows = slice(g * ROWS, (g + 1) * ROWS)
            b = {k: wide[k, rows, :] for k in (range(7) if gradient else (0, 1, 2, 6))}
            proj_a = proj[rows, span]
            proj_b = proj[rows, pl.ds(pl.multiple_of(count + at_lane, LANES), LANES)]
            d0, d1, d2 = a[0] - b[0], a[1] - b[1], a[2] - b[2]
            dist = d0 * d0 + d1 * d1 + (d2 * d2 + EPS2)
            inverse = 1.0 / dist
            square = inverse * inverse * b[6]
            if not gradient:
                s[SUMS] += (proj_a * proj_a + proj_b * proj_b) * square
                continue
            alpha = proj_a * square
            beta = proj_b * square
            kernel = proj_a * alpha + proj_b * beta
            gamma = kernel * inverse
            s[0] += beta * b[3]
            s[1] += beta * b[4]
            s[2] += beta * b[5]
            s[3] += alpha * d0
            s[4] += alpha * d1
            s[5] += alpha * d2
            s[6] += alpha
            s[7] += gamma * d0
            s[8] += gamma * d1
            s[9] += gamma * d2
            if factor:
                s[SUMS] += kernel
        for k in places:
            sums[k, :, span] = s[k]

    def over_chunks(now, u, slot):
        def step(index, carried):
            for k in range(together):
                fill(u, index * together + k, slot)
            for k in range(together):
                work(index * together + k, now, slot, k == together - 1)
            return carried

        if together == chunks:
            step(0, 0)
        else:
            lax.fori_loop(0, chunks // together, step, 0)

    if not lead:
        for chunk in range(chunks):
            fill(0, chunk, slots[0])
    for u in range(units):
        over_chunks(led if lead and u == 0 else slots[u % 2], min(u + 1, len(plan) - 1), slots[(u + 1) % 2])
    if gradient:
        for k in range(SUMS):
            line = jnp.sum(sums[k], axis=0, keepdims=True)
            out[k : k + 1, :] = line + total[k : k + 1, :] if carry else line
    if factor:
        weighted = sums[SUMS] * (factor * own[6:7, :])
        part_share = weighted[:, 0:LANES]
        for chunk in range(1, chunks):
            part_share = part_share + weighted[:, chunk * LANES : (chunk + 1) * LANES]
        share[...] = part_share + share_in[...] if carry else part_share


def tiles(times, own, arrays, plan, factor, gradient, state, trail, blocks):
    count = own.shape[1]
    unit = count // 2
    total, share, right, led = state
    first, carry, lead = right is None, total is not None, led is not None
    number = len(plan) - (1 if trail else 0)
    body = functools.partial(tiles_kernel, plan, blocks, factor, gradient, first, carry, lead, trail)
    operands = [own, *arrays] + ([times] if any(item[2] == "grp" for item in plan) else [])
    operands += ([] if first else [right]) + ([total] if carry and gradient else [])
    operands += ([share] if carry and factor else []) + (list(led) if lead else [])
    slot = [((7, unit, LANES), F32), ((unit, 2 * count), F32)]
    shapes = [jax.ShapeDtypeStruct((SUMS, count), F32)] if gradient else []
    if factor:
        shapes.append(jax.ShapeDtypeStruct((ROWS, LANES), F32))
    if first:
        shapes.append(jax.ShapeDtypeStruct((DEPTH, 2 * count), BF16))
    if trail:
        shapes += [jax.ShapeDtypeStruct(*each) for each in slot]
    pairs = number * unit * count
    result = list(
        pl.pallas_call(
            body,
            out_shape=shapes,
            in_specs=[VMEM] * len(operands),
            out_specs=[VMEM] * len(shapes),
            scratch_shapes=[
                pltpu.VMEM((len(plan) * unit, ROWS), F32),
                pltpu.VMEM((len(plan) * unit, DEPTH), BF16),
                pltpu.VMEM((SUMS + 1, ROWS, count), F32),
                *[pltpu.VMEM(*each) for each in slot],
                *([] if trail else [pltpu.VMEM(*each) for each in slot]),
            ],
            compiler_params=PARAMS,
            cost_estimate=pl.CostEstimate(
                flops=FLOPS_PER_PAIR * pairs, bytes_accessed=32 * unit * number, transcendentals=pairs
            ),
        )(*operands)
    )
    total = result.pop(0) if gradient else total
    share = result.pop(0) if factor else share
    right = result.pop(0) if first else right
    return total, share, right, (tuple(result) if trail else None)


def finish_kernel(own, edges, sums, faces, grad):
    verts = grad.shape[1]
    count = own.shape[1]
    twice = 2.0 * own[6:7, :]
    total = sums[6:7, :]
    g_center = [
        twice * (own[3 + c : 4 + c, :] * total + sums[c : c + 1, :] - 2.0 * sums[7 + c : 8 + c, :]) for c in range(3)
    ]
    g_area = [twice * sums[3 + c : 4 + c, :] for c in range(3)]
    e1 = [edges[c : c + 1, :] for c in range(3)]
    e2 = [edges[3 + c : 4 + c, :] for c in range(3)]
    zero = jnp.zeros((ROWS - 3, count), F32)
    corners = [[], [], []]
    for c in range(3):
        n, m = (c + 1) % 3, (c + 2) % 3
        g1 = 0.5 * (e2[n] * g_area[m] - e2[m] * g_area[n])
        g2 = 0.5 * (g_area[n] * e1[m] - g_area[m] * e1[n])
        part = g_center[c] / 3.0
        corners[0].append(part - g1 - g2)
        corners[1].append(part + g1)
        corners[2].append(part + g2)
    total = jnp.zeros((3 * ROWS, verts), F32)
    for k in range(3):
        left = jnp.concatenate(pieces(jnp.concatenate(corners[k] + [zero], 0)), 0).astype(BF16)
        total += lax.dot_general(
            left, one_hot(faces[k : k + 1, :], verts), (((1,), (1,)), ((), ())), preferred_element_type=F32
        )
    total = total[0:ROWS] + total[ROWS : 2 * ROWS] + total[2 * ROWS : 3 * ROWS]
    grad[...] = total[0:3] / count


def gather(own, axis, size, wanted):
    if size & (size - 1) == 0 and len(wanted) == size - 1:
        found = {}
        held = own[None]
        mask = size // 2
        while mask:
            other = flip(held, axis, mask)
            for offset in wanted:
                if offset & -offset == mask:
                    found[offset] = (other, "ring")
            held = jnp.concatenate([held, other], 0) if mask > 1 else held
            mask //= 2
        return found
    return {offset: (from_ahead(own, axis, offset), None) for offset in wanted}


def shards(vertices, faces, trial_step, accepted, face_weight, partner_shift):
    count = faces.shape[1]
    verts = vertices.shape[1]
    groups, blocks = lax.axis_size("grp"), lax.axis_size("blk")
    block_shape = jax.ShapeDtypeStruct((ROWS, count), F32)
    arguments = (accepted, partner_shift, vertices, trial_step, faces, face_weight)
    arguments = arguments[:1] + tuple(pltpu.with_memory_space_constraint(each, pltpu.HBM) for each in arguments[1:])
    homes = [pltpu.SMEM] * 2 + [pltpu.VMEM] * 4
    met_shape = jax.ShapeDtypeStruct((-(-groups // ROWS) * ROWS, LANES), F32)
    sent, own, edges, times = pl.pallas_call(
        functools.partial(geometry_kernel, groups),
        out_shape=(block_shape, block_shape, block_shape, met_shape),
        in_specs=[pl.BlockSpec(memory_space=pltpu.HBM)] * 6,
        out_specs=(VMEM,) * 4,
        scratch_shapes=[home(a.shape, a.dtype) for home, a in zip(homes, arguments)]
        + [pltpu.VMEM((ROWS, verts), F32), pltpu.SemaphoreType.DMA((6,))],
        compiler_params=PARAMS,
    )(*arguments)

    window = [o for o in range(1, blocks) if window_times(o, blocks)]
    ring = gather(sent, "blk", blocks, window)
    across = gather(sent, "grp", groups, list(range(1, groups)))

    def halves(items):
        return [(axis, offset, half) for axis, offset in items for half in range(2)]

    def visit(parts, factor, gradient, state, following):
        arrays, plan = [], []
        for axis, offset, half in parts + following:
            if axis == "self":
                array, index = own, None
            else:
                array, index = (ring if axis == "blk" else across)[offset]
            where = [i for i, known in enumerate(arrays) if known is array]
            if not where:
                arrays.append(array)
                where = [len(arrays) - 1]
            plan.append((where[0], index, axis, offset, half))
        return tiles(times, own, arrays, tuple(plan), factor, gradient, state, len(following) > 0, blocks)

    def stage(offset, size):
        return -(offset & -offset) if size & (size - 1) == 0 else 0

    middle = [("blk", o) for o in window if 2 * o == blocks] + [("grp", o) for o in range(1, groups) if 2 * o == groups]
    early_blk = sorted((o for o in window if 2 * o < blocks), key=lambda o: (stage(o, blocks), o))
    early_grp = [("grp", o) for o in range(1, groups) if 2 * o < groups]
    late = [("grp", o) for o in range(1, groups) if 2 * o > groups]
    late += [("blk", o) for o in sorted((o for o in window if 2 * o > blocks), key=lambda o: (stage(o, blocks), o))]
    first = early_grp + [("blk", o) for o in early_blk[: len(early_blk) // 3]]
    second = [("blk", o) for o in early_blk[len(early_blk) // 3 :]]

    state = visit(halves([("self", 0)]), 0.5, True, (None, None, None, None), [])
    for items, factor in ((middle, 0.5), (first, 1.0)):
        if items:
            state = visit(halves(items), factor, True, state, [])
    late = halves(late + second)
    if second:
        state = visit(halves(second), 1.0, False, state, late[:1])
    share = state[1]
    rounds = []
    for axis, size in (("blk", blocks), ("grp", groups)):
        if size & (size - 1) == 0:
            rounds += [(axis, size >> k) for k in range(1, size.bit_length())]
        else:
            rounds.append((axis, 0))

    def exchange(value, axis, mask):
        if mask:
            return flip(value, axis, mask)
        return sum(from_ahead(value, axis, o) for o in range(1, lax.axis_size(axis)))

    def last_of(total):
        return pl.pallas_call(
            finish_kernel,
            out_shape=jax.ShapeDtypeStruct((3, verts), F32),
            in_specs=[VMEM] * 4,
            out_specs=VMEM,
            compiler_params=PARAMS,
            cost_estimate=pl.CostEstimate(flops=1500000000, bytes_accessed=64 * count, transcendentals=0),
        )(own, edges, total, faces)

    covers = max(1, len(rounds) - 1)
    edges_of = [len(late) * i // covers for i in range(covers + 1)]
    for index in range(max(covers, len(rounds))):
        received = None
        if index < len(rounds):
            received = exchange(share, *rounds[index])
        if index < covers:
            begin, end = edges_of[index], edges_of[index + 1]
            if end > begin:
                state = visit(late[begin:end], 0.0, True, state, late[end : end + 1])
            done = state
        if index == len(rounds) - 1:
            grad = last_of(state[0])
            done = grad
        if received is not None:
            if index < len(rounds) - 1:
                state, received = lax.optimization_barrier((done, received))
            share = share + received
    if not rounds:
        grad = last_of(state[0])
    energy = jnp.sum(share) / (count * count * groups * blocks)
    return grad, energy.reshape(1)


def solution(mesh):
    placed = (
        P(None, ("grp", "blk")),
        P(None, ("grp", "blk")),
        P(None, ("grp", "blk")),
        P("grp"),
        P(("grp", "blk")),
        P(),
    )
    return jax.shard_map(
        shards,
        mesh=mesh,
        in_specs=placed,
        out_specs=(P(None, ("grp", "blk")), P()),
        check_vma=False,
    )
```

```python
import functools

import jax
import jax.numpy as jnp
from jax import lax
from jax.experimental import pallas as pl
from jax.experimental.pallas import tpu as pltpu
from jax.sharding import PartitionSpec as P

HOPS = 4
EPS2 = 0.05
ROWS = 8
LANES = 128
DEPTH = 64
SUMS = 10
F32 = jnp.float32
BF16 = jnp.bfloat16
VMEM = pl.BlockSpec(memory_space=pltpu.VMEM)
SMEM = pl.BlockSpec(memory_space=pltpu.SMEM)
FLOPS_PER_PAIR = 8000
GRADIENT_CHUNKS = 1
PARAMS = pltpu.CompilerParams(vmem_limit_bytes=16 * 1024 * 1024)


def flip(value, axis, mask):
    count = lax.axis_size(axis)
    return lax.ppermute(value, axis, [(i, i ^ mask) for i in range(count)])


def from_ahead(value, axis, by):
    count = lax.axis_size(axis)
    return lax.ppermute(value, axis, [(i, (i - by) % count) for i in range(count)])


def pieces(value):
    high = value.astype(BF16).astype(F32)
    rest = value - high
    middle = rest.astype(BF16).astype(F32)
    return high, middle, rest - middle


def one_hot(row, count):
    rows = lax.broadcasted_iota(jnp.int32, (count, row.shape[1]), 0)
    return jnp.where(rows == row, 1.0, 0.0).astype(BF16)


def partner_times(shift, here, there, groups):
    times = jnp.int32(0)
    for r in range(shift.shape[0]):
        times += (lax.rem(here + shift[r, here], groups) == there).astype(jnp.int32)
        times += (lax.rem(there + shift[r, there], groups) == here).astype(jnp.int32)
    return times


def geometry_kernel(groups, *refs):
    far, (kept, own, edges, times), near, (padded, arrived) = refs[:6], refs[6:10], refs[10:16], refs[16:]
    accepted, shift, vertices, trial_step, faces, weight = near
    copies = [pltpu.make_async_copy(far[i], near[i], arrived.at[i]) for i in range(6)]
    for copy in copies:
        copy.start()
    verts = vertices.shape[1]
    count = faces.shape[1]
    padded[...] = jnp.zeros_like(padded)
    for copy in copies:
        copy.wait()
    here = lax.axis_index("grp")
    times[...] = jnp.zeros_like(times)
    for offset in range(1, groups):
        met = partner_times(shift, here, lax.rem(here + offset, groups), groups).astype(F32)
        times[offset : offset + 1, :] = jnp.zeros((1, LANES), F32) + met
    padded[0:3, :] = vertices[...] + accepted[0].astype(F32) * trial_step[...]
    left = jnp.concatenate(pieces(padded[...]), 0).astype(BF16)

    def corner(k):
        picked = jnp.dot(left, one_hot(faces[k : k + 1, :], verts), preferred_element_type=F32)
        picked = picked[0:ROWS] + picked[ROWS : 2 * ROWS] + picked[2 * ROWS : 3 * ROWS]
        return [picked[c : c + 1] for c in range(3)]

    first, second, third = corner(0), corner(1), corner(2)
    center = [(first[c] + second[c] + third[c]) / 3.0 for c in range(3)]
    e1 = [second[c] - first[c] for c in range(3)]
    e2 = [third[c] - first[c] for c in range(3)]
    area = []
    for c in range(3):
        n, m = (c + 1) % 3, (c + 2) % 3
        area.append(0.5 * (e1[n] * e2[m] - e1[m] * e2[n]))
    for c in range(3):
        own[c : c + 1, :] = center[c]
        own[3 + c : 4 + c, :] = area[c]
        edges[c : c + 1, :] = e1[c]
        edges[3 + c : 4 + c, :] = e2[c]
    own[6:7, :] = weight[...].reshape(1, count)
    own[7:8, :] = center[0] * area[0] + center[1] * area[1] + center[2] * area[2]
    edges[6:8, :] = jnp.zeros((2, count), F32)
    kept[...] = faces[...]


def window_times(offset, blocks):
    return sum(int((k - offset) % blocks == 0) + int((k + offset) % blocks == 0) for k in range(1, HOPS + 1))


def place_of(mask, size):
    place, step, bit = 0, 1, size // 2
    while bit:
        place = place + jnp.bitwise_and(mask // bit, 1) * step
        step, bit = step * 2, bit // 2
    return place


def tiles_kernel(plan, blocks, factor, gradient, first, carry, lead, trail, *refs):
    refs = list(refs)
    own = refs.pop(0)
    count = own.shape[1]
    unit = count // 2
    chunks = count // LANES
    part = unit // chunks
    others = [refs.pop(0) for _ in range(1 + max(item[0] for item in plan))]
    met = refs.pop(0) if any(item[2] == "grp" for item in plan) else None
    right = None if first else refs.pop(0)
    total = refs.pop(0) if carry and gradient else None
    share_in = refs.pop(0) if carry and factor else None
    led = (refs.pop(0), refs.pop(0)) if lead else None
    out = refs.pop(0) if gradient else None
    share = refs.pop(0) if factor else None
    right = refs.pop(0) if first else right
    units = len(plan) - (1 if trail else 0)
    slots = [None, None]
    if trail:
        slots[units % 2] = (refs.pop(0), refs.pop(0))
    columns, left, sums = refs[:3]
    refs = refs[3:]
    for side in range(2):
        if slots[side] is None:
            slots[side] = (refs.pop(0), refs.pop(0))
    places = (list(range(SUMS)) if gradient else []) + ([SUMS] if factor else [])

    if first:
        zero = jnp.zeros((ROWS, count), F32)
        zero1, zero3 = jnp.zeros((1, count), F32), jnp.zeros((3, count), F32)
        from_own = jnp.concatenate([-own[3:6, :], zero3, own[7:8, :], zero1], 0)
        from_other = jnp.concatenate([zero3, own[0:3, :], zero1, zero1 - 1.0], 0)
        for side, rows in enumerate((from_own, from_other)):
            high, middle, low = pieces(rows)
            right[:, side * count : (side + 1) * count] = jnp.concatenate(
                [zero, high, middle, low, high, middle, high, zero], 0
            ).astype(BF16)
    row = lax.broadcasted_iota(jnp.int32, (ROWS, unit), 0)
    for u, (source, index, axis, offset, half) in enumerate(plan):
        if lead and u == 0:
            continue
        if index == "ring":
            size = lax.axis_size(axis)
            here = lax.axis_index(axis)
            there = lax.rem(here + offset, size)
            block = others[source][place_of(jnp.bitwise_xor(here, there), size) - size // 2 // (offset & -offset)]
        elif index is None:
            block = others[source][...]
        else:
            block = others[source][index]
        block = block[:, half * unit : (half + 1) * unit]
        if axis == "self":
            times = 1.0 + window_times(0, blocks)
        elif axis == "blk":
            times = float(window_times(offset, blocks))
        else:
            times = jnp.concatenate([met[offset : offset + 1, :]] * (unit // LANES), 1)
        block = jnp.where(row == 6, block * times, block)
        high, middle, low = pieces(jnp.where(row == 6, 1.0, block))
        turned = jnp.concatenate([block, high, high, high, middle, middle, low, jnp.zeros_like(block)], 0).T
        columns[u * unit : (u + 1) * unit, :] = turned[:, 0:ROWS]
        left[u * unit : (u + 1) * unit, :] = turned.astype(BF16)
    for k in places:
        sums[k] = jnp.zeros((ROWS, count), F32)

    def fill(u, chunk, slot):
        wide, proj = slot
        source = pl.multiple_of(u * unit + chunk * part, part)
        target = pl.multiple_of(chunk * part, part)
        proj[pl.ds(target, part), :] = jnp.dot(left[pl.ds(source, part), :], right[...], preferred_element_type=F32)
        for k in range(7) if gradient or u == units else (0, 1, 2, 6):
            for g in range(part // ROWS):
                group = columns[pl.ds(pl.multiple_of(source + g * ROWS, ROWS), ROWS), :]
                wide[k, pl.ds(pl.multiple_of(target + g * ROWS, ROWS), ROWS), :] = jnp.broadcast_to(
                    group[:, k : k + 1], (ROWS, LANES)
                )

    together = GRADIENT_CHUNKS if gradient else chunks
    never = lax.axis_index("blk") < 0

    def work(chunk, slot, following, is_last):
        wide, proj = slot
        at_lane = pl.multiple_of(chunk * LANES, LANES)
        span = pl.ds(at_lane, LANES)
        a = [jnp.broadcast_to(own[k : k + 1, span], (ROWS, LANES)) for k in range(3)]
        s = {k: sums[k, :, span] for k in places}
        for g in range(unit // ROWS):
            if is_last and g == unit // ROWS - 1:
                stored = pl.ds(pl.multiple_of(chunk * part, ROWS), ROWS)
                seen = following[0][6, stored, :] + following[1][stored, 0:LANES]
                s[places[-1]] += jnp.where(never, seen, 0.0)
            rows = slice(g * ROWS, (g + 1) * ROWS)
            b = {k: wide[k, rows, :] for k in (range(7) if gradient else (0, 1, 2, 6))}
            proj_a = proj[rows, span]
            proj_b = proj[rows, pl.ds(pl.multiple_of(count + at_lane, LANES), LANES)]
            d0, d1, d2 = a[0] - b[0], a[1] - b[1], a[2] - b[2]
            dist = d0 * d0 + d1 * d1 + (d2 * d2 + EPS2)
            inverse = 1.0 / dist
            square = inverse * inverse * b[6]
            if not gradient:
                s[SUMS] += (proj_a * proj_a + proj_b * proj_b) * square
                continue
            alpha = proj_a * square
            beta = proj_b * square
            kernel = proj_a * alpha + proj_b * beta
            gamma = kernel * inverse
            s[0] += beta * b[3]
            s[1] += beta * b[4]
            s[2] += beta * b[5]
            s[3] += alpha * d0
            s[4] += alpha * d1
            s[5] += alpha * d2
            s[6] += alpha
            s[7] += gamma * d0
            s[8] += gamma * d1
            s[9] += gamma * d2
            if factor:
                s[SUMS] += kernel
        for k in places:
            sums[k, :, span] = s[k]

    def over_chunks(now, u, slot):
        def step(index, carried):
            for k in range(together):
                fill(u, index * together + k, slot)
            for k in range(together):
                work(index * together + k, now, slot, k == together - 1)
            return carried

        if together == chunks:
            step(0, 0)
        else:
            lax.fori_loop(0, chunks // together, step, 0)

    if not lead:
        for chunk in range(chunks):
            fill(0, chunk, slots[0])
    for u in range(units):
        over_chunks(led if lead and u == 0 else slots[u % 2], min(u + 1, len(plan) - 1), slots[(u + 1) % 2])
    if gradient:
        for k in range(SUMS):
            line = jnp.sum(sums[k], axis=0, keepdims=True)
            out[k : k + 1, :] = line + total[k : k + 1, :] if carry else line
    if factor:
        weighted = sums[SUMS] * (factor * own[6:7, :])
        part_share = weighted[:, 0:LANES]
        for chunk in range(1, chunks):
            part_share = part_share + weighted[:, chunk * LANES : (chunk + 1) * LANES]
        share[...] = part_share + share_in[...] if carry else part_share


def tiles(times, own, arrays, plan, factor, gradient, state, trail, blocks):
    count = own.shape[1]
    unit = count // 2
    total, share, right, led = state
    first, carry, lead = right is None, total is not None, led is not None
    number = len(plan) - (1 if trail else 0)
    body = functools.partial(tiles_kernel, plan, blocks, factor, gradient, first, carry, lead, trail)
    operands = [own, *arrays] + ([times] if any(item[2] == "grp" for item in plan) else [])
    operands += ([] if first else [right]) + ([total] if carry and gradient else [])
    operands += ([share] if carry and factor else []) + (list(led) if lead else [])
    slot = [((7, unit, LANES), F32), ((unit, 2 * count), F32)]
    shapes = [jax.ShapeDtypeStruct((SUMS, count), F32)] if gradient else []
    if factor:
        shapes.append(jax.ShapeDtypeStruct((ROWS, LANES), F32))
    if first:
        shapes.append(jax.ShapeDtypeStruct((DEPTH, 2 * count), BF16))
    if trail:
        shapes += [jax.ShapeDtypeStruct(*each) for each in slot]
    pairs = number * unit * count
    result = list(
        pl.pallas_call(
            body,
            out_shape=shapes,
            in_specs=[VMEM] * len(operands),
            out_specs=[VMEM] * len(shapes),
            scratch_shapes=[
                pltpu.VMEM((len(plan) * unit, ROWS), F32),
                pltpu.VMEM((len(plan) * unit, DEPTH), BF16),
                pltpu.VMEM((SUMS + 1, ROWS, count), F32),
                *[pltpu.VMEM(*each) for each in slot],
                *([] if trail else [pltpu.VMEM(*each) for each in slot]),
            ],
            compiler_params=PARAMS,
            cost_estimate=pl.CostEstimate(
                flops=FLOPS_PER_PAIR * pairs, bytes_accessed=32 * unit * number, transcendentals=pairs
            ),
        )(*operands)
    )
    total = result.pop(0) if gradient else total
    share = result.pop(0) if factor else share
    right = result.pop(0) if first else right
    return total, share, right, (tuple(result) if trail else None)


def finish_kernel(own, edges, sums, faces, grad):
    verts = grad.shape[1]
    count = own.shape[1]
    twice = 2.0 * own[6:7, :]
    total = sums[6:7, :]
    g_center = [
        twice * (own[3 + c : 4 + c, :] * total + sums[c : c + 1, :] - 2.0 * sums[7 + c : 8 + c, :]) for c in range(3)
    ]
    g_area = [twice * sums[3 + c : 4 + c, :] for c in range(3)]
    e1 = [edges[c : c + 1, :] for c in range(3)]
    e2 = [edges[3 + c : 4 + c, :] for c in range(3)]
    zero = jnp.zeros((ROWS - 3, count), F32)
    corners = [[], [], []]
    for c in range(3):
        n, m = (c + 1) % 3, (c + 2) % 3
        g1 = 0.5 * (e2[n] * g_area[m] - e2[m] * g_area[n])
        g2 = 0.5 * (g_area[n] * e1[m] - g_area[m] * e1[n])
        part = g_center[c] / 3.0
        corners[0].append(part - g1 - g2)
        corners[1].append(part + g1)
        corners[2].append(part + g2)
    total = jnp.zeros((3 * ROWS, verts), F32)
    for k in range(3):
        left = jnp.concatenate(pieces(jnp.concatenate(corners[k] + [zero], 0)), 0).astype(BF16)
        total += lax.dot_general(
            left, one_hot(faces[k : k + 1, :], verts), (((1,), (1,)), ((), ())), preferred_element_type=F32
        )
    total = total[0:ROWS] + total[ROWS : 2 * ROWS] + total[2 * ROWS : 3 * ROWS]
    grad[...] = total[0:3] / count


def gather(own, axis, size, wanted):
    if size & (size - 1) == 0 and len(wanted) == size - 1:
        found = {}
        held = own[None]
        mask = size // 2
        while mask:
            other = flip(held, axis, mask)
            for offset in wanted:
                if offset & -offset == mask:
                    found[offset] = (other, "ring")
            held = jnp.concatenate([held, other], 0) if mask > 1 else held
            mask //= 2
        return found
    return {offset: (from_ahead(own, axis, offset), None) for offset in wanted}


def shards(vertices, faces, trial_step, accepted, face_weight, partner_shift):
    count = faces.shape[1]
    verts = vertices.shape[1]
    groups, blocks = lax.axis_size("grp"), lax.axis_size("blk")
    block_shape = jax.ShapeDtypeStruct((ROWS, count), F32)
    arguments = (accepted, partner_shift, vertices, trial_step, faces, face_weight)
    arguments = arguments[:1] + tuple(pltpu.with_memory_space_constraint(each, pltpu.HBM) for each in arguments[1:])
    homes = [pltpu.SMEM] * 2 + [pltpu.VMEM] * 4
    met_shape = jax.ShapeDtypeStruct((-(-groups // ROWS) * ROWS, LANES), F32)
    kept, own, edges, times = pl.pallas_call(
        functools.partial(geometry_kernel, groups),
        out_shape=(jax.ShapeDtypeStruct(faces.shape, faces.dtype), block_shape, block_shape, met_shape),
        in_specs=[pl.BlockSpec(memory_space=pltpu.HBM)] * 6,
        out_specs=(VMEM,) * 4,
        scratch_shapes=[home(a.shape, a.dtype) for home, a in zip(homes, arguments)]
        + [pltpu.VMEM((ROWS, verts), F32), pltpu.SemaphoreType.DMA((6,))],
        compiler_params=PARAMS,
    )(*arguments)

    window = [o for o in range(1, blocks) if window_times(o, blocks)]
    ring = gather(own, "blk", blocks, window)
    across = gather(own, "grp", groups, list(range(1, groups)))

    def halves(items):
        return [(axis, offset, half) for axis, offset in items for half in range(2)]

    def visit(parts, factor, gradient, state, following):
        arrays, plan = [], []
        for axis, offset, half in parts + following:
            if axis == "self":
                array, index = own, None
            else:
                array, index = (ring if axis == "blk" else across)[offset]
            where = [i for i, known in enumerate(arrays) if known is array]
            if not where:
                arrays.append(array)
                where = [len(arrays) - 1]
            plan.append((where[0], index, axis, offset, half))
        return tiles(times, own, arrays, tuple(plan), factor, gradient, state, len(following) > 0, blocks)

    def stage(offset, size):
        return -(offset & -offset) if size & (size - 1) == 0 else 0

    middle = [("blk", o) for o in window if 2 * o == blocks] + [("grp", o) for o in range(1, groups) if 2 * o == groups]
    early_blk = sorted((o for o in window if 2 * o < blocks), key=lambda o: (stage(o, blocks), o))
    early_grp = [("grp", o) for o in range(1, groups) if 2 * o < groups]
    late = [("grp", o) for o in range(1, groups) if 2 * o > groups]
    late += [("blk", o) for o in sorted((o for o in window if 2 * o > blocks), key=lambda o: (stage(o, blocks), o))]
    first = early_grp + [("blk", o) for o in early_blk[: len(early_blk) // 3]]
    second = [("blk", o) for o in early_blk[len(early_blk) // 3 :]]

    state = visit(halves([("self", 0)]), 0.5, True, (None, None, None, None), [])
    for items, factor in ((middle, 0.5), (first, 1.0)):
        if items:
            state = visit(halves(items), factor, True, state, [])
    late = halves(late + second)
    if second:
        state = visit(halves(second), 1.0, False, state, late[:1])
    share = state[1]
    rounds = []
    for axis, size in (("blk", blocks), ("grp", groups)):
        if size & (size - 1) == 0:
            masks = [1 << k for k in range(size.bit_length() - 1)]
            rounds += [(axis, mask) for mask in (masks if axis == "blk" else masks[::-1])]
        else:
            rounds.append((axis, 0))

    def exchange(value, axis, mask):
        if mask:
            return flip(value, axis, mask)
        return sum(from_ahead(value, axis, o) for o in range(1, lax.axis_size(axis)))

    def last_of(total):
        return pl.pallas_call(
            finish_kernel,
            out_shape=jax.ShapeDtypeStruct((3, verts), F32),
            in_specs=[VMEM] * 4,
            out_specs=VMEM,
            compiler_params=PARAMS,
            cost_estimate=pl.CostEstimate(flops=1500000000, bytes_accessed=64 * count, transcendentals=0),
        )(own, edges, total, kept)

    covers = max(1, len(rounds) - 1)
    edges_of = [len(late) * i // covers for i in range(covers + 1)]
    for index in range(max(covers, len(rounds))):
        received = None
        if index < len(rounds):
            received = exchange(share, *rounds[index])
        if index < covers:
            begin, end = edges_of[index], edges_of[index + 1]
            if end > begin:
                state = visit(late[begin:end], 0.0, True, state, late[end : end + 1])
            done = state
        if index == len(rounds) - 1:
            grad = last_of(state[0])
            done = grad
        if received is not None:
            if index < len(rounds) - 1:
                state, received = lax.optimization_barrier((done, received))
            share = share + received
    if not rounds:
        grad = last_of(state[0])
    energy = jnp.sum(share) / (count * count * groups * blocks)
    return grad, energy.reshape(1)


def solution(mesh):
    placed = (
        P(None, ("grp", "blk")),
        P(None, ("grp", "blk")),
        P(None, ("grp", "blk")),
        P("grp"),
        P(("grp", "blk")),
        P(),
    )
    return jax.shard_map(
        shards,
        mesh=mesh,
        in_specs=placed,
        out_specs=(P(None, ("grp", "blk")), P()),
        check_vma=False,
    )
```

```python
import functools

import jax
import jax.numpy as jnp
from jax import lax
from jax.experimental import pallas as pl
from jax.experimental.pallas import tpu as pltpu
from jax.sharding import PartitionSpec as P

HOPS = 4
EPS2 = 0.05
ROWS = 8
LANES = 128
DEPTH = 64
SUMS = 10
F32 = jnp.float32
BF16 = jnp.bfloat16
VMEM = pl.BlockSpec(memory_space=pltpu.VMEM)
SMEM = pl.BlockSpec(memory_space=pltpu.SMEM)
FLOPS_PER_PAIR = 8000
GRADIENT_CHUNKS = 1
PARAMS = pltpu.CompilerParams(vmem_limit_bytes=16 * 1024 * 1024)


def flip(value, axis, mask):
    count = lax.axis_size(axis)
    return lax.ppermute(value, axis, [(i, i ^ mask) for i in range(count)])


def from_ahead(value, axis, by):
    count = lax.axis_size(axis)
    return lax.ppermute(value, axis, [(i, (i - by) % count) for i in range(count)])


def pieces(value):
    high = value.astype(BF16).astype(F32)
    rest = value - high
    middle = rest.astype(BF16).astype(F32)
    return high, middle, rest - middle


def one_hot(row, count):
    rows = lax.broadcasted_iota(jnp.int32, (count, row.shape[1]), 0)
    return jnp.where(rows == row, 1.0, 0.0).astype(BF16)


def partner_times(shift, here, there, groups):
    times = jnp.int32(0)
    for r in range(shift.shape[0]):
        times += (lax.rem(here + shift[r, here], groups) == there).astype(jnp.int32)
        times += (lax.rem(there + shift[r, there], groups) == here).astype(jnp.int32)
    return times


def geometry_kernel(groups, *refs):
    far, (kept, own, edges, times), near, (padded, arrived) = refs[:6], refs[6:10], refs[10:16], refs[16:]
    accepted, shift, vertices, trial_step, faces, weight = near
    copies = [pltpu.make_async_copy(far[i], near[i], arrived.at[i]) for i in range(6)]
    for copy in copies:
        copy.start()
    verts = vertices.shape[1]
    count = faces.shape[1]
    padded[...] = jnp.zeros_like(padded)
    for copy in copies:
        copy.wait()
    here = lax.axis_index("grp")
    times[...] = jnp.zeros_like(times)
    for offset in range(1, groups):
        met = partner_times(shift, here, lax.rem(here + offset, groups), groups).astype(F32)
        times[offset : offset + 1, :] = jnp.zeros((1, LANES), F32) + met
    padded[0:3, :] = vertices[...] + accepted[0].astype(F32) * trial_step[...]
    left = jnp.concatenate(pieces(padded[...]), 0).astype(BF16)

    def corner(k):
        picked = jnp.dot(left, one_hot(faces[k : k + 1, :], verts), preferred_element_type=F32)
        picked = picked[0:ROWS] + picked[ROWS : 2 * ROWS] + picked[2 * ROWS : 3 * ROWS]
        return [picked[c : c + 1] for c in range(3)]

    first, second, third = corner(0), corner(1), corner(2)
    center = [(first[c] + second[c] + third[c]) / 3.0 for c in range(3)]
    e1 = [second[c] - first[c] for c in range(3)]
    e2 = [third[c] - first[c] for c in range(3)]
    area = []
    for c in range(3):
        n, m = (c + 1) % 3, (c + 2) % 3
        area.append(0.5 * (e1[n] * e2[m] - e1[m] * e2[n]))
    for c in range(3):
        own[c : c + 1, :] = center[c]
        own[3 + c : 4 + c, :] = area[c]
        edges[c : c + 1, :] = e1[c]
        edges[3 + c : 4 + c, :] = e2[c]
    own[6:7, :] = weight[...].reshape(1, count)
    own[7:8, :] = center[0] * area[0] + center[1] * area[1] + center[2] * area[2]
    edges[6:8, :] = jnp.zeros((2, count), F32)
    kept[...] = faces[...]


def window_times(offset, blocks):
    return sum(int((k - offset) % blocks == 0) + int((k + offset) % blocks == 0) for k in range(1, HOPS + 1))


def place_of(mask, size):
    place, step, bit = 0, 1, size // 2
    while bit:
        place = place + jnp.bitwise_and(mask // bit, 1) * step
        step, bit = step * 2, bit // 2
    return place


def tiles_kernel(plan, blocks, factor, gradient, first, carry, lead, trail, *refs):
    refs = list(refs)
    own = refs.pop(0)
    count = own.shape[1]
    unit = count // 2
    chunks = count // LANES
    part = unit // chunks
    others = [refs.pop(0) for _ in range(1 + max(item[0] for item in plan))]
    met = refs.pop(0) if any(item[2] == "grp" for item in plan) else None
    right = None if first else refs.pop(0)
    total = refs.pop(0) if carry and gradient else None
    share_in = refs.pop(0) if carry and factor else None
    led = (refs.pop(0), refs.pop(0)) if lead else None
    out = refs.pop(0) if gradient else None
    share = refs.pop(0) if factor else None
    right = refs.pop(0) if first else right
    units = len(plan) - (1 if trail else 0)
    slots = [None, None]
    if trail:
        slots[units % 2] = (refs.pop(0), refs.pop(0))
    columns, left, sums = refs[:3]
    refs = refs[3:]
    for side in range(2):
        if slots[side] is None:
            slots[side] = (refs.pop(0), refs.pop(0))
    places = (list(range(SUMS)) if gradient else []) + ([SUMS] if factor else [])

    if first:
        zero = jnp.zeros((ROWS, count), F32)
        zero1, zero3 = jnp.zeros((1, count), F32), jnp.zeros((3, count), F32)
        from_own = jnp.concatenate([-own[3:6, :], zero3, own[7:8, :], zero1], 0)
        from_other = jnp.concatenate([zero3, own[0:3, :], zero1, zero1 - 1.0], 0)
        for side, rows in enumerate((from_own, from_other)):
            high, middle, low = pieces(rows)
            right[:, side * count : (side + 1) * count] = jnp.concatenate(
                [zero, high, middle, low, high, middle, high, zero], 0
            ).astype(BF16)
    row = lax.broadcasted_iota(jnp.int32, (ROWS, unit), 0)
    for u, (source, index, axis, offset, half) in enumerate(plan):
        if lead and u == 0:
            continue
        if index == "ring":
            size = lax.axis_size(axis)
            here = lax.axis_index(axis)
            there = lax.rem(here + offset, size)
            block = others[source][place_of(jnp.bitwise_xor(here, there), size) - size // 2 // (offset & -offset)]
        elif index is None:
            block = others[source][...]
        else:
            block = others[source][index]
        block = block[:, half * unit : (half + 1) * unit]
        if axis == "self":
            times = 1.0 + window_times(0, blocks)
        elif axis == "blk":
            times = float(window_times(offset, blocks))
        else:
            times = jnp.concatenate([met[offset : offset + 1, :]] * (unit // LANES), 1)
        block = jnp.where(row == 6, block * times, block)
        high, middle, low = pieces(jnp.where(row == 6, 1.0, block))
        turned = jnp.concatenate([block, high, high, high, middle, middle, low, jnp.zeros_like(block)], 0).T
        columns[u * unit : (u + 1) * unit, :] = turned[:, 0:ROWS]
        left[u * unit : (u + 1) * unit, :] = turned.astype(BF16)
    for k in places:
        sums[k] = jnp.zeros((ROWS, count), F32)

    def fill(u, chunk, slot):
        wide, proj = slot
        source = pl.multiple_of(u * unit + chunk * part, part)
        target = pl.multiple_of(chunk * part, part)
        proj[pl.ds(target, part), :] = jnp.dot(left[pl.ds(source, part), :], right[...], preferred_element_type=F32)
        for k in range(7) if gradient or u == units else (0, 1, 2, 6):
            for g in range(part // ROWS):
                group = columns[pl.ds(pl.multiple_of(source + g * ROWS, ROWS), ROWS), :]
                wide[k, pl.ds(pl.multiple_of(target + g * ROWS, ROWS), ROWS), :] = jnp.broadcast_to(
                    group[:, k : k + 1], (ROWS, LANES)
                )

    together = GRADIENT_CHUNKS if gradient else chunks
    never = lax.axis_index("blk") < 0

    def work(chunk, slot, following, is_last):
        wide, proj = slot
        at_lane = pl.multiple_of(chunk * LANES, LANES)
        span = pl.ds(at_lane, LANES)
        a = [jnp.broadcast_to(own[k : k + 1, span], (ROWS, LANES)) for k in range(3)]
        s = {k: sums[k, :, span] for k in places}
        for g in range(unit // ROWS):
            if is_last and g == unit // ROWS - 1:
                stored = pl.ds(pl.multiple_of(chunk * part, ROWS), ROWS)
                seen = following[0][6, stored, :] + following[1][stored, 0:LANES]
                s[places[-1]] += jnp.where(never, seen, 0.0)
            rows = slice(g * ROWS, (g + 1) * ROWS)
            b = {k: wide[k, rows, :] for k in (range(7) if gradient else (0, 1, 2, 6))}
            proj_a = proj[rows, span]
            proj_b = proj[rows, pl.ds(pl.multiple_of(count + at_lane, LANES), LANES)]
            d0, d1, d2 = a[0] - b[0], a[1] - b[1], a[2] - b[2]
            dist = d0 * d0 + d1 * d1 + (d2 * d2 + EPS2)
            inverse = 1.0 / dist
            square = inverse * inverse * b[6]
            if not gradient:
                s[SUMS] += (proj_a * proj_a + proj_b * proj_b) * square
                continue
            alpha = proj_a * square
            beta = proj_b * square
            kernel = proj_a * alpha + proj_b * beta
            gamma = kernel * inverse
            s[0] += beta * b[3]
            s[1] += beta * b[4]
            s[2] += beta * b[5]
            s[3] += alpha * d0
            s[4] += alpha * d1
            s[5] += alpha * d2
            s[6] += alpha
            s[7] += gamma * d0
            s[8] += gamma * d1
            s[9] += gamma * d2
            if factor:
                s[SUMS] += kernel
        for k in places:
            sums[k, :, span] = s[k]

    def over_chunks(now, u, slot):
        def step(index, carried):
            for k in range(together):
                fill(u, index * together + k, slot)
            for k in range(together):
                work(index * together + k, now, slot, k == together - 1)
            return carried

        if together == chunks:
            step(0, 0)
        else:
            lax.fori_loop(0, chunks // together, step, 0)

    if not lead:
        for chunk in range(chunks):
            fill(0, chunk, slots[0])
    for u in range(units):
        over_chunks(led if lead and u == 0 else slots[u % 2], min(u + 1, len(plan) - 1), slots[(u + 1) % 2])
    if gradient:
        for k in range(SUMS):
            line = jnp.sum(sums[k], axis=0, keepdims=True)
            out[k : k + 1, :] = line + total[k : k + 1, :] if carry else line
    if factor:
        weighted = sums[SUMS] * (factor * own[6:7, :])
        part_share = weighted[:, 0:LANES]
        for chunk in range(1, chunks):
            part_share = part_share + weighted[:, chunk * LANES : (chunk + 1) * LANES]
        share[...] = part_share + share_in[...] if carry else part_share


def tiles(times, own, arrays, plan, factor, gradient, state, trail, blocks):
    count = own.shape[1]
    unit = count // 2
    total, share, right, led = state
    first, carry, lead = right is None, total is not None, led is not None
    number = len(plan) - (1 if trail else 0)
    body = functools.partial(tiles_kernel, plan, blocks, factor, gradient, first, carry, lead, trail)
    operands = [own, *arrays] + ([times] if any(item[2] == "grp" for item in plan) else [])
    operands += ([] if first else [right]) + ([total] if carry and gradient else [])
    operands += ([share] if carry and factor else []) + (list(led) if lead else [])
    slot = [((7, unit, LANES), F32), ((unit, 2 * count), F32)]
    shapes = [jax.ShapeDtypeStruct((SUMS, count), F32)] if gradient else []
    if factor:
        shapes.append(jax.ShapeDtypeStruct((ROWS, LANES), F32))
    if first:
        shapes.append(jax.ShapeDtypeStruct((DEPTH, 2 * count), BF16))
    if trail:
        shapes += [jax.ShapeDtypeStruct(*each) for each in slot]
    pairs = number * unit * count
    result = list(
        pl.pallas_call(
            body,
            out_shape=shapes,
            in_specs=[VMEM] * len(operands),
            out_specs=[VMEM] * len(shapes),
            scratch_shapes=[
                pltpu.VMEM((len(plan) * unit, ROWS), F32),
                pltpu.VMEM((len(plan) * unit, DEPTH), BF16),
                pltpu.VMEM((SUMS + 1, ROWS, count), F32),
                *[pltpu.VMEM(*each) for each in slot],
                *([] if trail else [pltpu.VMEM(*each) for each in slot]),
            ],
            compiler_params=PARAMS,
            cost_estimate=pl.CostEstimate(
                flops=FLOPS_PER_PAIR * pairs, bytes_accessed=32 * unit * number, transcendentals=pairs
            ),
        )(*operands)
    )
    total = result.pop(0) if gradient else total
    share = result.pop(0) if factor else share
    right = result.pop(0) if first else right
    return total, share, right, (tuple(result) if trail else None)


def finish_kernel(own, edges, sums, faces, grad):
    verts = grad.shape[1]
    count = own.shape[1]
    twice = 2.0 * own[6:7, :]
    total = sums[6:7, :]
    g_center = [
        twice * (own[3 + c : 4 + c, :] * total + sums[c : c + 1, :] - 2.0 * sums[7 + c : 8 + c, :]) for c in range(3)
    ]
    g_area = [twice * sums[3 + c : 4 + c, :] for c in range(3)]
    e1 = [edges[c : c + 1, :] for c in range(3)]
    e2 = [edges[3 + c : 4 + c, :] for c in range(3)]
    zero = jnp.zeros((ROWS - 3, count), F32)
    corners = [[], [], []]
    for c in range(3):
        n, m = (c + 1) % 3, (c + 2) % 3
        g1 = 0.5 * (e2[n] * g_area[m] - e2[m] * g_area[n])
        g2 = 0.5 * (g_area[n] * e1[m] - g_area[m] * e1[n])
        part = g_center[c] / 3.0
        corners[0].append(part - g1 - g2)
        corners[1].append(part + g1)
        corners[2].append(part + g2)
    total = jnp.zeros((3 * ROWS, verts), F32)
    for k in range(3):
        left = jnp.concatenate(pieces(jnp.concatenate(corners[k] + [zero], 0)), 0).astype(BF16)
        total += lax.dot_general(
            left, one_hot(faces[k : k + 1, :], verts), (((1,), (1,)), ((), ())), preferred_element_type=F32
        )
    total = total[0:ROWS] + total[ROWS : 2 * ROWS] + total[2 * ROWS : 3 * ROWS]
    grad[...] = total[0:3] / count


def gather(own, axis, size, wanted):
    if size & (size - 1) == 0 and len(wanted) == size - 1:
        found = {}
        held = own[None]
        mask = size // 2
        while mask:
            other = flip(held, axis, mask)
            for offset in wanted:
                if offset & -offset == mask:
                    found[offset] = (other, "ring")
            held = jnp.concatenate([held, other], 0) if mask > 1 else held
            mask //= 2
        return found
    return {offset: (from_ahead(own, axis, offset), None) for offset in wanted}


def shards(vertices, faces, trial_step, accepted, face_weight, partner_shift):
    count = faces.shape[1]
    verts = vertices.shape[1]
    groups, blocks = lax.axis_size("grp"), lax.axis_size("blk")
    block_shape = jax.ShapeDtypeStruct((ROWS, count), F32)
    arguments = (accepted, partner_shift, vertices, trial_step, faces, face_weight)
    arguments = arguments[:1] + tuple(pltpu.with_memory_space_constraint(each, pltpu.HBM) for each in arguments[1:])
    homes = [pltpu.SMEM] * 2 + [pltpu.VMEM] * 4
    met_shape = jax.ShapeDtypeStruct((-(-groups // ROWS) * ROWS, LANES), F32)
    kept, own, edges, times = pl.pallas_call(
        functools.partial(geometry_kernel, groups),
        out_shape=(jax.ShapeDtypeStruct(faces.shape, faces.dtype), block_shape, block_shape, met_shape),
        in_specs=[pl.BlockSpec(memory_space=pltpu.HBM)] * 6,
        out_specs=(VMEM,) * 4,
        scratch_shapes=[home(a.shape, a.dtype) for home, a in zip(homes, arguments)]
        + [pltpu.VMEM((ROWS, verts), F32), pltpu.SemaphoreType.DMA((6,))],
        compiler_params=PARAMS,
    )(*arguments)

    window = [o for o in range(1, blocks) if window_times(o, blocks)]
    ring = gather(own, "blk", blocks, window)
    across = gather(own, "grp", groups, list(range(1, groups)))

    def halves(items):
        return [(axis, offset, half) for axis, offset in items for half in range(2)]

    def visit(parts, factor, gradient, state, following):
        arrays, plan = [], []
        for axis, offset, half in parts + following:
            if axis == "self":
                array, index = own, None
            else:
                array, index = (ring if axis == "blk" else across)[offset]
            where = [i for i, known in enumerate(arrays) if known is array]
            if not where:
                arrays.append(array)
                where = [len(arrays) - 1]
            plan.append((where[0], index, axis, offset, half))
        return tiles(times, own, arrays, tuple(plan), factor, gradient, state, len(following) > 0, blocks)

    def stage(offset, size):
        return -(offset & -offset) if size & (size - 1) == 0 else 0

    middle = [("blk", o) for o in window if 2 * o == blocks] + [("grp", o) for o in range(1, groups) if 2 * o == groups]
    early_blk = sorted((o for o in window if 2 * o < blocks), key=lambda o: (stage(o, blocks), o))
    early_grp = [("grp", o) for o in range(1, groups) if 2 * o < groups]
    late = [("grp", o) for o in range(1, groups) if 2 * o > groups]
    late += [("blk", o) for o in sorted((o for o in window if 2 * o > blocks), key=lambda o: (stage(o, blocks), o))]
    first = early_grp + [("blk", o) for o in early_blk[: len(early_blk) // 3]]
    second = [("blk", o) for o in early_blk[len(early_blk) // 3 :]]

    state = visit(halves([("self", 0)]), 0.5, True, (None, None, None, None), [])
    for items, factor in ((middle, 0.5), (first, 1.0)):
        if items:
            state = visit(halves(items), factor, True, state, [])
    late = halves(late + second)
    if second:
        state = visit(halves(second), 1.0, False, state, late[:1])
    share = state[1]
    rounds = []
    for axis, size in (("blk", blocks), ("grp", groups)):
        if size & (size - 1) == 0:
            masks = [1 << k for k in range(size.bit_length() - 1)]
            rounds += [(axis, mask) for mask in (masks if axis == "blk" else masks[::-1])]
        else:
            rounds.append((axis, 0))

    rounds.sort(key=lambda each: (each == ("grp", 1), each == ("blk", blocks // 2)))

    def exchange(value, axis, mask):
        if mask:
            return flip(value, axis, mask)
        return sum(from_ahead(value, axis, o) for o in range(1, lax.axis_size(axis)))

    def last_of(total):
        return pl.pallas_call(
            finish_kernel,
            out_shape=jax.ShapeDtypeStruct((3, verts), F32),
            in_specs=[VMEM] * 4,
            out_specs=VMEM,
            compiler_params=PARAMS,
            cost_estimate=pl.CostEstimate(flops=1500000000, bytes_accessed=64 * count, transcendentals=0),
        )(own, edges, total, kept)

    covers = max(1, len(rounds) - 1)
    edges_of = [len(late) * i // covers for i in range(covers + 1)]
    for index in range(max(covers, len(rounds))):
        received = None
        if index < len(rounds):
            received = exchange(share, *rounds[index])
        if index < covers:
            begin, end = edges_of[index], edges_of[index + 1]
            if end > begin:
                state = visit(late[begin:end], 0.0, True, state, late[end : end + 1])
            done = state
        if index == len(rounds) - 1:
            grad = last_of(state[0])
            done = grad
        if received is not None:
            if index < len(rounds) - 1:
                state, received = lax.optimization_barrier((done, received))
            share = share + received
    if not rounds:
        grad = last_of(state[0])
    energy = jnp.sum(share) / (count * count * groups * blocks)
    return grad, energy.reshape(1)


def solution(mesh):
    placed = (
        P(None, ("grp", "blk")),
        P(None, ("grp", "blk")),
        P(None, ("grp", "blk")),
        P("grp"),
        P(("grp", "blk")),
        P(),
    )
    return jax.shard_map(
        shards,
        mesh=mesh,
        in_specs=placed,
        out_specs=(P(None, ("grp", "blk")), P()),
        check_vma=False,
    )
```
